32 devices in a mesh: ctx: 16 (over z, x, core), wa: 2 (over y).
Axes of the slice: x: 2, y: 2, z: 4, core: 2. Of those that a mesh axis runs over, the one named last changes fastest.
Arguments:
- hidden_in: bfloat16 [2, 2048, 1024], P('wa', 'ctx')
- out_grad: bfloat16 [2, 2048, 1024], P('wa', 'ctx'), may hold values from -6 to 6
- lengths: int32 [2, 8], P('wa'), may hold values from 1 to 1024, 1792 in all within a row
- permutation: int32 [2, 2048], P('wa'), may hold values from 0 to 2047, each once within a row
- routes: int32 [2, 2048, 2], P('wa', 'ctx'), may hold values from 0 to 7, all different within a row; in each aligned block of 128 rows (0 to 127, 128 to 255, ..., all dimensions but the last counted through in order) at most 64 rows name the same one
- bucket_table: int32 [1024], replicated, may hold values from 0 to 31, never falling along the last dimension, each value on 1 to 256 neighbouring positions
- w_qkv: bfloat16 [1024, 3072], P('wa'), may hold values from -0.1875 to 0.1875
- w_out: bfloat16 [1024, 1024], P('wa'), may hold values from -0.75 to 0.75
- w_in: bfloat16 [16, 1024, 2816], P('ctx', 'wa'), may hold values from -0.1875 to 0.1875
- w_down: bfloat16 [16, 1024, 1408], P('ctx', 'wa'), may hold values from -0.109375 to 0.109375
- w_router: float32 [1024, 8], replicated, may hold values from -0.125 to 0.125
- gain_attn: float32 [1024], replicated, may hold values from 0.5 to 1.5
- gain_moe: float32 [1024], replicated, may hold values from 0.5 to 1.5
- rel_bias: float32 [32, 16], replicated, may hold values from -4 to 4
Outputs:
- block_out: bfloat16 [2, 2048, 1024], P('wa', 'ctx')
- hidden_grad: bfloat16 [2, 2048, 1024], P('wa', 'ctx')
- qkv_grad: float32 [1024, 3072], P('wa')
- out_proj_grad: float32 [1024, 1024], P('wa')
- expert_in_grad: float32 [16, 1024, 2816], P('ctx', 'wa')
- expert_down_grad: float32 [16, 1024, 1408], P('ctx', 'wa')
- router_grad: float32 [1024, 8], replicated
- gain_attn_grad: float32 [1024], replicated
- gain_moe_grad: float32 [1024], replicated
- rel_bias_grad: float32 [32, 16], replicated
- stats: float32 [3], replicated
The draws below stay inside these ranges and needn't reach their ends.
Inputs may be any that keep to these rules, and one draw needn't show every extreme that they name: In every batch the lengths sum to 1792 and the largest is exactly 1024; sequences lie in order from stream position 0, the rest is padding. Every row is a permutation of the 2048 stream positions of its batch. `routes`: each token names two different experts. Among the 128 slots of one device no expert is named more than 64 times, and on some device some expert is named exactly 64 times. `bucket_table`: never falls as the distance grows; every bucket appears, for at most 256 distances.
All inputs are finite; a program needn't handle non-finite values.
Results may differ from the reference program's by a relative error of at most 0.034.
Values may be sent and summed in bfloat16 or wider, within the bound.
No kernel may reach another device: no remote copies, remote signals or barrier semaphores. Data moves between devices by JAX's collectives and lax.ppermute only.
A program may use at most 192 MiB of HBM per device.

```python
import math
import jax
import jax.numpy as jnp
import numpy as np
from jax import lax

D = 1024
H = 16
HD = 64
FF = 2816
NB = 32
NSEQ = 8
TOK_DEV = 128
SLOTS = 2048
FILLED = 1792
MAXLEN = 1024
EXPERTS = 8
HALVES = 16
CAP = 64
N_WA = 2


def draw_hidden_in(key, part):
    first_key = jax.random.fold_in(jax.random.fold_in(key, 11), 0)
    place = jnp.arange(SLOTS, dtype=jnp.float32)[None, :, None]
    rising = jnp.exp(jnp.log(3.0) * place / SLOTS)
    base = jax.random.normal(first_key, (N_WA, SLOTS, D), jnp.float32)
    return (base * rising).astype(jnp.bfloat16)


def shard_levels(rng, dims, shards, low, high):
    def one(axis_at, parts):
        draws = jax.random.uniform(jax.random.fold_in(jax.random.fold_in(rng, 6), axis_at), (parts,), jnp.float32, low / len(shards), high / len(shards))
        return jnp.repeat(jnp.exp(draws), dims[axis_at] // parts).reshape((-1,) + (1,) * (len(dims) - axis_at - 1))

    gain = one(*shards[0])
    for cut in shards[1:]:
        gain = gain * one(*cut)
    return gain


def length_profile(amount, total, bound, slope):
    portions = [(1 << 20) // math.isqrt(grade ** slope) + 1 for grade in range(2, amount + 1)]
    spare, given = total - bound - (amount - 1), [1] * (amount - 1)
    while spare > 0:
        candidates = [i for i in range(amount - 1) if given[i] < bound]
        whole, budget = sum([portions[i] for i in candidates]), spare
        for i in candidates:
            addition = min(bound - given[i], max(1, budget * portions[i] // whole), spare)
            given[i] = given[i] + addition
            spare = spare - addition
    return np.array([bound] + given)


def uneven_parts(rng, number_of, total, most, skew):
    if number_of == 2:
        one = jax.random.randint(rng, (), max(1, total - most), min(most, total - 1) + 1)
        return jnp.stack([one, total - one])
    sizes = jnp.asarray(length_profile(number_of, total, most, skew), jnp.int32)
    pairs = (number_of - 1) // 2
    donor, sink = sizes[1:1 + 2 * pairs:2], sizes[2:2 + 2 * pairs:2]
    room = jnp.minimum(donor - 1, most - sink)
    passed = jax.random.randint(jax.random.fold_in(rng, 1), (pairs,), 0, 1 << 20) % (room + 1)
    sizes = sizes.at[1:1 + 2 * pairs:2].set(donor - passed).at[2:2 + 2 * pairs:2].set(sink + passed)
    return sizes[jax.random.permutation(jax.random.fold_in(rng, 2), number_of)]


def deal_out(own_key, own, number, rows, count, top, reach, lean):
    order = jax.random.permutation(own_key, count)
    crowded, common = load_shares(count, rows * top, reach, lean, True), load_shares(count, rows * top, reach, lean, False)
    places = jnp.arange(count)

    def named(tallies, rotation):
        used = int((tallies > 0).sum())
        fixed = max(1, used // 4)
        moved = fixed + (places - fixed + rotation * (used - fixed)) % max(1, count - fixed)
        return jnp.zeros((count,), jnp.int32).at[order[jnp.where(places < fixed, places, moved)]].set(jnp.asarray(tallies, jnp.int32))

    tallies = jnp.where(number % 4 == 0, named(crowded, number // 4), named(common, number - number // 4 - 1))
    mixed = jax.random.permutation(jax.random.fold_in(own, 3), count)
    source_of, taker = mixed[0:count // 2 * 2:2], mixed[1:count // 2 * 2:2]
    room = jnp.minimum(tallies[source_of] - 1, reach - tallies[taker]) // 2
    room = jnp.where((source_of == order[0]) | (taker == order[0]) | (tallies[taker] == 0), 0, jnp.maximum(room, 0))
    moved = jax.random.randint(jax.random.fold_in(own, 4), (count // 2,), 0, 1 << 20) % (room + 1)
    tallies = tallies.at[source_of].add(-moved).at[taker].add(moved)
    members = jnp.searchsorted(jnp.cumsum(tallies), jnp.arange(rows * top), side="right").astype(jnp.int32)
    grid = members.reshape(top, rows).T
    grid = grid[jax.random.permutation(jax.random.fold_in(own, 1), rows)]
    rotation = jax.random.randint(jax.random.fold_in(own, 2), (rows, 1), 0, top)
    return jnp.take_along_axis(grid, (jnp.arange(top)[None, :] + rotation) % top, axis=1)


def load_shares(number_of, total, bound, slope, full):
    loads = [(1 << 20) // math.isqrt(rank ** slope) + 1 for rank in range(1, number_of + 1)]
    largest = bound if full else min(bound, max(-(-total // number_of), total * loads[0] // sum(loads)))
    least = 1 if total - largest >= number_of - 1 else 0
    holding, surplus = [largest] + [least] * (number_of - 1), total - largest - least * (number_of - 1)
    while surplus > 0:
        candidates = [i for i in range(1, number_of) if holding[i] < largest] or [i for i in range(1, number_of) if holding[i] < bound]
        mass, remaining = sum([loads[i] for i in candidates]), surplus
        for i in candidates:
            extra = min(bound - holding[i], max(1, remaining * loads[i] // mass), surplus)
            holding[i] = holding[i] + extra
            surplus = surplus - extra
    return np.array(holding)


def normal_values(key, extent, spread, most, shards=(), held_as=jnp.bfloat16):
    values = jax.random.normal(key, extent, jnp.float32) * spread
    if len(shards) > 0:
        values = shard_levels(key, extent, shards, -0.22, 0.18) * values
    return jnp.clip(values, min=-most, max=most).astype(held_as)


def setup_inputs(seed: int = 0) -> dict:
    seeds = jax.random.split(jax.random.key(seed), 15)
    hidden_in = draw_hidden_in(jax.random.fold_in(seeds[14], 71), 0)
    out_grad = normal_values(seeds[1], (N_WA, SLOTS, D), 1.0, 6.0, ((0, 2), (1, 16)))
    lengths = jax.vmap(lambda own: uneven_parts(own, NSEQ, FILLED, MAXLEN, 2))(jax.random.split(seeds[2], N_WA)).reshape((N_WA, NSEQ)).astype(jnp.int32)
    permutation = jax.vmap(lambda own: jax.random.permutation(own, SLOTS))(jax.random.split(seeds[3], N_WA)).reshape((N_WA, SLOTS)).astype(jnp.int32)
    routes_keys = jax.random.split(jax.random.fold_in(seeds[4], 1), N_WA * SLOTS // TOK_DEV)
    routes_turns = jax.random.permutation(jax.random.fold_in(seeds[4], 3), N_WA * SLOTS // TOK_DEV)
    routes = jax.vmap(lambda own, number: deal_out(jax.random.fold_in(seeds[4], 2), own, number, TOK_DEV, EXPERTS, 2, CAP, 1))(routes_keys, routes_turns).reshape((N_WA, SLOTS, 2))
    bucket_table = jnp.searchsorted(jnp.cumsum(uneven_parts(seeds[5], NB, MAXLEN, MAXLEN // 4, 1)), jnp.arange(MAXLEN), side="right").astype(jnp.int32)
    w_qkv = normal_values(seeds[6], (D, 3 * D), D ** -0.5, 0.1875, ((0, 2),))
    w_out = normal_values(seeds[7], (D, D), (D // 16) ** -0.5, 0.75, ((0, 2),))
    w_in = normal_values(seeds[8], (HALVES, D, FF), D ** -0.5, 0.1875, ((0, 16), (1, 2)))
    w_down = normal_values(seeds[9], (HALVES, D, FF // 2), FF ** -0.5, 0.109375, ((0, 16), (1, 2)))
    w_router = normal_values(seeds[10], (D, EXPERTS), (2 * D) ** -0.5, 0.125, (), jnp.float32)
    gain_attn = jnp.clip(1.0 + 0.1 * jax.random.normal(seeds[11], (D,), jnp.float32), 0.5, 1.5)
    gain_moe = jnp.clip(1.0 + 0.1 * jax.random.normal(seeds[12], (D,), jnp.float32), 0.5, 1.5)
    rel_bias = normal_values(seeds[13], (NB, H), 1.0, 4.0, (), jnp.float32)
    return dict(hidden_in=hidden_in, out_grad=out_grad, lengths=lengths, permutation=permutation, routes=routes, bucket_table=bucket_table, w_qkv=w_qkv, w_out=w_out, w_in=w_in, w_down=w_down, w_router=w_router, gain_attn=gain_attn, gain_moe=gain_moe, rel_bias=rel_bias)


@jax.custom_vjp
def low(v):
    return lax.optimization_barrier(v.astype(jnp.bfloat16)).astype(jnp.float32)

@jax.custom_vjp
def low_back(v):
    return v

def low_keep(v):
    return (low(v), None)

def low_pass(kept, grad):
    return (grad,)

def back_keep(v):
    return (v, None)

def back_low(kept, grad):
    return (low(grad),)
low.defvjp(low_keep, low_pass)
low_back.defvjp(back_keep, back_low)
NORM_EPSILON = 1e-06
MASKED_SCORE = -1e+30
TOP_PRECISION = lax.Precision.HIGHEST

def rms_norm(features, scale_gain):
    return features * lax.rsqrt(lax.optimization_barrier(jnp.mean(features * features, axis=-1, keepdims=True)) + NORM_EPSILON) * scale_gain

def glu_act(gate_up):
    middle = gate_up.shape[-1] // 2
    return jax.nn.gelu(gate_up[..., :middle], approximate=True) * gate_up[..., middle:]

def both_round(values):
    return low(low_back(values))

def to_stream(rows_in, order):
    return jnp.zeros_like(rows_in).at[order].set(rows_in)

def from_stream(rows_in, order):
    return jnp.take(rows_in, order, axis=0)

def reference(hidden_in, out_grad, lengths, permutation, routes, bucket_table, w_qkv, w_out, w_in, w_down, w_router, gain_attn, gain_moe, rel_bias):
    batches = hidden_in.shape[0]
    slots = hidden_in.shape[1]
    stream = jax.vmap(to_stream)(hidden_in.astype(jnp.float32), permutation)
    grad_stream = jax.vmap(to_stream)(out_grad.astype(jnp.float32), permutation)
    route_stream = jax.vmap(to_stream)(routes, permutation).reshape(-1, 2)
    places = jnp.arange(slots, dtype=jnp.int32)
    bounds = jnp.cumsum(lengths, axis=1).astype(jnp.int32)
    segment = lax.optimization_barrier(jnp.sum((places[None, :, None] >= bounds[:, None, :]).astype(jnp.int32), axis=2))
    is_valid = (segment < NSEQ).astype(jnp.float32)
    block_rows = math.gcd(slots, 512)
    expert_ids = jnp.arange(EXPERTS, dtype=jnp.int32)
    first_hot = (route_stream[:, 0:1] == expert_ids[None, :]).astype(jnp.float32)
    second_hot = (route_stream[:, 1:2] == expert_ids[None, :]).astype(jnp.float32)

    def forward(stream_in, qkv_weight, out_weight, in_weight, down_weight, router_weight, attn_gain, moe_gain, bias_table):
        bias_rows = jnp.take(bias_table, bucket_table, axis=0).T
        normed_attn = low(rms_norm(stream_in, attn_gain))
        qkv = both_round(jnp.einsum('bsd,de->bse', normed_attn, qkv_weight, precision=TOP_PRECISION))
        queries = qkv[..., :D].reshape(batches, slots, H, HD)
        key_rows = qkv[..., D:2 * D].reshape(batches, slots, H, HD)
        value_rows = qkv[..., 2 * D:].reshape(batches, slots, H, HD)

        def attend_batch(inputs):
            query_all, key_all, value_all, seg_row = inputs

            def attend_block(step_index):
                row_begin = step_index * block_rows
                query_part = lax.dynamic_slice_in_dim(query_all, row_begin, block_rows, 0)
                query_seg = lax.dynamic_slice_in_dim(seg_row, row_begin, block_rows, 0)
                query_pos = row_begin + jnp.arange(block_rows, dtype=jnp.int32)
                raw_scores = jnp.einsum('qhd,khd->hqk', query_part, key_all, precision=TOP_PRECISION)
                distance = query_pos[:, None] - places[None, :]
                clipped = jnp.clip(distance, 0, MAXLEN - 1)
                scores = low_back(raw_scores * 0.125 + jnp.take(bias_rows, clipped, axis=1))
                allowed = (query_seg[:, None] == seg_row[None, :]) & (distance >= 0) & (query_seg[:, None] < NSEQ)
                row_max = lax.optimization_barrier(jnp.max(jnp.where(allowed, scores, MASKED_SCORE), axis=2, keepdims=True))
                exp_scores = jnp.exp(jnp.where(allowed, scores - row_max, MASKED_SCORE))
                totals = lax.optimization_barrier(jnp.sum(exp_scores, axis=2, keepdims=True))
                attn_probs = low(exp_scores / jnp.where(query_seg[None, :, None] < NSEQ, totals, 1.0))
                return jnp.einsum('hqk,khd->qhd', attn_probs, value_all, precision=TOP_PRECISION)
            blocks_out = lax.map(jax.checkpoint(attend_block), jnp.arange(slots // block_rows, dtype=jnp.int32))
            return blocks_out.reshape(slots, D)
        mixed = both_round(lax.map(attend_batch, (queries, key_rows, value_rows, segment)))
        attn_out = low_back(jnp.einsum('bsd,de->bse', mixed, out_weight, precision=TOP_PRECISION))
        resid = stream_in + attn_out
        normed_moe = low(rms_norm(resid, moe_gain)).reshape(-1, D)
        logits = jnp.dot(normed_moe, router_weight, precision=TOP_PRECISION)
        chosen = jnp.stack([lax.optimization_barrier(jnp.sum(logits * first_hot, axis=1)), lax.optimization_barrier(jnp.sum(logits * second_hot, axis=1))], axis=1)
        gate_probs = jax.nn.softmax(chosen, axis=1)
        gate_table = gate_probs[:, 0:1] * first_hot + gate_probs[:, 1:2] * second_hot
        in_pairs = in_weight.reshape(EXPERTS, 2, D, FF)
        down_pairs = down_weight.reshape(EXPERTS, 2, D, FF // 2)

        def expert_step(running, inputs):
            in_pair, down_pair, column = inputs
            expert_sum = jnp.zeros_like(normed_moe)
            for portion in range(2):
                row_copy = low_back(normed_moe)
                gate_up = low_back(jnp.dot(row_copy, in_pair[portion], precision=TOP_PRECISION))
                hidden = low(glu_act(gate_up))
                expert_sum = expert_sum + low(jnp.dot(hidden, down_pair[portion].T, precision=TOP_PRECISION))
            return (running + column[:, None] * low_back(expert_sum), None)
        moe_flat, _ = lax.scan(jax.checkpoint(expert_step), jnp.zeros_like(normed_moe), (in_pairs, down_pairs, gate_table.T))
        moe_out = moe_flat.reshape(batches, slots, D)
        final = resid + moe_out
        return (final, (final, attn_out, moe_out))
    primals = (stream, w_qkv.astype(jnp.float32), w_out.astype(jnp.float32), w_in.astype(jnp.float32), w_down.astype(jnp.float32), w_router, gain_attn, gain_moe, rel_bias)
    final, backward, extras = jax.vjp(forward, *primals, has_aux=True)
    gradients = backward(grad_stream)
    valid_count = jnp.sum(is_valid) * D
    stats = jnp.stack([jnp.sqrt(jnp.sum(is_valid[:, :, None] * member * member) / valid_count) for member in extras])
    block_out = jax.vmap(from_stream)(final, permutation).astype(jnp.bfloat16)
    hidden_grad = jax.vmap(from_stream)(gradients[0], permutation).astype(jnp.bfloat16)
    return (block_out, hidden_grad, gradients[1], gradients[2], gradients[3], gradients[4], gradients[5], gradients[6], gradients[7], gradients[8], stats)
```

```python
import math

import jax
import jax.numpy as jnp
from jax import lax
from jax.experimental import pallas as pl
from jax.experimental.pallas import tpu as pltpu
from jax.sharding import PartitionSpec as P
import functools
import numpy as np

NSEQ = 8


NORM_EPSILON = 1e-06
MASKED_SCORE = -1e30
TOP_PRECISION = lax.Precision.HIGHEST


def rms_norm(features, scale_gain):
    return (
        features
        * lax.rsqrt(jnp.mean(features * features, axis=-1, keepdims=True) + NORM_EPSILON)
        * scale_gain
    )


def glu_act(gate_up):
    middle = gate_up.shape[-1] // 2
    return jax.nn.gelu(gate_up[..., :middle], approximate=True) * gate_up[..., middle:]


def segment_of(positions, bounds):
    return jnp.sum((positions[:, None] >= bounds[None, :]).astype(jnp.int32), axis=1)


def lead_dot(left, right, precision=None):
    return lax.dot_general(
        left,
        right,
        (((0,), (0,)), ((), ())),
        precision=precision,
        preferred_element_type=jnp.float32,
    )


def tail_dot(left, right):
    return lax.dot_general(
        left, right, (((1,), (1,)), ((), ())), preferred_element_type=jnp.float32
    )


def pair_scores(
    queries, key_rows, query_pos, query_seg, key_pos, key_seg, bucket_starts, bias_table
):
    bucket_count = bias_table.shape[0]
    raw_scores = jnp.einsum("qhd,khd->hqk", queries, key_rows, preferred_element_type=jnp.float32)
    distance = query_pos[:, None] - key_pos[None, :]
    clipped = jnp.maximum(distance, 0)
    bucket_ids = jnp.sum(
        (clipped[:, :, None] >= bucket_starts[None, None, 1:]).astype(jnp.int32), axis=2
    )
    bucket_hot = (
        bucket_ids[:, :, None] == jnp.arange(bucket_count, dtype=jnp.int32)[None, None, :]
    ).astype(jnp.float32)
    bias_block = jnp.einsum("qkb,bh->hqk", bucket_hot, bias_table, precision=TOP_PRECISION)
    scores = raw_scores * 0.125 + bias_block
    allowed = (
        (query_seg[:, None] == key_seg[None, :]) & (distance >= 0) & (query_seg[:, None] < NSEQ)
    )
    return (scores, allowed, bucket_hot)


def attend_piece(
    running, pieces, queries, query_pos, query_seg, perm_row, bounds, bucket_starts, bias_table
):
    key_rows, value_rows = pieces
    piece_rows = key_rows.shape[0]
    head_count = queries.shape[1]
    block_rows = math.gcd(piece_rows, 512)
    keys_split = key_rows.reshape(piece_rows, head_count, -1)
    values_split = value_rows.reshape(piece_rows, head_count, -1)

    def step(step_index, state):
        row_max, totals, weighted = state
        offset = step_index * block_rows
        key_block = lax.dynamic_slice_in_dim(keys_split, offset, block_rows, 0)
        value_block = lax.dynamic_slice_in_dim(values_split, offset, block_rows, 0)
        key_pos = lax.dynamic_slice_in_dim(perm_row, offset, block_rows, 0)
        key_seg = segment_of(key_pos, bounds)
        scores, allowed, _ = pair_scores(
            queries, key_block, query_pos, query_seg, key_pos, key_seg, bucket_starts, bias_table
        )
        new_max = jnp.maximum(row_max, jnp.max(jnp.where(allowed, scores, MASKED_SCORE), axis=2))
        factor = jnp.exp(row_max - new_max)
        exp_scores = jnp.exp(jnp.where(allowed, scores - new_max[:, :, None], MASKED_SCORE))
        totals = totals * factor + jnp.sum(exp_scores, axis=2)
        weighted = weighted * factor[:, :, None] + jnp.einsum(
            "hqk,khd->hqd",
            exp_scores.astype(jnp.bfloat16),
            value_block,
            preferred_element_type=jnp.float32,
        )
        return (new_max, totals, weighted)

    return lax.fori_loop(0, piece_rows // block_rows, step, running)


def block_grads(
    queries,
    dout_low,
    log_total,
    row_delta,
    query_pos,
    query_seg,
    key_block,
    value_block,
    key_pos,
    key_seg,
    bucket_starts,
    bias_table,
):
    scores, allowed, bucket_hot = pair_scores(
        queries, key_block, query_pos, query_seg, key_pos, key_seg, bucket_starts, bias_table
    )
    attn_probs = jnp.exp(jnp.where(allowed, scores - log_total[:, :, None], MASKED_SCORE))
    prob_grad = jnp.einsum(
        "qhd,khd->hqk", dout_low, value_block, preferred_element_type=jnp.float32
    )
    score_grad = (attn_probs * (prob_grad - row_delta[:, :, None])).astype(jnp.bfloat16)
    query_grad = 0.125 * jnp.einsum(
        "hqk,khd->qhd", score_grad, key_block, preferred_element_type=jnp.float32
    )
    key_grad = 0.125 * jnp.einsum(
        "hqk,qhd->khd", score_grad, queries, preferred_element_type=jnp.float32
    )
    value_grad = jnp.einsum(
        "hqk,qhd->khd",
        attn_probs.astype(jnp.bfloat16),
        dout_low,
        preferred_element_type=jnp.float32,
    )
    bias_grad = jnp.einsum(
        "hqk,qkb->bh",
        score_grad,
        bucket_hot.astype(jnp.bfloat16),
        preferred_element_type=jnp.float32,
    )
    return (query_grad, key_grad, value_grad, bias_grad)


def general_device(
    hidden_in,
    out_grad,
    lengths,
    permutation,
    routes,
    bucket_table,
    w_qkv,
    w_out,
    w_in,
    w_down,
    w_router,
    gain_attn,
    gain_moe,
    rel_bias,
):
    stream = hidden_in[0].astype(jnp.float32)
    local_rows = stream.shape[0]
    model_width = stream.shape[1]
    head_count = rel_bias.shape[1]
    bucket_count = rel_bias.shape[0]
    head_dim = model_width // head_count
    experts = w_router.shape[1]
    slot_cap = 4 * local_rows // experts
    groups = lax.axis_size("ctx")
    perm_row = permutation[0]
    bounds = jnp.cumsum(lengths[0])
    own_start = lax.axis_index("ctx") * local_rows
    query_pos = lax.dynamic_slice_in_dim(perm_row, own_start, local_rows, 0)
    query_seg = segment_of(query_pos, bounds)
    is_valid = (query_seg < NSEQ).astype(jnp.float32)
    bucket_starts = jnp.sum(
        (bucket_table[:, None] < jnp.arange(bucket_count, dtype=jnp.int32)[None, :]).astype(
            jnp.int32
        ),
        axis=0,
    )
    qkv_full, out_full, in_full, down_full = (
        lax.all_gather(w_qkv, "wa", axis=0, tiled=True),
        lax.all_gather(w_out, "wa", axis=0, tiled=True),
        lax.all_gather(w_in[0], "wa", axis=0, tiled=True),
        lax.all_gather(w_down[0], "wa", axis=0, tiled=True),
    )
    normed_attn = rms_norm(stream, gain_attn)
    normed_attn_low = normed_attn.astype(jnp.bfloat16)
    qkv = jnp.dot(normed_attn_low, qkv_full, preferred_element_type=jnp.float32).astype(
        jnp.bfloat16
    )
    queries = qkv[:, :model_width].reshape(local_rows, head_count, head_dim)
    key_rows = qkv[:, model_width : 2 * model_width]
    value_rows = qkv[:, 2 * model_width :]
    initial = (
        jnp.full((head_count, local_rows), MASKED_SCORE, jnp.float32),
        jnp.zeros((head_count, local_rows), jnp.float32),
        jnp.zeros((head_count, local_rows, head_dim), jnp.float32),
    )
    row_max, totals, weighted = attend_piece(
        initial,
        (
            lax.all_gather(key_rows, "ctx", axis=0, tiled=True),
            lax.all_gather(value_rows, "ctx", axis=0, tiled=True),
        ),
        queries,
        query_pos,
        query_seg,
        perm_row,
        bounds,
        bucket_starts,
        rel_bias,
    )
    safe_totals = jnp.where(query_seg[None, :] < NSEQ, totals, 1.0)
    log_total = row_max + jnp.log(safe_totals)
    attn_heads = weighted / safe_totals[:, :, None]
    attn_mix = jnp.transpose(attn_heads, (1, 0, 2)).reshape(local_rows, model_width)
    attn_low = attn_mix.astype(jnp.bfloat16)
    attn_out = jnp.dot(attn_low, out_full, preferred_element_type=jnp.float32)
    resid = stream + attn_out
    normed_moe = rms_norm(resid, gain_moe)
    normed_moe_low = normed_moe.astype(jnp.bfloat16)
    normed_moe_wide = normed_moe_low.astype(jnp.float32)
    logits = jnp.dot(normed_moe_wide, w_router, precision=TOP_PRECISION)
    route_rows = routes[0]
    expert_ids = jnp.arange(experts, dtype=jnp.int32)
    first_hot = route_rows[:, 0:1] == expert_ids[None, :]
    second_hot = route_rows[:, 1:2] == expert_ids[None, :]
    chosen = jnp.stack(
        [
            jnp.sum(jnp.where(first_hot, logits, 0.0), axis=1),
            jnp.sum(jnp.where(second_hot, logits, 0.0), axis=1),
        ],
        axis=1,
    )
    gate_probs = jax.nn.softmax(chosen, axis=1)
    counts = jnp.cumsum((first_hot | second_hot).astype(jnp.int32), axis=0)
    first_slot = jnp.sum(jnp.where(first_hot, counts - 1, 0), axis=1)
    second_slot = jnp.sum(jnp.where(second_hot, counts - 1, 0), axis=1)
    first_lane = route_rows[:, 0] * slot_cap + first_slot
    second_lane = route_rows[:, 1] * slot_cap + second_slot
    lane_ids = jnp.arange(experts * slot_cap, dtype=jnp.int32)
    first_pick = (first_lane[:, None] == lane_ids[None, :]).astype(jnp.bfloat16)
    second_pick = (second_lane[:, None] == lane_ids[None, :]).astype(jnp.bfloat16)
    dispatch = (
        lead_dot(first_pick, normed_moe_low) + lead_dot(second_pick, normed_moe_low)
    ).astype(jnp.bfloat16)
    spread = jnp.broadcast_to(
        dispatch.reshape(experts, 1, slot_cap, model_width), (experts, 2, slot_cap, model_width)
    ).reshape(groups, slot_cap, model_width)
    received = lax.all_to_all(spread, "ctx", split_axis=0, concat_axis=0, tiled=True)
    item_count = received.shape[1]
    row_block = received.reshape(-1, model_width)
    gate_up = jnp.dot(row_block, in_full, preferred_element_type=jnp.float32)
    hidden = glu_act(gate_up).astype(jnp.bfloat16)
    partial_value = tail_dot(hidden, down_full).astype(jnp.bfloat16)
    returned = lax.all_to_all(
        partial_value.reshape(groups, item_count, model_width),
        "ctx",
        split_axis=0,
        concat_axis=0,
        tiled=True,
    )
    returned, gate_up_kept, received_kept = (
        returned,
        gate_up.reshape(groups, item_count, -1),
        received,
    )
    halves = returned.reshape(experts, 2, slot_cap, model_width)
    first_half = halves[:, 0].reshape(-1, model_width)
    second_half = halves[:, 1].reshape(-1, model_width)
    picked_first = jnp.dot(first_pick, first_half, preferred_element_type=jnp.float32) + jnp.dot(
        first_pick, second_half, preferred_element_type=jnp.float32
    )
    picked_second = jnp.dot(second_pick, first_half, preferred_element_type=jnp.float32) + jnp.dot(
        second_pick, second_half, preferred_element_type=jnp.float32
    )
    moe_out = gate_probs[:, 0:1] * picked_first + gate_probs[:, 1:2] * picked_second
    final = resid + moe_out
    valid_col = is_valid[:, None]
    stat_terms = jnp.stack(
        [
            jnp.sum(valid_col * final * final),
            jnp.sum(valid_col * attn_out * attn_out),
            jnp.sum(valid_col * moe_out * moe_out),
        ]
    )
    valid_count = jnp.sum(is_valid)
    grad_final = out_grad[0].astype(jnp.float32)
    first_dy = (gate_probs[:, 0:1] * grad_final).astype(jnp.bfloat16)
    second_dy = (gate_probs[:, 1:2] * grad_final).astype(jnp.bfloat16)
    gate_grad = jnp.stack(
        [jnp.sum(grad_final * picked_first, axis=1), jnp.sum(grad_final * picked_second, axis=1)],
        axis=1,
    )
    _, gate_back = jax.vjp(lambda chosen_in: jax.nn.softmax(chosen_in, axis=1), chosen)
    (chosen_grad,) = gate_back(gate_grad)
    logit_grad = jnp.where(first_hot, chosen_grad[:, 0:1], 0.0) + jnp.where(
        second_hot, chosen_grad[:, 1:2], 0.0
    )
    router_grad = lead_dot(normed_moe_wide, logit_grad, TOP_PRECISION)
    norm_moe_grad = jnp.dot(logit_grad, w_router.T, precision=TOP_PRECISION)
    dy_slots = (lead_dot(first_pick, first_dy) + lead_dot(second_pick, second_dy)).astype(
        jnp.bfloat16
    )
    dy_spread = jnp.broadcast_to(
        dy_slots.reshape(experts, 1, slot_cap, model_width), (experts, 2, slot_cap, model_width)
    ).reshape(groups, slot_cap, model_width)
    received_grad = lax.all_to_all(dy_spread, "ctx", split_axis=0, concat_axis=0, tiled=True)
    rows_grad = received_grad.reshape(-1, model_width)
    rows_kept = received_kept.reshape(-1, model_width)
    gate_up_rows = gate_up_kept.reshape(rows_grad.shape[0], -1)
    hidden_rows, act_back = jax.vjp(glu_act, gate_up_rows)
    hidden_low = hidden_rows.astype(jnp.bfloat16)
    hidden_grad_rows = jnp.dot(rows_grad, down_full, preferred_element_type=jnp.float32)
    down_grad = lead_dot(rows_grad, hidden_low)
    (gate_up_grad,) = act_back(hidden_grad_rows)
    gate_up_low = gate_up_grad.astype(jnp.bfloat16)
    in_grad = lead_dot(rows_kept, gate_up_low)
    rows_back = tail_dot(gate_up_low, in_full).astype(jnp.bfloat16)
    returned_grad = lax.all_to_all(
        rows_back.reshape(groups, slot_cap, model_width),
        "ctx",
        split_axis=0,
        concat_axis=0,
        tiled=True,
    )
    grad_halves = returned_grad.reshape(experts, 2, slot_cap, model_width)
    first_back = grad_halves[:, 0].reshape(-1, model_width)
    second_back = grad_halves[:, 1].reshape(-1, model_width)
    norm_moe_grad = (
        norm_moe_grad
        + jnp.dot(first_pick, first_back, preferred_element_type=jnp.float32)
        + jnp.dot(first_pick, second_back, preferred_element_type=jnp.float32)
    )
    norm_moe_grad = (
        norm_moe_grad
        + jnp.dot(second_pick, first_back, preferred_element_type=jnp.float32)
        + jnp.dot(second_pick, second_back, preferred_element_type=jnp.float32)
    )
    _, norm_moe_back = jax.vjp(rms_norm, resid, gain_moe)
    resid_from_norm, gain_moe_grad = norm_moe_back(norm_moe_grad)
    resid_grad = grad_final + resid_from_norm
    attn_grad_low = resid_grad.astype(jnp.bfloat16)
    out_proj_grad = lead_dot(attn_low, attn_grad_low)
    mix_grad = tail_dot(attn_grad_low, out_full)
    dout_low = mix_grad.astype(jnp.bfloat16).reshape(local_rows, head_count, head_dim)
    row_delta = jnp.einsum("qhd,hqd->hq", dout_low.astype(jnp.float32), attn_heads)
    key_all, value_all = (
        lax.all_gather(key_rows, "ctx", axis=0, tiled=True),
        lax.all_gather(value_rows, "ctx", axis=0, tiled=True),
    )
    total_rows = key_all.shape[0]
    block_rows = math.gcd(total_rows, 512)
    keys_split = key_all.reshape(total_rows, head_count, head_dim)
    values_split = value_all.reshape(total_rows, head_count, head_dim)
    seg_all = segment_of(perm_row, bounds)

    def key_step(step_index, state):
        query_acc, bias_acc, pair_buffer = state
        offset = step_index * block_rows
        key_block = lax.dynamic_slice_in_dim(keys_split, offset, block_rows, 0)
        value_block = lax.dynamic_slice_in_dim(values_split, offset, block_rows, 0)
        key_pos = lax.dynamic_slice_in_dim(perm_row, offset, block_rows, 0)
        key_seg = lax.dynamic_slice_in_dim(seg_all, offset, block_rows, 0)
        query_grad, key_grad, value_grad, bias_grad = block_grads(
            queries,
            dout_low,
            log_total,
            row_delta,
            query_pos,
            query_seg,
            key_block,
            value_block,
            key_pos,
            key_seg,
            bucket_starts,
            rel_bias,
        )
        joined = jnp.concatenate(
            [
                key_grad.reshape(block_rows, model_width),
                value_grad.reshape(block_rows, model_width),
            ],
            axis=1,
        )
        pair_buffer = lax.dynamic_update_slice_in_dim(pair_buffer, joined, offset, 0)
        return (query_acc + query_grad, bias_acc + bias_grad, pair_buffer)

    start_state = (
        jnp.zeros((local_rows, head_count, head_dim), jnp.float32),
        jnp.zeros((bucket_count, head_count), jnp.float32),
        jnp.zeros((total_rows, 2 * model_width), jnp.float32),
    )
    query_acc, bias_total, pair_buffer = lax.fori_loop(
        0, total_rows // block_rows, key_step, start_state
    )
    pair_grad = lax.psum_scatter(
        pair_buffer.astype(jnp.bfloat16), "ctx", scatter_dimension=0, tiled=True
    ).astype(jnp.float32)
    query_total = query_acc.reshape(local_rows, model_width)
    key_total = pair_grad[:, :model_width]
    value_total = pair_grad[:, model_width:]
    qkv_grad_low = jnp.concatenate([query_total, key_total, value_total], axis=1).astype(
        jnp.bfloat16
    )
    qkv_weight_grad = lead_dot(normed_attn_low, qkv_grad_low)
    norm_attn_grad = tail_dot(qkv_grad_low, qkv_full)
    _, norm_attn_back = jax.vjp(rms_norm, stream, gain_attn)
    stream_from_norm, gain_attn_grad = norm_attn_back(norm_attn_grad)
    hidden_grad = (resid_grad + stream_from_norm).astype(jnp.bfloat16)
    qkv_shard, out_shard, in_shard, down_shard = (
        lax.psum_scatter(
            qkv_weight_grad.astype(jnp.bfloat16), "wa", scatter_dimension=0, tiled=True
        ).astype(jnp.float32),
        lax.psum_scatter(
            out_proj_grad.astype(jnp.bfloat16), "wa", scatter_dimension=0, tiled=True
        ).astype(jnp.float32),
        lax.psum_scatter(
            in_grad.astype(jnp.bfloat16), "wa", scatter_dimension=0, tiled=True
        ).astype(jnp.float32),
        lax.psum_scatter(
            down_grad.astype(jnp.bfloat16), "wa", scatter_dimension=0, tiled=True
        ).astype(jnp.float32),
    )
    qkv_shard, out_shard = (
        lax.psum(qkv_shard.astype(jnp.bfloat16), "ctx").astype(jnp.float32),
        lax.psum(out_shard.astype(jnp.bfloat16), "ctx").astype(jnp.float32),
    )
    stat_sums, count_sum, router_sum, gain_attn_sum, gain_moe_sum, bias_sum = lax.psum(
        (stat_terms, valid_count, router_grad, gain_attn_grad, gain_moe_grad, bias_total),
        ("ctx", "wa"),
    )
    stats = jnp.sqrt(stat_sums / (count_sum * model_width))
    return (
        final.astype(jnp.bfloat16)[None],
        hidden_grad[None],
        qkv_shard,
        out_shard,
        in_shard[None],
        down_shard[None],
        router_sum,
        gain_attn_sum,
        gain_moe_sum,
        bias_sum,
        stats,
    )


BLOCK = 256


def nt_dot(left, right):
    return lax.dot_general(
        left, right, (((1,), (1,)), ((), ())), preferred_element_type=jnp.float32
    )


def plain_dot(left, right):
    return jnp.dot(left, right, preferred_element_type=jnp.float32)


def block_at(index):
    return pl.ds(pl.multiple_of(index * BLOCK, BLOCK), BLOCK)


def segment_begin(positions, bounds):
    begin = positions * 0
    for index in range(NSEQ):
        begin = jnp.where(positions >= bounds[index], bounds[index], begin)
    return begin


def fill_bias_tiles(distance_rows, tiles):
    for level in range(tiles.shape[0]):
        spread = jnp.broadcast_to(distance_rows[level : level + 1, :], (BLOCK, 2 * BLOCK))
        tiles[level] = pltpu.roll(spread, BLOCK + 1, 1, stride=1, stride_axis=0)[:, :BLOCK]


def fill_sorter(perm, sorter):
    slots = perm.shape[1]

    def step(index, carry):
        wanted = lax.broadcasted_iota(jnp.int32, (BLOCK, slots), 0) + index * BLOCK
        sorter[block_at(index), :] = jnp.where(perm[...] == wanted, 1.0, 0.0).astype(jnp.bfloat16)
        return carry

    lax.fori_loop(0, slots // BLOCK, step, 0)


def pair_mask(key_block, query_pos, query_begin):
    key_pos = lax.broadcasted_iota(jnp.int32, (BLOCK, BLOCK), 0) + key_block * BLOCK
    return (key_pos <= query_pos) & (key_pos >= query_begin)


def attention_forward_kernel(
    piece_count, head_dim, source, bounds, weight, perm, distance_rows, *refs
):
    pieces = refs[:piece_count]
    mixed, sorted_out, rows_out, wide_out, log_out = refs[piece_count : piece_count + 5]
    raw, sorter, tiles, mixed_sorted = refs[piece_count + 5 :]
    slots = perm.shape[1]
    blocks = slots // BLOCK
    local_rows = pieces[0].shape[0]
    for index in range(piece_count):
        offset = pl.multiple_of(source[index] * local_rows, local_rows)
        raw[:, pl.ds(offset, local_rows)] = nt_dot(weight[...], pieces[index][...]).astype(
            jnp.bfloat16
        )
    fill_bias_tiles(distance_rows, tiles)
    fill_sorter(perm, sorter)

    def sort_step(index, carry):
        columns = nt_dot(raw[...], sorter[block_at(index), :])
        sorted_out[:, block_at(index)] = columns.astype(jnp.bfloat16)
        rows_out[block_at(index), :] = jnp.transpose(columns[head_dim:]).astype(jnp.bfloat16)
        return carry

    lax.fori_loop(0, blocks, sort_step, 0)
    mixed_sorted[...] = jnp.zeros_like(mixed_sorted)
    total = bounds[NSEQ - 1]

    def query_step(query_block, carry):
        queries = sorted_out[:head_dim, block_at(query_block)] * 0.125
        query_pos = lax.broadcasted_iota(jnp.int32, (1, BLOCK), 1) + query_block * BLOCK
        query_begin = segment_begin(query_pos, bounds)
        first = segment_begin(query_block * BLOCK, bounds) // BLOCK

        def key_step(key_block, state):
            row_max, totals, weighted = state
            scores = plain_dot(rows_out[block_at(key_block), :head_dim], queries)
            scores = jnp.where(
                pair_mask(key_block, query_pos, query_begin),
                scores + tiles[query_block - key_block],
                MASKED_SCORE,
            )
            new_max = jnp.maximum(row_max, jnp.max(scores, axis=0, keepdims=True))
            factor = jnp.exp(row_max - new_max)
            exp_scores = jnp.exp(scores - new_max)
            totals = totals * factor + jnp.sum(exp_scores, axis=0, keepdims=True)
            values = sorted_out[2 * head_dim :, block_at(key_block)]
            weighted = weighted * factor + plain_dot(values, exp_scores.astype(jnp.bfloat16))
            return (new_max, totals, weighted)

        row_max, totals, weighted = lax.fori_loop(
            first,
            query_block + 1,
            key_step,
            (
                jnp.full((1, BLOCK), MASKED_SCORE, jnp.float32),
                jnp.zeros((1, BLOCK), jnp.float32),
                jnp.zeros((head_dim, BLOCK), jnp.float32),
            ),
        )
        outcome = jnp.where(query_pos < total, weighted / totals, 0.0)
        wide_out[:, block_at(query_block)] = outcome
        log_out[:, block_at(query_block)] = row_max + jnp.log(totals)
        mixed_sorted[:, block_at(query_block)] = outcome.astype(jnp.bfloat16)
        return carry

    lax.fori_loop(0, (total + BLOCK - 1) // BLOCK, query_step, 0)
    for index in range(blocks):
        columns = plain_dot(mixed_sorted[...], sorter[:, index * BLOCK : (index + 1) * BLOCK])
        columns = columns.astype(jnp.bfloat16)
        for part in range(BLOCK // local_rows):
            mixed[index * (BLOCK // local_rows) + part] = columns[
                :, part * local_rows : (part + 1) * local_rows
            ]


def attention_backward_kernel(
    head_dim,
    bounds,
    received,
    perm,
    distance_rows,
    sorted_in,
    rows_in,
    wide_in,
    log_in,
    sent,
    grad_out,
    distance_out,
    dout_raw,
    dout_sorted,
    delta,
    sorter,
    tiles,
    tile_grads,
    grad_acc,
    grad_sorted,
):
    slots = perm.shape[1]
    blocks = slots // BLOCK
    groups, _, local_rows = received.shape
    for index in range(groups):
        dout_raw[:, index * local_rows : (index + 1) * local_rows] = received[index]
    fill_bias_tiles(distance_rows, tiles)
    fill_sorter(perm, sorter)

    def sort_step(index, carry):
        columns = nt_dot(dout_raw[...], sorter[block_at(index), :])
        dout_sorted[:, block_at(index)] = columns.astype(jnp.bfloat16)
        return carry

    lax.fori_loop(0, blocks, sort_step, 0)
    tile_grads[...] = jnp.zeros_like(tile_grads)
    grad_acc[...] = jnp.zeros_like(grad_acc)
    total = bounds[NSEQ - 1]

    def query_step(query_block, carry):
        queries = sorted_in[:head_dim, block_at(query_block)] * 0.125
        douts = dout_sorted[:, block_at(query_block)]
        row_delta = jnp.sum(
            douts.astype(jnp.float32) * wide_in[:, block_at(query_block)], axis=0, keepdims=True
        )
        log_total = log_in[:, block_at(query_block)]
        query_pos = lax.broadcasted_iota(jnp.int32, (1, BLOCK), 1) + query_block * BLOCK
        query_begin = segment_begin(query_pos, bounds)
        inside = query_pos < total
        first = segment_begin(query_block * BLOCK, bounds) // BLOCK

        def key_step(key_block, query_grad):
            rows = rows_in[block_at(key_block), :]
            scores = plain_dot(rows[:, :head_dim], queries) + tiles[query_block - key_block]
            probs = jnp.exp(
                jnp.where(
                    pair_mask(key_block, query_pos, query_begin) & inside,
                    scores - log_total,
                    MASKED_SCORE,
                )
            )
            prob_grad = plain_dot(rows[:, head_dim:], douts)
            score_grad = (probs * (prob_grad - row_delta)).astype(jnp.bfloat16)
            tile_grads[query_block - key_block] += score_grad.astype(jnp.float32)
            grad_acc[head_dim : 2 * head_dim, block_at(key_block)] += nt_dot(queries, score_grad)
            grad_acc[2 * head_dim :, block_at(key_block)] += nt_dot(
                douts, probs.astype(jnp.bfloat16)
            )
            keys = sorted_in[head_dim : 2 * head_dim, block_at(key_block)]
            return query_grad + plain_dot(keys, score_grad)

        query_grad = lax.fori_loop(
            first, query_block + 1, key_step, jnp.zeros((head_dim, BLOCK), jnp.float32)
        )
        grad_acc[:head_dim, block_at(query_block)] = query_grad * 0.125
        return carry

    lax.fori_loop(0, (total + BLOCK - 1) // BLOCK, query_step, 0)
    grad_sorted[...] = grad_acc[...].astype(jnp.bfloat16)
    for index in range(blocks):
        columns = plain_dot(grad_sorted[...], sorter[:, index * BLOCK : (index + 1) * BLOCK])
        columns = columns.astype(jnp.bfloat16)
        grad_out[:, index * BLOCK : (index + 1) * BLOCK] = columns
        for part in range(BLOCK // local_rows):
            sent[index * (BLOCK // local_rows) + part] = columns[
                :, part * local_rows : (part + 1) * local_rows
            ]
    row_ids = lax.broadcasted_iota(jnp.int32, (BLOCK, BLOCK), 0)
    column_ids = lax.broadcasted_iota(jnp.int32, (BLOCK, BLOCK), 1)
    mirror = jnp.where(row_ids + column_ids == BLOCK - 1, 1.0, 0.0)
    for level in range(tiles.shape[0]):
        turned = jnp.dot(
            mirror, tile_grads[level], precision=TOP_PRECISION, preferred_element_type=jnp.float32
        )
        wide = jnp.concatenate([turned, jnp.zeros((BLOCK, BLOCK), jnp.float32)], axis=1)
        turned = pltpu.roll(wide, 0, 1, stride=1, stride_axis=0)
        distance_out[level : level + 1, :] = jnp.sum(turned, axis=0, keepdims=True)


def weight_gradient_kernel(piece_count, source, grads, *refs):
    pieces = refs[:piece_count]
    out = refs[piece_count]
    local_rows = pieces[0].shape[0]
    total = jnp.zeros(out.shape, jnp.float32)
    for index in range(piece_count):
        offset = pl.multiple_of(source[index] * local_rows, local_rows)
        total = total + plain_dot(grads[:, pl.ds(offset, local_rows)], pieces[index][...])
    out[...] = total


def vmem():
    return pl.BlockSpec(memory_space=pltpu.VMEM)


def smem():
    return pl.BlockSpec(memory_space=pltpu.SMEM)


def shaped(shape, dtype):
    return jax.ShapeDtypeStruct(shape, dtype)


def attention_forward(source, bounds, weight, perm, distance_rows, pieces, head_dim):
    groups = len(pieces)
    slots = perm.shape[1]
    local_rows = pieces[0].shape[0]
    levels = distance_rows.shape[0]
    flops = 2 * slots * (3 * head_dim * pieces[0].shape[1] + 4 * head_dim * slots + head_dim * slots)
    return pl.pallas_call(
        functools.partial(attention_forward_kernel, groups, head_dim),
        out_shape=(
            shaped((groups, head_dim, local_rows), jnp.bfloat16),
            shaped((3 * head_dim, slots), jnp.bfloat16),
            shaped((slots, 2 * head_dim), jnp.bfloat16),
            shaped((head_dim, slots), jnp.float32),
            shaped((1, slots), jnp.float32),
        ),
        in_specs=[smem(), smem()] + [vmem()] * (3 + groups),
        out_specs=(vmem(),) * 5,
        scratch_shapes=[
            pltpu.VMEM((3 * head_dim, slots), jnp.bfloat16),
            pltpu.VMEM((slots, slots), jnp.bfloat16),
            pltpu.VMEM((levels, BLOCK, BLOCK), jnp.float32),
            pltpu.VMEM((head_dim, slots), jnp.bfloat16),
        ],
        compiler_params=pltpu.CompilerParams(vmem_limit_bytes=48 << 20),
        cost_estimate=pl.CostEstimate(
            flops=flops, bytes_accessed=8 << 20, transcendentals=slots * slots // 4
        ),
    )(source, bounds, weight, perm, distance_rows, *pieces)


def attention_backward(bounds, received, perm, distance_rows, saved, head_dim):
    slots = perm.shape[1]
    groups, _, local_rows = received.shape
    levels = distance_rows.shape[0]
    return pl.pallas_call(
        functools.partial(attention_backward_kernel, head_dim),
        out_shape=(
            shaped((groups, 3 * head_dim, local_rows), jnp.bfloat16),
            shaped((3 * head_dim, slots), jnp.bfloat16),
            shaped((levels, 2 * BLOCK), jnp.float32),
        ),
        in_specs=[smem()] + [vmem()] * 7,
        out_specs=(vmem(),) * 3,
        scratch_shapes=[
            pltpu.VMEM((head_dim, slots), jnp.bfloat16),
            pltpu.VMEM((head_dim, slots), jnp.bfloat16),
            pltpu.VMEM((1, slots), jnp.float32),
            pltpu.VMEM((slots, slots), jnp.bfloat16),
            pltpu.VMEM((levels, BLOCK, BLOCK), jnp.float32),
            pltpu.VMEM((levels, BLOCK, BLOCK), jnp.float32),
            pltpu.VMEM((3 * head_dim, slots), jnp.float32),
            pltpu.VMEM((3 * head_dim, slots), jnp.bfloat16),
        ],
        compiler_params=pltpu.CompilerParams(vmem_limit_bytes=48 << 20),
        cost_estimate=pl.CostEstimate(
            flops=2 * slots * slots * 6 * head_dim,
            bytes_accessed=4 << 20,
            transcendentals=slots * slots // 4,
        ),
    )(bounds, received, perm, distance_rows, *saved)


def weight_gradient(source, grads, pieces):
    width = pieces[0].shape[1]
    return pl.pallas_call(
        functools.partial(weight_gradient_kernel, len(pieces)),
        out_shape=shaped((grads.shape[0], width), jnp.float32),
        in_specs=[smem(), vmem()] + [vmem()] * len(pieces),
        out_specs=vmem(),
        compiler_params=pltpu.CompilerParams(vmem_limit_bytes=32 << 20),
        cost_estimate=pl.CostEstimate(
            flops=2 * grads.shape[0] * grads.shape[1] * width,
            bytes_accessed=6 << 20,
            transcendentals=0,
        ),
    )(source, grads, *pieces)


class Ring:
    def __init__(self, groups):
        self.chips = groups // 2
        order = list(range(0, self.chips, 2)) + list(range(1, self.chips, 2))[::-1]
        self.order = order
        self.forward = self.shift(1)
        self.backward = self.shift(-1)
        self.swap = [(index, index ^ 1) for index in range(groups)]
        self.same_core = [[2 * chip + core for chip in range(self.chips)] for core in range(2)]
        table = np.zeros((groups, groups), np.int32)
        for at, chip in enumerate(order):
            for core in range(2):
                steps = self.offsets()
                near = [2 * order[(at + step) % self.chips] + core for step in steps]
                table[2 * chip + core] = near + [index ^ 1 for index in near]
        self.table = table

    def offsets(self):
        steps = [0]
        for step in range(1, (self.chips + 1) // 2):
            steps += [-step, step]
        return steps + ([self.chips // 2] if self.chips % 2 == 0 else [])

    def shift(self, step):
        return [
            (2 * self.order[at] + core, 2 * self.order[(at + step) % self.chips] + core)
            for at in range(self.chips)
            for core in range(2)
        ]

    def swapped(self, piece):
        return lax.ppermute(piece, "ctx", self.swap)

    def gather(self, piece):
        pieces = [piece]
        ahead = behind = piece
        for _ in range(1, (self.chips + 1) // 2):
            ahead = lax.ppermute(ahead, "ctx", self.forward)
            behind = lax.ppermute(behind, "ctx", self.backward)
            pieces += [ahead, behind]
        if self.chips % 2 == 0:
            half = piece.shape[0] // 2
            pieces.append(
                jnp.concatenate(
                    [
                        lax.ppermute(ahead[:half], "ctx", self.forward),
                        lax.ppermute(behind[half:], "ctx", self.backward),
                    ],
                    axis=0,
                )
            )
        return pieces + [self.swapped(item) for item in pieces]


def across(values):
    return lax.ppermute(values, "wa", [(0, 1), (1, 0)])


def all_sum(values, groups):
    stride = 1
    while stride < groups:
        values = values + lax.ppermute(
            values, "ctx", [(index, index ^ stride) for index in range(groups)]
        )
        stride *= 2
    return values + across(values)


def flat_pack(parts, rows):
    flat = jnp.concatenate([part.reshape(-1) for part in parts])
    return jnp.pad(flat, (0, rows * 128 - flat.shape[0])).reshape(rows, 128)


def fast_device(
    hidden_in,
    out_grad,
    lengths,
    permutation,
    routes,
    bucket_table,
    w_qkv,
    w_out,
    w_in,
    w_down,
    w_router,
    gain_attn,
    gain_moe,
    rel_bias,
):
    stream = hidden_in[0].astype(jnp.float32)
    local_rows, width = stream.shape
    bucket_count, head_count = rel_bias.shape
    head_dim = width // head_count
    experts = w_router.shape[1]
    slot_cap = 4 * local_rows // experts
    groups = lax.axis_size("ctx")
    half_width = width // 2
    ring = Ring(groups)
    ctx = lax.axis_index("ctx")
    core = ctx % 2
    on_low = lax.axis_index("wa") == 0
    perm_row = permutation[0]
    slots = perm_row.shape[0]
    bounds = jnp.cumsum(lengths[0])
    own_start = ctx * local_rows
    query_pos = lax.dynamic_slice_in_dim(perm_row, own_start, local_rows, 0)
    is_valid = (segment_of(query_pos, bounds) < NSEQ).astype(jnp.float32)
    source = lax.dynamic_index_in_dim(jnp.asarray(ring.table), ctx, 0, keepdims=False)

    def in_order(own, other, axis):
        return jnp.where(
            on_low,
            jnp.concatenate([own, other], axis=axis),
            jnp.concatenate([other, own], axis=axis),
        )

    def own_first(values):
        low, high = values[:, :half_width], values[:, half_width:]
        return jnp.where(on_low, values, jnp.concatenate([high, low], axis=1))

    def other_half(weight):
        half = weight.shape[0] // 2
        mine = across(lax.dynamic_slice_in_dim(weight, core * half, half, 0))
        theirs = ring.swapped(mine)
        return jnp.where(
            core == 0,
            jnp.concatenate([mine, theirs], axis=0),
            jnp.concatenate([theirs, mine], axis=0),
        )

    head_weight = jnp.concatenate(
        [
            lax.dynamic_slice_in_dim(w_qkv, block * width + ctx * head_dim, head_dim, 1)
            for block in range(3)
        ],
        axis=1,
    ).T
    head_weight = in_order(head_weight, across(head_weight), 1)
    out_own, out_other = w_out, other_half(w_out)
    in_weight = jnp.concatenate([w_in[0], across(w_in[0])], axis=0)
    down_weight = jnp.concatenate([w_down[0], across(w_down[0])], axis=0)
    qkv_other = other_half(w_qkv)

    head_hot = (jnp.arange(head_count, dtype=jnp.int32) == ctx).astype(jnp.float32)
    head_bias = jnp.sum(rel_bias * head_hot[None, :], axis=1)
    reach = bucket_table.shape[0]
    bucket_hot = bucket_table[:, None] == jnp.arange(bucket_count, dtype=jnp.int32)[None, :]
    by_distance = jnp.sum(jnp.where(bucket_hot, head_bias[None, :], 0.0), axis=1)
    levels = reach // BLOCK + 1
    padded = jnp.pad(by_distance, (BLOCK - 1, levels * BLOCK + BLOCK - reach + 1))
    distance_rows = jnp.stack(
        [padded[level * BLOCK : level * BLOCK + 2 * BLOCK] for level in range(levels)]
    )

    normed_attn_low = rms_norm(stream, gain_attn).astype(jnp.bfloat16)
    pieces = ring.gather(normed_attn_low)
    perm_lanes = perm_row[None, :]
    mixed, *saved = attention_forward(
        source, bounds, head_weight, perm_lanes, distance_rows, pieces, head_dim
    )
    mixed = lax.all_to_all(mixed, "ctx", split_axis=0, concat_axis=0, tiled=True)
    mixed = mixed.reshape(width, local_rows)
    mixed_low, mixed_high = mixed[:half_width], mixed[half_width:]
    mixed_own = jnp.where(on_low, mixed_low, mixed_high)
    mixed_other = jnp.where(on_low, mixed_high, mixed_low)
    attn_out = lead_dot(mixed_own, out_own) + lead_dot(mixed_other, out_other)
    resid = stream + attn_out
    normed_moe_low = rms_norm(resid, gain_moe).astype(jnp.bfloat16)
    normed_moe_wide = normed_moe_low.astype(jnp.float32)
    logits = jnp.dot(normed_moe_wide, w_router, precision=TOP_PRECISION)
    route_rows = routes[0]
    expert_ids = jnp.arange(experts, dtype=jnp.int32)
    first_hot = route_rows[:, 0:1] == expert_ids[None, :]
    second_hot = route_rows[:, 1:2] == expert_ids[None, :]
    chosen = jnp.stack(
        [
            jnp.sum(jnp.where(first_hot, logits, 0.0), axis=1),
            jnp.sum(jnp.where(second_hot, logits, 0.0), axis=1),
        ],
        axis=1,
    )
    gate_probs = jax.nn.softmax(chosen, axis=1)
    counts = jnp.cumsum((first_hot | second_hot).astype(jnp.int32), axis=0)
    first_slot = jnp.sum(jnp.where(first_hot, counts - 1, 0), axis=1)
    second_slot = jnp.sum(jnp.where(second_hot, counts - 1, 0), axis=1)
    first_lane = route_rows[:, 0] * slot_cap + first_slot
    second_lane = route_rows[:, 1] * slot_cap + second_slot
    lane_ids = jnp.arange(experts * slot_cap, dtype=jnp.int32)
    first_at = first_lane[:, None] == lane_ids[None, :]
    second_at = second_lane[:, None] == lane_ids[None, :]
    first_pick = first_at.astype(jnp.bfloat16)
    second_pick = second_at.astype(jnp.bfloat16)
    any_pick = (first_at | second_at).astype(jnp.bfloat16)

    def exchange(values):
        return lax.all_to_all(
            values,
            "ctx",
            split_axis=0,
            concat_axis=0,
            tiled=True,
            axis_index_groups=ring.same_core,
        )

    def to_experts(rows):
        mine = exchange(rows)
        return jnp.concatenate([mine, ring.swapped(mine)], axis=0)

    def from_experts(rows):
        count = rows.shape[0] // 2
        theirs = ring.swapped(rows[count:].astype(jnp.bfloat16))
        return exchange((rows[:count] + theirs.astype(jnp.float32)).astype(jnp.bfloat16))

    rows = to_experts(lead_dot(any_pick, own_first(normed_moe_low)).astype(jnp.bfloat16))
    grad_final = out_grad[0].astype(jnp.float32)
    slot_gate = jnp.sum(
        jnp.where(first_at, gate_probs[:, 0:1], 0.0)
        + jnp.where(second_at, gate_probs[:, 1:2], 0.0),
        axis=0,
    )
    dy_slots = slot_gate[:, None] * lead_dot(any_pick, own_first(out_grad[0]))
    rows_grad = to_experts(dy_slots.astype(jnp.bfloat16))

    gate_up = jnp.dot(rows, in_weight, preferred_element_type=jnp.float32)
    hidden_rows, act_back = jax.vjp(glu_act, gate_up)
    hidden = hidden_rows.astype(jnp.bfloat16)
    part = tail_dot(hidden, down_weight)
    returned = own_first(from_experts(part))
    picked_first = plain_dot(first_pick, returned)
    picked_second = plain_dot(second_pick, returned)
    moe_out = gate_probs[:, 0:1] * picked_first + gate_probs[:, 1:2] * picked_second
    final = resid + moe_out

    hidden_grad_rows = jnp.dot(rows_grad, down_weight, preferred_element_type=jnp.float32)
    (gate_up_grad,) = act_back(hidden_grad_rows)
    gate_up_low = gate_up_grad.astype(jnp.bfloat16)
    rows_back = own_first(from_experts(tail_dot(gate_up_low, in_weight)))
    in_other = across(lead_dot(rows[:, half_width:], gate_up_low).astype(jnp.bfloat16))
    down_other = across(lead_dot(rows_grad[:, half_width:], hidden).astype(jnp.bfloat16))
    in_shard = lead_dot(rows[:, :half_width], gate_up_low) + in_other.astype(jnp.float32)
    down_shard = lead_dot(rows_grad[:, :half_width], hidden) + down_other.astype(jnp.float32)

    valid_col = is_valid[:, None]
    stat_terms = jnp.stack(
        [
            jnp.sum(valid_col * final * final),
            jnp.sum(valid_col * attn_out * attn_out),
            jnp.sum(valid_col * moe_out * moe_out),
            jnp.sum(is_valid),
        ]
    )
    gate_grad = jnp.stack(
        [jnp.sum(grad_final * picked_first, axis=1), jnp.sum(grad_final * picked_second, axis=1)],
        axis=1,
    )
    _, gate_back = jax.vjp(lambda chosen_in: jax.nn.softmax(chosen_in, axis=1), chosen)
    (chosen_grad,) = gate_back(gate_grad)
    logit_grad = jnp.where(first_hot, chosen_grad[:, 0:1], 0.0) + jnp.where(
        second_hot, chosen_grad[:, 1:2], 0.0
    )
    router_grad = lead_dot(normed_moe_wide, logit_grad, TOP_PRECISION)
    norm_moe_grad = jnp.dot(logit_grad, w_router.T, precision=TOP_PRECISION)
    norm_moe_grad = norm_moe_grad + plain_dot(any_pick, rows_back)
    _, norm_moe_back = jax.vjp(rms_norm, resid, gain_moe)
    resid_from_norm, gain_moe_grad = norm_moe_back(norm_moe_grad)
    resid_grad = grad_final + resid_from_norm
    attn_grad_low = resid_grad.astype(jnp.bfloat16)

    mix_grad = in_order(tail_dot(out_own, attn_grad_low), tail_dot(out_other, attn_grad_low), 0)
    dout = lax.all_to_all(
        mix_grad.astype(jnp.bfloat16).reshape(groups, head_dim, local_rows),
        "ctx",
        split_axis=0,
        concat_axis=0,
        tiled=True,
    )
    out_from_other = across(plain_dot(mixed_other, attn_grad_low).astype(jnp.bfloat16))
    out_shard = plain_dot(mixed_own, attn_grad_low) + out_from_other.astype(jnp.float32)
    out_shard = lax.psum(out_shard.astype(jnp.bfloat16), "ctx").astype(jnp.float32)

    sent, head_grads, distance_grads = attention_backward(
        bounds, dout, perm_lanes, distance_rows, saved, head_dim
    )
    qkv_grad = lax.all_to_all(sent, "ctx", split_axis=0, concat_axis=0, tiled=True)
    qkv_grad = jnp.transpose(qkv_grad.reshape(head_count, 3, head_dim, local_rows), (1, 0, 2, 3))
    qkv_grad = qkv_grad.reshape(3 * width, local_rows)

    def feature_grad(weight):
        return lax.dot_general(
            qkv_grad, weight, (((0,), (1,)), ((), ())), preferred_element_type=jnp.float32
        )

    norm_attn_grad = in_order(feature_grad(w_qkv), feature_grad(qkv_other), 1)
    _, norm_attn_back = jax.vjp(rms_norm, stream, gain_attn)
    stream_from_norm, gain_attn_grad = norm_attn_back(norm_attn_grad)
    hidden_grad = (resid_grad + stream_from_norm).astype(jnp.bfloat16)

    head_total = weight_gradient(source, head_grads, pieces)
    low_part, high_part = head_total[:, :half_width], head_total[:, half_width:]
    head_other = across(jnp.where(on_low, high_part, low_part).astype(jnp.bfloat16))
    head_shard = jnp.where(on_low, low_part, high_part) + head_other.astype(jnp.float32)
    gathered = jnp.stack(ring.gather(head_shard.astype(jnp.bfloat16)))
    back = lax.dynamic_index_in_dim(
        jnp.asarray(np.argsort(ring.table, axis=1).astype(np.int32)), ctx, 0, keepdims=False
    )
    gathered = jnp.take(gathered, back, axis=0)
    gathered = gathered.reshape(head_count, 3, head_dim, half_width)
    qkv_shard = jnp.transpose(gathered, (3, 1, 0, 2)).reshape(half_width, 3 * width)
    qkv_shard = qkv_shard.astype(jnp.float32)

    spread_len = levels * BLOCK + BLOCK
    by_distance_grad = sum(
        jnp.pad(distance_grads[level], (level * BLOCK, spread_len - (level + 2) * BLOCK))
        for level in range(levels)
    )[BLOCK - 1 : BLOCK - 1 + reach]
    head_bias_grad = jnp.sum(jnp.where(bucket_hot, by_distance_grad[:, None], 0.0), axis=0)
    bias_grad = head_bias_grad[:, None] * head_hot[None, :]

    early = all_sum(flat_pack((router_grad, gain_moe_grad, stat_terms), 80), groups)
    late = all_sum(flat_pack((gain_attn_grad, bias_grad), 16), groups)
    early, late = early.reshape(-1), late.reshape(-1)
    router_sum = early[: width * experts].reshape(width, experts)
    gain_moe_sum = early[width * experts : width * (experts + 1)]
    sums = early[width * (experts + 1) : width * (experts + 1) + 4]
    gain_attn_sum = late[:width]
    bias_sum = late[width : width + bucket_count * head_count].reshape(bucket_count, head_count)
    stats = jnp.sqrt(sums[:3] / (sums[3] * width))
    return (
        final.astype(jnp.bfloat16)[None],
        hidden_grad[None],
        qkv_shard,
        out_shard,
        in_shard[None],
        down_shard[None],
        router_sum,
        gain_attn_sum,
        gain_moe_sum,
        bias_sum,
        stats,
    )


def choose_device(groups, planes, *arguments):
    w_router, rel_bias = arguments[10], arguments[13]
    local_rows = arguments[0].shape[1]
    fits = (
        planes == 2
        and rel_bias.shape[1] == groups
        and 2 * w_router.shape[1] == groups
        and local_rows == 128
    )
    return (fast_device if fits else general_device)(*arguments)


def solution(mesh):
    per_device = functools.partial(choose_device, mesh.shape["ctx"], mesh.shape["wa"])
    placed = (
        P("wa", "ctx", None),
        P("wa", "ctx", None),
        P("wa", None),
        P("wa", None),
        P("wa", "ctx", None),
        P(),
        P("wa", None),
        P("wa", None),
        P("ctx", "wa", None),
        P("ctx", "wa", None),
        P(),
        P(),
        P(),
        P(),
    )
    return jax.shard_map(
        per_device,
        mesh=mesh,
        in_specs=placed,
        out_specs=(
            P("wa", "ctx", None),
            P("wa", "ctx", None),
            P("wa", None),
            P("wa", None),
            P("ctx", "wa", None),
            P("ctx", "wa", None),
            P(),
            P(),
            P(),
            P(),
            P(),
        ),
        check_vma=False,
    )
```

```python
import math

import jax
import jax.numpy as jnp
from jax import lax
from jax.experimental import pallas as pl
from jax.experimental.pallas import tpu as pltpu
from jax.sharding import PartitionSpec as P
import functools
import numpy as np

NSEQ = 8


NORM_EPSILON = 1e-06
MASKED_SCORE = -1e30
TOP_PRECISION = lax.Precision.HIGHEST


def rms_norm(features, scale_gain):
    return (
        features
        * lax.rsqrt(jnp.mean(features * features, axis=-1, keepdims=True) + NORM_EPSILON)
        * scale_gain
    )


def glu_act(gate_up):
    middle = gate_up.shape[-1] // 2
    return jax.nn.gelu(gate_up[..., :middle], approximate=True) * gate_up[..., middle:]


def segment_of(positions, bounds):
    return jnp.sum((positions[:, None] >= bounds[None, :]).astype(jnp.int32), axis=1)


def lead_dot(left, right, precision=None):
    return lax.dot_general(
        left,
        right,
        (((0,), (0,)), ((), ())),
        precision=precision,
        preferred_element_type=jnp.float32,
    )


def tail_dot(left, right):
    return lax.dot_general(
        left, right, (((1,), (1,)), ((), ())), preferred_element_type=jnp.float32
    )


def pair_scores(
    queries, key_rows, query_pos, query_seg, key_pos, key_seg, bucket_starts, bias_table
):
    bucket_count = bias_table.shape[0]
    raw_scores = jnp.einsum("qhd,khd->hqk", queries, key_rows, preferred_element_type=jnp.float32)
    distance = query_pos[:, None] - key_pos[None, :]
    clipped = jnp.maximum(distance, 0)
    bucket_ids = jnp.sum(
        (clipped[:, :, None] >= bucket_starts[None, None, 1:]).astype(jnp.int32), axis=2
    )
    bucket_hot = (
        bucket_ids[:, :, None] == jnp.arange(bucket_count, dtype=jnp.int32)[None, None, :]
    ).astype(jnp.float32)
    bias_block = jnp.einsum("qkb,bh->hqk", bucket_hot, bias_table, precision=TOP_PRECISION)
    scores = raw_scores * 0.125 + bias_block
    allowed = (
        (query_seg[:, None] == key_seg[None, :]) & (distance >= 0) & (query_seg[:, None] < NSEQ)
    )
    return (scores, allowed, bucket_hot)


def attend_piece(
    running, pieces, queries, query_pos, query_seg, perm_row, bounds, bucket_starts, bias_table
):
    key_rows, value_rows = pieces
    piece_rows = key_rows.shape[0]
    head_count = queries.shape[1]
    block_rows = math.gcd(piece_rows, 512)
    keys_split = key_rows.reshape(piece_rows, head_count, -1)
    values_split = value_rows.reshape(piece_rows, head_count, -1)

    def step(step_index, state):
        row_max, totals, weighted = state
        offset = step_index * block_rows
        key_block = lax.dynamic_slice_in_dim(keys_split, offset, block_rows, 0)
        value_block = lax.dynamic_slice_in_dim(values_split, offset, block_rows, 0)
        key_pos = lax.dynamic_slice_in_dim(perm_row, offset, block_rows, 0)
        key_seg = segment_of(key_pos, bounds)
        scores, allowed, _ = pair_scores(
            queries, key_block, query_pos, query_seg, key_pos, key_seg, bucket_starts, bias_table
        )
        new_max = jnp.maximum(row_max, jnp.max(jnp.where(allowed, scores, MASKED_SCORE), axis=2))
        factor = jnp.exp(row_max - new_max)
        exp_scores = jnp.exp(jnp.where(allowed, scores - new_max[:, :, None], MASKED_SCORE))
        totals = totals * factor + jnp.sum(exp_scores, axis=2)
        weighted = weighted * factor[:, :, None] + jnp.einsum(
            "hqk,khd->hqd",
            exp_scores.astype(jnp.bfloat16),
            value_block,
            preferred_element_type=jnp.float32,
        )
        return (new_max, totals, weighted)

    return lax.fori_loop(0, piece_rows // block_rows, step, running)


def block_grads(
    queries,
    dout_low,
    log_total,
    row_delta,
    query_pos,
    query_seg,
    key_block,
    value_block,
    key_pos,
    key_seg,
    bucket_starts,
    bias_table,
):
    scores, allowed, bucket_hot = pair_scores(
        queries, key_block, query_pos, query_seg, key_pos, key_seg, bucket_starts, bias_table
    )
    attn_probs = jnp.exp(jnp.where(allowed, scores - log_total[:, :, None], MASKED_SCORE))
    prob_grad = jnp.einsum(
        "qhd,khd->hqk", dout_low, value_block, preferred_element_type=jnp.float32
    )
    score_grad = (attn_probs * (prob_grad - row_delta[:, :, None])).astype(jnp.bfloat16)
    query_grad = 0.125 * jnp.einsum(
        "hqk,khd->qhd", score_grad, key_block, preferred_element_type=jnp.float32
    )
    key_grad = 0.125 * jnp.einsum(
        "hqk,qhd->khd", score_grad, queries, preferred_element_type=jnp.float32
    )
    value_grad = jnp.einsum(
        "hqk,qhd->khd",
        attn_probs.astype(jnp.bfloat16),
        dout_low,
        preferred_element_type=jnp.float32,
    )
    bias_grad = jnp.einsum(
        "hqk,qkb->bh",
        score_grad,
        bucket_hot.astype(jnp.bfloat16),
        preferred_element_type=jnp.float32,
    )
    return (query_grad, key_grad, value_grad, bias_grad)


def general_device(
    hidden_in,
    out_grad,
    lengths,
    permutation,
    routes,
    bucket_table,
    w_qkv,
    w_out,
    w_in,
    w_down,
    w_router,
    gain_attn,
    gain_moe,
    rel_bias,
):
    stream = hidden_in[0].astype(jnp.float32)
    local_rows = stream.shape[0]
    model_width = stream.shape[1]
    head_count = rel_bias.shape[1]
    bucket_count = rel_bias.shape[0]
    head_dim = model_width // head_count
    experts = w_router.shape[1]
    slot_cap = 4 * local_rows // experts
    groups = lax.axis_size("ctx")
    perm_row = permutation[0]
    bounds = jnp.cumsum(lengths[0])
    own_start = lax.axis_index("ctx") * local_rows
    query_pos = lax.dynamic_slice_in_dim(perm_row, own_start, local_rows, 0)
    query_seg = segment_of(query_pos, bounds)
    is_valid = (query_seg < NSEQ).astype(jnp.float32)
    bucket_starts = jnp.sum(
        (bucket_table[:, None] < jnp.arange(bucket_count, dtype=jnp.int32)[None, :]).astype(
            jnp.int32
        ),
        axis=0,
    )
    qkv_full, out_full, in_full, down_full = (
        lax.all_gather(w_qkv, "wa", axis=0, tiled=True),
        lax.all_gather(w_out, "wa", axis=0, tiled=True),
        lax.all_gather(w_in[0], "wa", axis=0, tiled=True),
        lax.all_gather(w_down[0], "wa", axis=0, tiled=True),
    )
    normed_attn = rms_norm(stream, gain_attn)
    normed_attn_low = normed_attn.astype(jnp.bfloat16)
    qkv = jnp.dot(normed_attn_low, qkv_full, preferred_element_type=jnp.float32).astype(
        jnp.bfloat16
    )
    queries = qkv[:, :model_width].reshape(local_rows, head_count, head_dim)
    key_rows = qkv[:, model_width : 2 * model_width]
    value_rows = qkv[:, 2 * model_width :]
    initial = (
        jnp.full((head_count, local_rows), MASKED_SCORE, jnp.float32),
        jnp.zeros((head_count, local_rows), jnp.float32),
        jnp.zeros((head_count, local_rows, head_dim), jnp.float32),
    )
    row_max, totals, weighted = attend_piece(
        initial,
        (
            lax.all_gather(key_rows, "ctx", axis=0, tiled=True),
            lax.all_gather(value_rows, "ctx", axis=0, tiled=True),
        ),
        queries,
        query_pos,
        query_seg,
        perm_row,
        bounds,
        bucket_starts,
        rel_bias,
    )
    safe_totals = jnp.where(query_seg[None, :] < NSEQ, totals, 1.0)
    log_total = row_max + jnp.log(safe_totals)
    attn_heads = weighted / safe_totals[:, :, None]
    attn_mix = jnp.transpose(attn_heads, (1, 0, 2)).reshape(local_rows, model_width)
    attn_low = attn_mix.astype(jnp.bfloat16)
    attn_out = jnp.dot(attn_low, out_full, preferred_element_type=jnp.float32)
    resid = stream + attn_out
    normed_moe = rms_norm(resid, gain_moe)
    normed_moe_low = normed_moe.astype(jnp.bfloat16)
    normed_moe_wide = normed_moe_low.astype(jnp.float32)
    logits = jnp.dot(normed_moe_wide, w_router, precision=TOP_PRECISION)
    route_rows = routes[0]
    expert_ids = jnp.arange(experts, dtype=jnp.int32)
    first_hot = route_rows[:, 0:1] == expert_ids[None, :]
    second_hot = route_rows[:, 1:2] == expert_ids[None, :]
    chosen = jnp.stack(
        [
            jnp.sum(jnp.where(first_hot, logits, 0.0), axis=1),
            jnp.sum(jnp.where(second_hot, logits, 0.0), axis=1),
        ],
        axis=1,
    )
    gate_probs = jax.nn.softmax(chosen, axis=1)
    counts = jnp.cumsum((first_hot | second_hot).astype(jnp.int32), axis=0)
    first_slot = jnp.sum(jnp.where(first_hot, counts - 1, 0), axis=1)
    second_slot = jnp.sum(jnp.where(second_hot, counts - 1, 0), axis=1)
    first_lane = route_rows[:, 0] * slot_cap + first_slot
    second_lane = route_rows[:, 1] * slot_cap + second_slot
    lane_ids = jnp.arange(experts * slot_cap, dtype=jnp.int32)
    first_pick = (first_lane[:, None] == lane_ids[None, :]).astype(jnp.bfloat16)
    second_pick = (second_lane[:, None] == lane_ids[None, :]).astype(jnp.bfloat16)
    dispatch = (
        lead_dot(first_pick, normed_moe_low) + lead_dot(second_pick, normed_moe_low)
    ).astype(jnp.bfloat16)
    spread = jnp.broadcast_to(
        dispatch.reshape(experts, 1, slot_cap, model_width), (experts, 2, slot_cap, model_width)
    ).reshape(groups, slot_cap, model_width)
    received = lax.all_to_all(spread, "ctx", split_axis=0, concat_axis=0, tiled=True)
    item_count = received.shape[1]
    row_block = received.reshape(-1, model_width)
    gate_up = jnp.dot(row_block, in_full, preferred_element_type=jnp.float32)
    hidden = glu_act(gate_up).astype(jnp.bfloat16)
    partial_value = tail_dot(hidden, down_full).astype(jnp.bfloat16)
    returned = lax.all_to_all(
        partial_value.reshape(groups, item_count, model_width),
        "ctx",
        split_axis=0,
        concat_axis=0,
        tiled=True,
    )
    returned, gate_up_kept, received_kept = (
        returned,
        gate_up.reshape(groups, item_count, -1),
        received,
    )
    halves = returned.reshape(experts, 2, slot_cap, model_width)
    first_half = halves[:, 0].reshape(-1, model_width)
    second_half = halves[:, 1].reshape(-1, model_width)
    picked_first = jnp.dot(first_pick, first_half, preferred_element_type=jnp.float32) + jnp.dot(
        first_pick, second_half, preferred_element_type=jnp.float32
    )
    picked_second = jnp.dot(second_pick, first_half, preferred_element_type=jnp.float32) + jnp.dot(
        second_pick, second_half, preferred_element_type=jnp.float32
    )
    moe_out = gate_probs[:, 0:1] * picked_first + gate_probs[:, 1:2] * picked_second
    final = resid + moe_out
    valid_col = is_valid[:, None]
    stat_terms = jnp.stack(
        [
            jnp.sum(valid_col * final * final),
            jnp.sum(valid_col * attn_out * attn_out),
            jnp.sum(valid_col * moe_out * moe_out),
        ]
    )
    valid_count = jnp.sum(is_valid)
    grad_final = out_grad[0].astype(jnp.float32)
    first_dy = (gate_probs[:, 0:1] * grad_final).astype(jnp.bfloat16)
    second_dy = (gate_probs[:, 1:2] * grad_final).astype(jnp.bfloat16)
    gate_grad = jnp.stack(
        [jnp.sum(grad_final * picked_first, axis=1), jnp.sum(grad_final * picked_second, axis=1)],
        axis=1,
    )
    _, gate_back = jax.vjp(lambda chosen_in: jax.nn.softmax(chosen_in, axis=1), chosen)
    (chosen_grad,) = gate_back(gate_grad)
    logit_grad = jnp.where(first_hot, chosen_grad[:, 0:1], 0.0) + jnp.where(
        second_hot, chosen_grad[:, 1:2], 0.0
    )
    router_grad = lead_dot(normed_moe_wide, logit_grad, TOP_PRECISION)
    norm_moe_grad = jnp.dot(logit_grad, w_router.T, precision=TOP_PRECISION)
    dy_slots = (lead_dot(first_pick, first_dy) + lead_dot(second_pick, second_dy)).astype(
        jnp.bfloat16
    )
    dy_spread = jnp.broadcast_to(
        dy_slots.reshape(experts, 1, slot_cap, model_width), (experts, 2, slot_cap, model_width)
    ).reshape(groups, slot_cap, model_width)
    received_grad = lax.all_to_all(dy_spread, "ctx", split_axis=0, concat_axis=0, tiled=True)
    rows_grad = received_grad.reshape(-1, model_width)
    rows_kept = received_kept.reshape(-1, model_width)
    gate_up_rows = gate_up_kept.reshape(rows_grad.shape[0], -1)
    hidden_rows, act_back = jax.vjp(glu_act, gate_up_rows)
    hidden_low = hidden_rows.astype(jnp.bfloat16)
    hidden_grad_rows = jnp.dot(rows_grad, down_full, preferred_element_type=jnp.float32)
    down_grad = lead_dot(rows_grad, hidden_low)
    (gate_up_grad,) = act_back(hidden_grad_rows)
    gate_up_low = gate_up_grad.astype(jnp.bfloat16)
    in_grad = lead_dot(rows_kept, gate_up_low)
    rows_back = tail_dot(gate_up_low, in_full).astype(jnp.bfloat16)
    returned_grad = lax.all_to_all(
        rows_back.reshape(groups, slot_cap, model_width),
        "ctx",
        split_axis=0,
        concat_axis=0,
        tiled=True,
    )
    grad_halves = returned_grad.reshape(experts, 2, slot_cap, model_width)
    first_back = grad_halves[:, 0].reshape(-1, model_width)
    second_back = grad_halves[:, 1].reshape(-1, model_width)
    norm_moe_grad = (
        norm_moe_grad
        + jnp.dot(first_pick, first_back, preferred_element_type=jnp.float32)
        + jnp.dot(first_pick, second_back, preferred_element_type=jnp.float32)
    )
    norm_moe_grad = (
        norm_moe_grad
        + jnp.dot(second_pick, first_back, preferred_element_type=jnp.float32)
        + jnp.dot(second_pick, second_back, preferred_element_type=jnp.float32)
    )
    _, norm_moe_back = jax.vjp(rms_norm, resid, gain_moe)
    resid_from_norm, gain_moe_grad = norm_moe_back(norm_moe_grad)
    resid_grad = grad_final + resid_from_norm
    attn_grad_low = resid_grad.astype(jnp.bfloat16)
    out_proj_grad = lead_dot(attn_low, attn_grad_low)
    mix_grad = tail_dot(attn_grad_low, out_full)
    dout_low = mix_grad.astype(jnp.bfloat16).reshape(local_rows, head_count, head_dim)
    row_delta = jnp.einsum("qhd,hqd->hq", dout_low.astype(jnp.float32), attn_heads)
    key_all, value_all = (
        lax.all_gather(key_rows, "ctx", axis=0, tiled=True),
        lax.all_gather(value_rows, "ctx", axis=0, tiled=True),
    )
    total_rows = key_all.shape[0]
    block_rows = math.gcd(total_rows, 512)
    keys_split = key_all.reshape(total_rows, head_count, head_dim)
    values_split = value_all.reshape(total_rows, head_count, head_dim)
    seg_all = segment_of(perm_row, bounds)

    def key_step(step_index, state):
        query_acc, bias_acc, pair_buffer = state
        offset = step_index * block_rows
        key_block = lax.dynamic_slice_in_dim(keys_split, offset, block_rows, 0)
        value_block = lax.dynamic_slice_in_dim(values_split, offset, block_rows, 0)
        key_pos = lax.dynamic_slice_in_dim(perm_row, offset, block_rows, 0)
        key_seg = lax.dynamic_slice_in_dim(seg_all, offset, block_rows, 0)
        query_grad, key_grad, value_grad, bias_grad = block_grads(
            queries,
            dout_low,
            log_total,
            row_delta,
            query_pos,
            query_seg,
            key_block,
            value_block,
            key_pos,
            key_seg,
            bucket_starts,
            rel_bias,
        )
        joined = jnp.concatenate(
            [
                key_grad.reshape(block_rows, model_width),
                value_grad.reshape(block_rows, model_width),
            ],
            axis=1,
        )
        pair_buffer = lax.dynamic_update_slice_in_dim(pair_buffer, joined, offset, 0)
        return (query_acc + query_grad, bias_acc + bias_grad, pair_buffer)

    start_state = (
        jnp.zeros((local_rows, head_count, head_dim), jnp.float32),
        jnp.zeros((bucket_count, head_count), jnp.float32),
        jnp.zeros((total_rows, 2 * model_width), jnp.float32),
    )
    query_acc, bias_total, pair_buffer = lax.fori_loop(
        0, total_rows // block_rows, key_step, start_state
    )
    pair_grad = lax.psum_scatter(
        pair_buffer.astype(jnp.bfloat16), "ctx", scatter_dimension=0, tiled=True
    ).astype(jnp.float32)
    query_total = query_acc.reshape(local_rows, model_width)
    key_total = pair_grad[:, :model_width]
    value_total = pair_grad[:, model_width:]
    qkv_grad_low = jnp.concatenate([query_total, key_total, value_total], axis=1).astype(
        jnp.bfloat16
    )
    qkv_weight_grad = lead_dot(normed_attn_low, qkv_grad_low)
    norm_attn_grad = tail_dot(qkv_grad_low, qkv_full)
    _, norm_attn_back = jax.vjp(rms_norm, stream, gain_attn)
    stream_from_norm, gain_attn_grad = norm_attn_back(norm_attn_grad)
    hidden_grad = (resid_grad + stream_from_norm).astype(jnp.bfloat16)
    qkv_shard, out_shard, in_shard, down_shard = (
        lax.psum_scatter(
            qkv_weight_grad.astype(jnp.bfloat16), "wa", scatter_dimension=0, tiled=True
        ).astype(jnp.float32),
        lax.psum_scatter(
            out_proj_grad.astype(jnp.bfloat16), "wa", scatter_dimension=0, tiled=True
        ).astype(jnp.float32),
        lax.psum_scatter(
            in_grad.astype(jnp.bfloat16), "wa", scatter_dimension=0, tiled=True
        ).astype(jnp.float32),
        lax.psum_scatter(
            down_grad.astype(jnp.bfloat16), "wa", scatter_dimension=0, tiled=True
        ).astype(jnp.float32),
    )
    qkv_shard, out_shard = (
        lax.psum(qkv_shard.astype(jnp.bfloat16), "ctx").astype(jnp.float32),
        lax.psum(out_shard.astype(jnp.bfloat16), "ctx").astype(jnp.float32),
    )
    stat_sums, count_sum, router_sum, gain_attn_sum, gain_moe_sum, bias_sum = lax.psum(
        (stat_terms, valid_count, router_grad, gain_attn_grad, gain_moe_grad, bias_total),
        ("ctx", "wa"),
    )
    stats = jnp.sqrt(stat_sums / (count_sum * model_width))
    return (
        final.astype(jnp.bfloat16)[None],
        hidden_grad[None],
        qkv_shard,
        out_shard,
        in_shard[None],
        down_shard[None],
        router_sum,
        gain_attn_sum,
        gain_moe_sum,
        bias_sum,
        stats,
    )


BLOCK = 256


def nt_dot(left, right):
    return lax.dot_general(
        left, right, (((1,), (1,)), ((), ())), preferred_element_type=jnp.float32
    )


def plain_dot(left, right):
    return jnp.dot(left, right, preferred_element_type=jnp.float32)


def block_at(index):
    return pl.ds(pl.multiple_of(index * BLOCK, BLOCK), BLOCK)


def segment_begin(positions, bounds):
    begin = positions * 0
    for index in range(NSEQ):
        begin = jnp.where(positions >= bounds[index], bounds[index], begin)
    return begin


def fill_bias_tiles(distance_rows, tiles):
    for level in range(tiles.shape[0]):
        spread = jnp.broadcast_to(distance_rows[level : level + 1, :], (BLOCK, 2 * BLOCK))
        tiles[level] = pltpu.roll(spread, BLOCK + 1, 1, stride=1, stride_axis=0)[:, :BLOCK]


def fill_sorter(perm, sorter):
    slots = perm.shape[1]

    def step(index, carry):
        wanted = lax.broadcasted_iota(jnp.int32, (BLOCK, slots), 0) + index * BLOCK
        sorter[block_at(index), :] = jnp.where(perm[...] == wanted, 1.0, 0.0).astype(jnp.bfloat16)
        return carry

    lax.fori_loop(0, slots // BLOCK, step, 0)


def pair_mask(key_block, query_pos, query_begin):
    key_pos = lax.broadcasted_iota(jnp.int32, (BLOCK, BLOCK), 0) + key_block * BLOCK
    return (key_pos <= query_pos) & (key_pos >= query_begin)


def attention_forward_kernel(
    piece_count, head_dim, source, bounds, weight, perm, distance_rows, *refs
):
    pieces = refs[:piece_count]
    mixed, sorted_out, rows_out, wide_out, log_out = refs[piece_count : piece_count + 5]
    raw, sorter, tiles, mixed_sorted = refs[piece_count + 5 :]
    slots = perm.shape[1]
    blocks = slots // BLOCK
    local_rows = pieces[0].shape[0]
    for index in range(piece_count):
        offset = pl.multiple_of(source[index] * local_rows, local_rows)
        raw[:, pl.ds(offset, local_rows)] = nt_dot(weight[...], pieces[index][...]).astype(
            jnp.bfloat16
        )
    fill_bias_tiles(distance_rows, tiles)
    fill_sorter(perm, sorter)

    def sort_step(index, carry):
        columns = nt_dot(raw[...], sorter[block_at(index), :])
        sorted_out[:, block_at(index)] = columns.astype(jnp.bfloat16)
        rows_out[block_at(index), :] = jnp.transpose(columns[head_dim:]).astype(jnp.bfloat16)
        return carry

    lax.fori_loop(0, blocks, sort_step, 0)
    mixed_sorted[...] = jnp.zeros_like(mixed_sorted)
    total = bounds[NSEQ - 1]

    def query_step(query_block, carry):
        queries = sorted_out[:head_dim, block_at(query_block)] * 0.125
        query_pos = lax.broadcasted_iota(jnp.int32, (1, BLOCK), 1) + query_block * BLOCK
        query_begin = segment_begin(query_pos, bounds)
        first = segment_begin(query_block * BLOCK, bounds) // BLOCK

        def key_step(key_block, state):
            row_max, totals, weighted = state
            scores = plain_dot(rows_out[block_at(key_block), :head_dim], queries)
            scores = jnp.where(
                pair_mask(key_block, query_pos, query_begin),
                scores + tiles[query_block - key_block],
                MASKED_SCORE,
            )
            new_max = jnp.maximum(row_max, jnp.max(scores, axis=0, keepdims=True))
            factor = jnp.exp(row_max - new_max)
            exp_scores = jnp.exp(scores - new_max)
            totals = totals * factor + jnp.sum(exp_scores, axis=0, keepdims=True)
            values = sorted_out[2 * head_dim :, block_at(key_block)]
            weighted = weighted * factor + plain_dot(values, exp_scores.astype(jnp.bfloat16))
            return (new_max, totals, weighted)

        row_max, totals, weighted = lax.fori_loop(
            first,
            query_block + 1,
            key_step,
            (
                jnp.full((1, BLOCK), MASKED_SCORE, jnp.float32),
                jnp.zeros((1, BLOCK), jnp.float32),
                jnp.zeros((head_dim, BLOCK), jnp.float32),
            ),
        )
        outcome = jnp.where(query_pos < total, weighted / totals, 0.0)
        wide_out[:, block_at(query_block)] = outcome
        log_out[:, block_at(query_block)] = row_max + jnp.log(totals)
        mixed_sorted[:, block_at(query_block)] = outcome.astype(jnp.bfloat16)
        return carry

    lax.fori_loop(0, (total + BLOCK - 1) // BLOCK, query_step, 0)
    for index in range(blocks):
        columns = plain_dot(mixed_sorted[...], sorter[:, index * BLOCK : (index + 1) * BLOCK])
        columns = columns.astype(jnp.bfloat16)
        for part in range(BLOCK // local_rows):
            mixed[index * (BLOCK // local_rows) + part] = columns[
                :, part * local_rows : (part + 1) * local_rows
            ]


def attention_backward_kernel(
    piece_count,
    head_dim,
    source,
    plane,
    bounds,
    received,
    perm,
    distance_rows,
    sorted_in,
    rows_in,
    wide_in,
    log_in,
    weight,
    *refs,
):
    pieces = refs[:piece_count]
    sent, own_out, other_out, gain_out, distance_out = refs[piece_count : piece_count + 5]
    dout_raw, dout_sorted, sorter, tiles, tile_grads, grad_acc, grad_sorted, grad_out = refs[
        piece_count + 5 :
    ]
    slots = perm.shape[1]
    blocks = slots // BLOCK
    groups, _, local_rows = received.shape
    for index in range(groups):
        dout_raw[:, index * local_rows : (index + 1) * local_rows] = received[index]
    fill_bias_tiles(distance_rows, tiles)
    fill_sorter(perm, sorter)

    def sort_step(index, carry):
        columns = nt_dot(dout_raw[...], sorter[block_at(index), :])
        dout_sorted[:, block_at(index)] = columns.astype(jnp.bfloat16)
        return carry

    lax.fori_loop(0, blocks, sort_step, 0)
    tile_grads[...] = jnp.zeros_like(tile_grads)
    grad_acc[...] = jnp.zeros_like(grad_acc)
    total = bounds[NSEQ - 1]

    def query_step(query_block, carry):
        queries = sorted_in[:head_dim, block_at(query_block)] * 0.125
        douts = dout_sorted[:, block_at(query_block)]
        row_delta = jnp.sum(
            douts.astype(jnp.float32) * wide_in[:, block_at(query_block)], axis=0, keepdims=True
        )
        log_total = log_in[:, block_at(query_block)]
        query_pos = lax.broadcasted_iota(jnp.int32, (1, BLOCK), 1) + query_block * BLOCK
        query_begin = segment_begin(query_pos, bounds)
        inside = query_pos < total
        first = segment_begin(query_block * BLOCK, bounds) // BLOCK

        def key_step(key_block, query_grad):
            rows = rows_in[block_at(key_block), :]
            scores = plain_dot(rows[:, :head_dim], queries) + tiles[query_block - key_block]
            probs = jnp.exp(
                jnp.where(
                    pair_mask(key_block, query_pos, query_begin) & inside,
                    scores - log_total,
                    MASKED_SCORE,
                )
            )
            prob_grad = plain_dot(rows[:, head_dim:], douts)
            score_grad = (probs * (prob_grad - row_delta)).astype(jnp.bfloat16)
            tile_grads[query_block - key_block] += score_grad.astype(jnp.float32)
            grad_acc[head_dim : 2 * head_dim, block_at(key_block)] += nt_dot(queries, score_grad)
            grad_acc[2 * head_dim :, block_at(key_block)] += nt_dot(
                douts, probs.astype(jnp.bfloat16)
            )
            keys = sorted_in[head_dim : 2 * head_dim, block_at(key_block)]
            return query_grad + plain_dot(keys, score_grad)

        query_grad = lax.fori_loop(
            first, query_block + 1, key_step, jnp.zeros((head_dim, BLOCK), jnp.float32)
        )
        grad_acc[:head_dim, block_at(query_block)] = query_grad * 0.125
        return carry

    lax.fori_loop(0, (total + BLOCK - 1) // BLOCK, query_step, 0)
    grad_sorted[...] = grad_acc[...].astype(jnp.bfloat16)
    for index in range(blocks):
        columns = plain_dot(grad_sorted[...], sorter[:, index * BLOCK : (index + 1) * BLOCK])
        columns = columns.astype(jnp.bfloat16)
        grad_out[:, index * BLOCK : (index + 1) * BLOCK] = columns
        for part in range(BLOCK // local_rows):
            sent[index * (BLOCK // local_rows) + part] = columns[
                :, part * local_rows : (part + 1) * local_rows
            ]
    piece_rows = pieces[0].shape[0]
    head_total = jnp.zeros(weight.shape, jnp.float32)
    for index in range(piece_count):
        offset = pl.multiple_of(source[index] * piece_rows, piece_rows)
        head_total = head_total + plain_dot(
            grad_out[:, pl.ds(offset, piece_rows)], pieces[index][...]
        )
    gain_out[...] = jnp.sum(weight[...].astype(jnp.float32) * head_total, axis=0, keepdims=True)
    half = weight.shape[1] // 2

    @pl.when(plane[0] == 0)
    def _():
        own_out[...] = head_total[:, :half]
        other_out[...] = head_total[:, half:].astype(jnp.bfloat16)

    @pl.when(plane[0] != 0)
    def _():
        own_out[...] = head_total[:, half:]
        other_out[...] = head_total[:, :half].astype(jnp.bfloat16)

    row_ids = lax.broadcasted_iota(jnp.int32, (BLOCK, BLOCK), 0)
    column_ids = lax.broadcasted_iota(jnp.int32, (BLOCK, BLOCK), 1)
    mirror = jnp.where(row_ids + column_ids == BLOCK - 1, 1.0, 0.0)
    for level in range(tiles.shape[0]):
        turned = jnp.dot(
            mirror, tile_grads[level], precision=TOP_PRECISION, preferred_element_type=jnp.float32
        )
        wide = jnp.concatenate([turned, jnp.zeros((BLOCK, BLOCK), jnp.float32)], axis=1)
        turned = pltpu.roll(wide, 0, 1, stride=1, stride_axis=0)
        distance_out[level : level + 1, :] = jnp.sum(turned, axis=0, keepdims=True)


def assemble_kernel(piece_count, head_dim, source, *refs):
    pieces = refs[:piece_count]
    out = refs[piece_count]
    width = out.shape[1] // 3
    chips = piece_count // 2
    on_first = source[0] % 2 == 0
    for index in range(chips):
        mine, theirs = pieces[index][...], pieces[index + chips][...]
        first = jnp.where(on_first, mine, theirs).astype(jnp.float32)
        second = jnp.where(on_first, theirs, mine).astype(jnp.float32)
        chip = source[index] // 2
        for part in range(3):
            span = slice(part * head_dim, (part + 1) * head_dim)
            columns = jnp.concatenate([first[span], second[span]], axis=0)
            offset = pl.multiple_of(part * width + chip * 2 * head_dim, 2 * head_dim)
            out[:, pl.ds(offset, 2 * head_dim)] = jnp.transpose(columns)


def assemble_weight_gradient(source, pieces, head_dim):
    rows, width = pieces[0].shape[1], pieces[0].shape[0] * len(pieces)
    return pl.pallas_call(
        functools.partial(assemble_kernel, len(pieces), head_dim),
        out_shape=shaped((rows, width), jnp.float32),
        in_specs=[smem()] + [vmem()] * len(pieces),
        out_specs=vmem(),
        cost_estimate=pl.CostEstimate(
            flops=rows * width, bytes_accessed=6 * rows * width, transcendentals=0
        ),
    )(source, *pieces)


LANES = 128


GELU_SCALE = math.sqrt(2.0 / math.pi)


def tile_at(index, begin=0, size=LANES):
    return pl.ds(pl.multiple_of(begin + index * size, LANES), size)


def hbm():
    return pl.BlockSpec(memory_space=pl.ANY)


def expert_forward_kernel(
    units,
    mine,
    theirs,
    weights,
    part_mine,
    part_theirs,
    hidden_out,
    slope_out,
    act_out,
    in_weight,
    down_weight,
    hidden,
    gate_slope,
    act,
    even,
    odd,
    in_sem,
    down_sem,
    out_sem,
):
    count, width = mine.shape[0], in_weight.shape[0]
    tiles = units // LANES

    def fetch(tile, side):
        lanes = tile_at(tile, side * units)
        return pltpu.make_async_copy(
            weights.at[:, lanes], in_weight.at[:, lanes], in_sem.at[tile, side]
        )

    down_copy = pltpu.make_async_copy(weights.at[:, 2 * units :], down_weight, down_sem)
    for tile in range(tiles):
        for side in range(2):
            fetch(tile, side).start()
    down_copy.start()

    def multiply(tile, target):
        for side in range(2):
            fetch(tile, side).wait()
        weight = jnp.concatenate(
            [in_weight[:, tile_at(tile)], in_weight[:, tile_at(tile, units)]], axis=1
        )
        target[:count] = plain_dot(mine[:, :width], weight)
        target[count:] = plain_dot(theirs[:, :width], weight)

    def activate(tile, held):
        gate, up = held[:, :LANES], held[:, LANES:]
        square = gate * gate
        bent = jnp.tanh(gate * (GELU_SCALE + (0.044715 * GELU_SCALE) * square))
        share = 0.5 + 0.5 * bent
        slope = share + (0.5 - 0.5 * bent * bent) * (
            gate * (GELU_SCALE + (3.0 * 0.044715 * GELU_SCALE) * square)
        )
        active = gate * share
        hidden[:, tile_at(tile)] = (active * up).astype(jnp.bfloat16)
        gate_slope[:, tile_at(tile)] = (up * slope).astype(jnp.bfloat16)
        act[:, tile_at(tile)] = active.astype(jnp.bfloat16)

    multiply(0, even)

    def step(pair, carry):
        multiply(2 * pair + 1, odd)
        activate(2 * pair, even)
        multiply(2 * pair + 2, even)
        activate(2 * pair + 1, odd)
        return carry

    lax.fori_loop(0, (tiles - 1) // 2, step, 0)
    if tiles % 2 == 0:
        multiply(tiles - 1, odd)
        activate(tiles - 2, even)
        activate(tiles - 1, odd)
    else:
        activate(tiles - 1, even)
    copies = [
        pltpu.make_async_copy(held, out, out_sem.at[index])
        for index, (held, out) in enumerate(
            ((hidden, hidden_out), (gate_slope, slope_out), (act, act_out))
        )
    ]
    for copy in copies:
        copy.start()
    down_copy.wait()

    def down_step(tile, carry):
        weight = down_weight[block_at(tile), :]
        part_theirs[:, block_at(tile)] = nt_dot(hidden[count:], weight).astype(jnp.bfloat16)
        part_mine[:, block_at(tile)] = nt_dot(hidden[:count], weight)
        return carry

    lax.fori_loop(0, width // BLOCK, down_step, 0)
    for copy in copies:
        copy.wait()


def expert_forward(mine, theirs, weights, units):
    count, wide = mine.shape
    width = weights.shape[0]
    tall = (2 * count, units)
    return pl.pallas_call(
        functools.partial(expert_forward_kernel, units),
        out_shape=(
            shaped((count, width), jnp.float32),
            shaped((count, width), jnp.bfloat16),
        )
        + (shaped(tall, jnp.bfloat16),) * 3,
        in_specs=[vmem(), vmem(), hbm()],
        out_specs=(vmem(), vmem(), hbm(), hbm(), hbm()),
        scratch_shapes=[
            pltpu.VMEM((width, 2 * units), jnp.bfloat16),
            pltpu.VMEM((width, units), jnp.bfloat16),
            pltpu.VMEM(tall, jnp.bfloat16),
            pltpu.VMEM(tall, jnp.bfloat16),
            pltpu.VMEM(tall, jnp.bfloat16),
            pltpu.VMEM((2 * count, 2 * LANES), jnp.float32),
            pltpu.VMEM((2 * count, 2 * LANES), jnp.float32),
            pltpu.SemaphoreType.DMA((units // LANES, 2)),
            pltpu.SemaphoreType.DMA,
            pltpu.SemaphoreType.DMA((3,)),
        ],
        cost_estimate=pl.CostEstimate(
            flops=12 * count * width * units, bytes_accessed=1 << 20, transcendentals=0
        ),
    )(mine, theirs, weights)


def expert_backward_kernel(
    units,
    mine_left,
    mine_right,
    theirs_left,
    theirs_right,
    mine_rows,
    theirs_rows,
    slope_in,
    act_in,
    weights,
    back_mine,
    back_theirs,
    grads_out,
    scaled,
    in_weight,
    down_weight,
    gate_slope,
    act,
    unit_grads,
    tile_sem,
    in_sem,
    out_sem,
):
    count, half = mine_left.shape
    width = 2 * half
    spans = [(begin, min(BLOCK, units - begin)) for begin in range(0, units, BLOCK)]
    blocks = width // BLOCK
    tile_copies = []
    for index, (begin, size) in enumerate(spans):
        lanes = slice(begin, begin + size)
        far = slice(2 * units + begin, 2 * units + begin + size)
        tile_copies.append(
            (
                pltpu.make_async_copy(
                    weights.at[:, far], down_weight.at[:, lanes], tile_sem.at[index, 0]
                ),
                pltpu.make_async_copy(
                    slope_in.at[:, lanes], gate_slope.at[:, lanes], tile_sem.at[index, 1]
                ),
                pltpu.make_async_copy(act_in.at[:, lanes], act.at[:, lanes], tile_sem.at[index, 2]),
            )
        )
    in_copies = [
        pltpu.make_async_copy(
            weights.at[index * BLOCK : (index + 1) * BLOCK, : 2 * units],
            in_weight.at[index * BLOCK : (index + 1) * BLOCK, :],
            in_sem.at[index],
        )
        for index in range(blocks)
    ]
    for copies in tile_copies:
        for copy in copies:
            copy.start()
    for copy in in_copies:
        copy.start()
    for index, pair in enumerate(
        ((mine_left, mine_right, mine_rows), (theirs_left, theirs_right, theirs_rows))
    ):
        span = slice(index * count, (index + 1) * count)
        gate = jnp.sum(pair[2][:, width:].astype(jnp.float32), axis=1, keepdims=True)
        for side in range(2):
            scaled[span, side * half : (side + 1) * half] = (
                gate * pair[side][...].astype(jnp.float32)
            ).astype(jnp.bfloat16)
    for copies, (begin, size) in zip(tile_copies, spans):
        for copy in copies:
            copy.wait()
        lanes = slice(begin, begin + size)
        for index in range(2):
            span = slice(index * count, (index + 1) * count)
            hidden_grad = plain_dot(scaled[span], down_weight[:, lanes])
            unit_grads[span, lanes] = (
                hidden_grad * gate_slope[span, lanes].astype(jnp.float32)
            ).astype(jnp.bfloat16)
            unit_grads[span, units + begin : units + begin + size] = (
                hidden_grad * act[span, lanes].astype(jnp.float32)
            ).astype(jnp.bfloat16)
    out_copy = pltpu.make_async_copy(unit_grads, grads_out, out_sem)
    out_copy.start()
    for index in range(blocks):
        in_copies[index].wait()

    def step(tile, carry):
        weight = in_weight[block_at(tile), :]
        back_theirs[:, block_at(tile)] = nt_dot(unit_grads[count:], weight).astype(jnp.bfloat16)
        back_mine[:, block_at(tile)] = nt_dot(unit_grads[:count], weight)
        return carry

    lax.fori_loop(0, blocks, step, 0)
    out_copy.wait()


def expert_backward(parts, rows, gate_slope, act, weights):
    count, half = parts[0].shape
    units = act.shape[1]
    width = 2 * half
    return pl.pallas_call(
        functools.partial(expert_backward_kernel, units),
        out_shape=(
            shaped((count, width), jnp.float32),
            shaped((count, width), jnp.bfloat16),
            shaped((2 * count, 2 * units), jnp.bfloat16),
            shaped((2 * count, width), jnp.bfloat16),
        ),
        in_specs=[vmem()] * 6 + [hbm()] * 3,
        out_specs=(vmem(), vmem(), hbm(), vmem()),
        scratch_shapes=[
            pltpu.VMEM((width, 2 * units), jnp.bfloat16),
            pltpu.VMEM((width, units), jnp.bfloat16),
            pltpu.VMEM((2 * count, units), jnp.bfloat16),
            pltpu.VMEM((2 * count, units), jnp.bfloat16),
            pltpu.VMEM((2 * count, 2 * units), jnp.bfloat16),
            pltpu.SemaphoreType.DMA((-(-units // BLOCK), 3)),
            pltpu.SemaphoreType.DMA((width // BLOCK,)),
            pltpu.SemaphoreType.DMA,
        ],
        cost_estimate=pl.CostEstimate(
            flops=12 * count * width * units, bytes_accessed=1 << 20, transcendentals=0
        ),
    )(*parts, *rows, gate_slope, act, weights)


def turned_product_kernel(*refs):
    parts, right, out, turned = refs[:-3], refs[-3], refs[-2], refs[-1]
    width = turned.shape[0]
    at = 0
    for part in parts:
        count = part.shape[0]
        turned[:, at : at + count] = jnp.transpose(part[:, :width])
        at += count

    def step(tile, carry):
        out[:, block_at(tile)] = plain_dot(turned[...], right[:, block_at(tile)]).astype(
            jnp.bfloat16
        )
        return carry

    columns = out.shape[1]
    lax.fori_loop(0, columns // BLOCK, step, 0)
    if columns % BLOCK:
        rest = slice(columns - columns % BLOCK, columns)
        out[:, rest] = plain_dot(turned[...], right[:, rest]).astype(jnp.bfloat16)


def turned_product(parts, right, width):
    rows, columns = right.shape
    return pl.pallas_call(
        turned_product_kernel,
        out_shape=shaped((width, columns), jnp.bfloat16),
        in_specs=[vmem()] * (len(parts) + 1),
        out_specs=vmem(),
        scratch_shapes=[pltpu.VMEM((width, rows), jnp.bfloat16)],
        compiler_params=pltpu.CompilerParams(vmem_limit_bytes=EXPERT_VMEM),
        cost_estimate=pl.CostEstimate(
            flops=rows * width * columns // 4, bytes_accessed=1 << 20, transcendentals=0
        ),
    )(*parts, right)


def close_moe_kernel(
    plane,
    back,
    pick,
    base,
    resid,
    gain,
    out_grad,
    out_own,
    out_other,
    resid_grad,
    attn_grad,
    gain_grad,
    mix_grad,
):
    norm_grad = base[...] + plain_dot(pick[...], back[...])
    features = resid[...]
    scale = lax.rsqrt(jnp.mean(features * features, axis=1, keepdims=True) + NORM_EPSILON)
    shape = features * scale
    gain_grad[...] = jnp.sum(norm_grad * shape, axis=0, keepdims=True)
    inner = norm_grad * gain[...]
    total = scale * (inner - shape * jnp.mean(inner * shape, axis=1, keepdims=True))
    total = total + out_grad[...].astype(jnp.float32)
    resid_grad[...] = total
    low = total.astype(jnp.bfloat16)
    attn_grad[...] = low
    half = out_own.shape[0]
    own_at = pl.multiple_of(plane[0] * half, half)
    mix_grad[pl.ds(own_at, half), :] = nt_dot(out_own[...], low).astype(jnp.bfloat16)
    other_at = pl.multiple_of((1 - plane[0]) * half, half)
    mix_grad[pl.ds(other_at, half), :] = nt_dot(out_other[...], low).astype(jnp.bfloat16)


def close_moe(plane, back, pick, base, resid, gain, out_grad, out_own, out_other):
    rows, width = resid.shape
    return pl.pallas_call(
        close_moe_kernel,
        out_shape=(
            shaped((rows, width), jnp.float32),
            shaped((rows, width), jnp.bfloat16),
            shaped((1, width), jnp.float32),
            shaped((width, rows), jnp.bfloat16),
        ),
        in_specs=[smem()] + [vmem()] * 8,
        out_specs=(vmem(),) * 4,
        compiler_params=pltpu.CompilerParams(vmem_limit_bytes=EXPERT_VMEM),
        cost_estimate=pl.CostEstimate(
            flops=8 * rows * width * width, bytes_accessed=1 << 20, transcendentals=0
        ),
    )(plane, back, pick, base, resid, gain, out_grad, out_own, out_other)


EXPERT_VMEM = 36 << 20


def vmem():
    return pl.BlockSpec(memory_space=pltpu.VMEM)


def smem():
    return pl.BlockSpec(memory_space=pltpu.SMEM)


def shaped(shape, dtype):
    return jax.ShapeDtypeStruct(shape, dtype)


def attention_forward(source, bounds, weight, perm, distance_rows, pieces, head_dim):
    groups = len(pieces)
    slots = perm.shape[1]
    local_rows = pieces[0].shape[0]
    levels = distance_rows.shape[0]
    flops = 2 * slots * (3 * head_dim * pieces[0].shape[1] + 4 * head_dim * slots + head_dim * slots)
    return pl.pallas_call(
        functools.partial(attention_forward_kernel, groups, head_dim),
        out_shape=(
            shaped((groups, head_dim, local_rows), jnp.bfloat16),
            shaped((3 * head_dim, slots), jnp.bfloat16),
            shaped((slots, 2 * head_dim), jnp.bfloat16),
            shaped((head_dim, slots), jnp.float32),
            shaped((1, slots), jnp.float32),
        ),
        in_specs=[smem(), smem()] + [vmem()] * (3 + groups),
        out_specs=(vmem(),) * 5,
        scratch_shapes=[
            pltpu.VMEM((3 * head_dim, slots), jnp.bfloat16),
            pltpu.VMEM((slots, slots), jnp.bfloat16),
            pltpu.VMEM((levels, BLOCK, BLOCK), jnp.float32),
            pltpu.VMEM((head_dim, slots), jnp.bfloat16),
        ],
        cost_estimate=pl.CostEstimate(
            flops=flops, bytes_accessed=8 << 20, transcendentals=slots * slots // 4
        ),
    )(source, bounds, weight, perm, distance_rows, *pieces)


def attention_backward(
    source, plane, bounds, received, perm, distance_rows, saved, weight, pieces, head_dim
):
    slots = perm.shape[1]
    groups, _, local_rows = received.shape
    levels = distance_rows.shape[0]
    width = weight.shape[1]
    return pl.pallas_call(
        functools.partial(attention_backward_kernel, len(pieces), head_dim),
        out_shape=(
            shaped((groups, 3 * head_dim, local_rows), jnp.bfloat16),
            shaped((3 * head_dim, width // 2), jnp.float32),
            shaped((3 * head_dim, width // 2), jnp.bfloat16),
            shaped((1, width), jnp.float32),
            shaped((levels, 2 * BLOCK), jnp.float32),
        ),
        in_specs=[smem()] * 3 + [vmem()] * (8 + len(pieces)),
        out_specs=(vmem(),) * 5,
        scratch_shapes=[
            pltpu.VMEM((head_dim, slots), jnp.bfloat16),
            pltpu.VMEM((head_dim, slots), jnp.bfloat16),
            pltpu.VMEM((slots, slots), jnp.bfloat16),
            pltpu.VMEM((levels, BLOCK, BLOCK), jnp.float32),
            pltpu.VMEM((levels, BLOCK, BLOCK), jnp.float32),
            pltpu.VMEM((3 * head_dim, slots), jnp.float32),
            pltpu.VMEM((3 * head_dim, slots), jnp.bfloat16),
            pltpu.VMEM((3 * head_dim, slots), jnp.bfloat16),
        ],
        cost_estimate=pl.CostEstimate(
            flops=2 * slots * slots * 6 * head_dim,
            bytes_accessed=4 << 20,
            transcendentals=slots * slots // 4,
        ),
    )(source, plane, bounds, received, perm, distance_rows, *saved, weight, *pieces)


class Ring:
    def __init__(self, groups):
        self.chips = groups // 2
        order = list(range(0, self.chips, 2)) + list(range(1, self.chips, 2))[::-1]
        self.order = order
        self.forward = self.shift(1)
        self.backward = self.shift(-1)
        self.swap = [(index, index ^ 1) for index in range(groups)]
        self.same_core = [[2 * chip + core for chip in range(self.chips)] for core in range(2)]
        table = np.zeros((groups, groups), np.int32)
        for at, chip in enumerate(order):
            for core in range(2):
                steps = self.offsets()
                near = [2 * order[(at + step) % self.chips] + core for step in steps]
                table[2 * chip + core] = near + [index ^ 1 for index in near]
        self.table = table

    def offsets(self):
        steps = [0]
        for step in range(1, (self.chips + 1) // 2):
            steps += [-step, step]
        return steps + ([self.chips // 2] if self.chips % 2 == 0 else [])

    def shift(self, step):
        return [
            (2 * self.order[at] + core, 2 * self.order[(at + step) % self.chips] + core)
            for at in range(self.chips)
            for core in range(2)
        ]

    def swapped(self, piece):
        return lax.ppermute(piece, "ctx", self.swap)

    def gather(self, piece, beside=lambda piece: piece):
        pieces = [piece]
        ahead = behind = piece
        for _ in range(1, (self.chips + 1) // 2):
            ahead = beside(ahead)
            behind = lax.ppermute(behind, "ctx", self.backward)
            ahead = lax.ppermute(ahead, "ctx", self.forward)
            pieces += [ahead, behind]
        if self.chips % 2 == 0:
            half = piece.shape[0] // 2
            ahead = beside(ahead)
            pieces.append(
                jnp.concatenate(
                    [
                        lax.ppermute(ahead[:half], "ctx", self.forward),
                        lax.ppermute(behind[half:], "ctx", self.backward),
                    ],
                    axis=0,
                )
            )
        return pieces + [self.swapped(item) for item in pieces]


def across(values):
    return lax.ppermute(values, "wa", [(0, 1), (1, 0)])


def scatter_half(values, ctx, groups, stride):
    half = values.shape[1] // 2
    upper = (ctx // stride) % 2 == 1
    low, high = values[:, :half], values[:, half:]
    taken = lax.ppermute(
        jnp.where(upper, low, high).astype(jnp.bfloat16),
        "ctx",
        [(index, index ^ stride) for index in range(groups)],
    )
    return jnp.where(upper, high, low) + taken.astype(jnp.float32)


def gather_half(values, ctx, groups, stride):
    upper = (ctx // stride) % 2 == 1
    taken = lax.ppermute(values, "ctx", [(index, index ^ stride) for index in range(groups)])
    return jnp.where(
        upper,
        jnp.concatenate([taken, values], axis=0),
        jnp.concatenate([values, taken], axis=0),
    )


def sum_step(values, groups, stride):
    if stride >= groups:
        return values + across(values)
    return values + lax.ppermute(values, "ctx", [(index, index ^ stride) for index in range(groups)])


def flat_pack(parts, rows):
    flat = jnp.concatenate([part.reshape(-1) for part in parts])
    return jnp.pad(flat, (0, rows * 128 - flat.shape[0])).reshape(rows, 128)


def fast_device(
    hidden_in,
    out_grad,
    lengths,
    permutation,
    routes,
    bucket_table,
    w_qkv,
    w_out,
    w_in,
    w_down,
    w_router,
    gain_attn,
    gain_moe,
    rel_bias,
):
    stream = hidden_in[0].astype(jnp.float32)
    local_rows, width = stream.shape
    bucket_count, head_count = rel_bias.shape
    head_dim = width // head_count
    experts = w_router.shape[1]
    slot_cap = 4 * local_rows // experts
    groups = lax.axis_size("ctx")
    half_width = width // 2
    ring = Ring(groups)
    ctx = lax.axis_index("ctx")
    core = ctx % 2
    on_low = lax.axis_index("wa") == 0
    plane = lax.axis_index("wa").reshape(1)
    perm_row = permutation[0]
    slots = perm_row.shape[0]
    bounds = jnp.cumsum(lengths[0])
    own_start = ctx * local_rows
    query_pos = lax.dynamic_slice_in_dim(perm_row, own_start, local_rows, 0)
    is_valid = (segment_of(query_pos, bounds) < NSEQ).astype(jnp.float32)
    source = lax.dynamic_index_in_dim(jnp.asarray(ring.table), ctx, 0, keepdims=False)

    def in_order(own, other, axis):
        return jnp.where(
            on_low,
            jnp.concatenate([own, other], axis=axis),
            jnp.concatenate([other, own], axis=axis),
        )

    def fetch_part(weight):
        half = weight.shape[0] // 2
        return across(lax.dynamic_slice_in_dim(weight, core * half, half, 0))

    def join_parts(mine):
        theirs = ring.swapped(mine)
        return jnp.where(
            core == 0,
            jnp.concatenate([mine, theirs], axis=0),
            jnp.concatenate([theirs, mine], axis=0),
        )

    head_weight = jnp.concatenate(
        [
            lax.dynamic_slice_in_dim(w_qkv, block * width + ctx * head_dim, head_dim, 1)
            for block in range(3)
        ],
        axis=1,
    ).T
    head_weight = in_order(head_weight, across(head_weight), 1)
    units = w_down.shape[2]
    out_own = w_out
    out_mine = fetch_part(w_out)
    expert_weights = lax.all_gather(
        jnp.concatenate([w_in[0], w_down[0]], axis=1), "wa", axis=0, tiled=True
    )

    head_hot = (jnp.arange(head_count, dtype=jnp.int32) == ctx).astype(jnp.float32)
    head_bias = jnp.sum(rel_bias * head_hot[None, :], axis=1)
    reach = bucket_table.shape[0]
    bucket_hot = bucket_table[:, None] == jnp.arange(bucket_count, dtype=jnp.int32)[None, :]
    by_distance = jnp.sum(jnp.where(bucket_hot, head_bias[None, :], 0.0), axis=1)
    levels = reach // BLOCK + 1
    padded = jnp.pad(by_distance, (BLOCK - 1, levels * BLOCK + BLOCK - reach + 1))
    distance_rows = jnp.stack(
        [padded[level * BLOCK : level * BLOCK + 2 * BLOCK] for level in range(levels)]
    )

    normed_attn_low = rms_norm(stream, gain_attn).astype(jnp.bfloat16)
    perm_lanes = perm_row[None, :]
    turns = 0

    def prepare(piece):
        nonlocal turns, head_weight, distance_rows, source, bounds, perm_lanes, out_mine
        turns += 1
        if turns == 3:
            piece, head_weight, distance_rows, source, bounds, perm_lanes, out_mine = (
                lax.optimization_barrier(
                    (piece, head_weight, distance_rows, source, bounds, perm_lanes, out_mine)
                )
            )
        return piece

    pieces = ring.gather(normed_attn_low, prepare)
    out_other = join_parts(out_mine)

    route_rows = routes[0]
    expert_ids = jnp.arange(experts, dtype=jnp.int32)
    first_hot = route_rows[:, 0:1] == expert_ids[None, :]
    second_hot = route_rows[:, 1:2] == expert_ids[None, :]
    counts = jnp.cumsum((first_hot | second_hot).astype(jnp.int32), axis=0)
    first_slot = jnp.sum(jnp.where(first_hot, counts - 1, 0), axis=1)
    second_slot = jnp.sum(jnp.where(second_hot, counts - 1, 0), axis=1)
    first_lane = route_rows[:, 0] * slot_cap + first_slot
    second_lane = route_rows[:, 1] * slot_cap + second_slot
    lane_ids = jnp.arange(experts * slot_cap, dtype=jnp.int32)
    first_at = first_lane[:, None] == lane_ids[None, :]
    second_at = second_lane[:, None] == lane_ids[None, :]
    first_pick = first_at.astype(jnp.bfloat16)
    second_pick = second_at.astype(jnp.bfloat16)
    any_pick = (first_at | second_at).astype(jnp.bfloat16)

    def exchange(values):
        return lax.all_to_all(
            values,
            "ctx",
            split_axis=0,
            concat_axis=0,
            tiled=True,
            axis_index_groups=ring.same_core,
        )

    out_grad_slots = lead_dot(any_pick, out_grad[0]).astype(jnp.bfloat16)

    out_grad_slots, _ = lax.optimization_barrier((out_grad_slots, pieces[-1]))
    grads_left = exchange(out_grad_slots[:, :half_width])
    mixed, *saved = attention_forward(
        source, bounds, head_weight, perm_lanes, distance_rows, pieces, head_dim
    )
    mixed, grads_left = lax.optimization_barrier((mixed, grads_left))
    mixed = lax.all_to_all(mixed, "ctx", split_axis=0, concat_axis=0, tiled=True)
    mixed = mixed.reshape(width, local_rows)
    mixed_low, mixed_high = mixed[:half_width], mixed[half_width:]
    mixed_own = jnp.where(on_low, mixed_low, mixed_high)
    mixed_other = jnp.where(on_low, mixed_high, mixed_low)
    attn_out = lead_dot(mixed_own, out_own) + lead_dot(mixed_other, out_other)
    resid = stream + attn_out
    normed_moe_low = rms_norm(resid, gain_moe).astype(jnp.bfloat16)
    normed_moe_wide = normed_moe_low.astype(jnp.float32)
    logits = jnp.dot(normed_moe_wide, w_router, precision=TOP_PRECISION)
    chosen = jnp.stack(
        [
            jnp.sum(jnp.where(first_hot, logits, 0.0), axis=1),
            jnp.sum(jnp.where(second_hot, logits, 0.0), axis=1),
        ],
        axis=1,
    )
    gate_probs = jax.nn.softmax(chosen, axis=1)
    grad_final = out_grad[0].astype(jnp.float32)
    slot_gate = jnp.sum(
        jnp.where(first_at, gate_probs[:, 0:1], 0.0)
        + jnp.where(second_at, gate_probs[:, 1:2], 0.0),
        axis=0,
    )
    gate_parts = []
    for _ in range(3):
        gate_parts.append(lax.reduce_precision(slot_gate, 8, 7))
        slot_gate = slot_gate - gate_parts[-1]
    gate_parts = jnp.pad(jnp.stack(gate_parts, axis=1), ((0, 0), (0, LANES - 3)))
    rows_mine = exchange(
        jnp.concatenate(
            [
                lead_dot(any_pick, normed_moe_low).astype(jnp.bfloat16),
                gate_parts.astype(jnp.bfloat16),
            ],
            axis=1,
        )
    )
    rows_theirs = ring.swapped(rows_mine)
    out_grad_slots, rows_mine = lax.optimization_barrier((out_grad_slots, rows_mine))
    grads_right = exchange(out_grad_slots[:, half_width:])
    later_qkv, rows_mine = lax.optimization_barrier((w_qkv, rows_mine))
    qkv_mine = fetch_part(later_qkv)
    def chip_total(mine, theirs):
        return (mine + ring.swapped(theirs).astype(jnp.float32)).astype(jnp.bfloat16)

    part_mine, part_theirs, hidden, gate_slope, act = expert_forward(
        rows_mine, rows_theirs, expert_weights, units
    )
    part_theirs, grads_right = lax.optimization_barrier((part_theirs, grads_right))
    partial_total = chip_total(part_mine, part_theirs)
    partial_total, gate_slope = lax.optimization_barrier((partial_total, gate_slope))
    returned = exchange(partial_total)
    back_mine, back_theirs, unit_grads, scaled = expert_backward(
        (grads_left, grads_right, ring.swapped(grads_left), ring.swapped(grads_right)),
        (rows_mine, rows_theirs),
        gate_slope,
        act,
        expert_weights,
    )
    back_total = chip_total(back_mine, back_theirs)
    back_total, unit_grads, scaled, qkv_mine, returned = lax.optimization_barrier(
        (back_total, unit_grads, scaled, qkv_mine, returned)
    )
    qkv_other = join_parts(qkv_mine)
    rows_back = exchange(back_total)

    def plane_sum(values):
        return lax.psum_scatter(
            values, "wa", scatter_dimension=0, tiled=True
        ).astype(jnp.float32)

    down_grads = turned_product((scaled,), hidden, width)
    rows_mine, down_grads = lax.optimization_barrier((rows_mine, down_grads))
    in_grads = turned_product((rows_mine, rows_theirs), unit_grads, width)
    rows_back, in_grads = lax.optimization_barrier((rows_back, in_grads))
    down_shard = plane_sum(down_grads)
    in_shard = plane_sum(in_grads)

    picked_first = plain_dot(first_pick, returned)
    picked_second = plain_dot(second_pick, returned)
    moe_out = gate_probs[:, 0:1] * picked_first + gate_probs[:, 1:2] * picked_second
    final = resid + moe_out

    valid_col = is_valid[:, None]
    stat_terms = jnp.stack(
        [
            jnp.sum(valid_col * final * final),
            jnp.sum(valid_col * attn_out * attn_out),
            jnp.sum(valid_col * moe_out * moe_out),
            jnp.sum(is_valid),
        ]
    )
    gate_grad = jnp.stack(
        [jnp.sum(grad_final * picked_first, axis=1), jnp.sum(grad_final * picked_second, axis=1)],
        axis=1,
    )
    _, gate_back = jax.vjp(lambda chosen_in: jax.nn.softmax(chosen_in, axis=1), chosen)
    (chosen_grad,) = gate_back(gate_grad)
    logit_grad = jnp.where(first_hot, chosen_grad[:, 0:1], 0.0) + jnp.where(
        second_hot, chosen_grad[:, 1:2], 0.0
    )
    router_grad = lead_dot(normed_moe_wide, logit_grad, TOP_PRECISION)
    norm_moe_grad = jnp.dot(logit_grad, w_router.T, precision=TOP_PRECISION)
    resid_grad, attn_grad_low, gain_moe_grad, mix_grad = close_moe(
        plane,
        rows_back,
        any_pick,
        norm_moe_grad,
        resid,
        gain_moe[None, :],
        out_grad[0],
        out_own,
        out_other,
    )
    dout = lax.all_to_all(
        mix_grad.reshape(groups, head_dim, local_rows),
        "ctx",
        split_axis=0,
        concat_axis=0,
        tiled=True,
    )
    quarter = half_width // 2
    both_mixed = jnp.stack([mixed_own, mixed_other])

    def core_rows(index):
        return lax.dynamic_slice_in_dim(both_mixed, index * quarter, quarter, 1).reshape(
            2 * quarter, local_rows
        )

    taken = ring.swapped(plain_dot(core_rows(1 - core), attn_grad_low).astype(jnp.bfloat16))
    out_part = plain_dot(core_rows(core), attn_grad_low) + taken.astype(jnp.float32)
    out_part = out_part.reshape(2, quarter, width)
    stride = 2
    out_part = scatter_half(out_part, ctx, groups, stride)

    sent, head_own, head_given, gain_sums, distance_grads = attention_backward(
        source,
        plane,
        bounds,
        dout,
        perm_lanes,
        distance_rows,
        saved,
        head_weight,
        pieces,
        head_dim,
    )
    head_shard = (head_own + across(head_given).astype(jnp.float32)).astype(jnp.bfloat16)
    gain_attn_grad = gain_sums[0] / gain_attn
    sent, out_part = lax.optimization_barrier((sent, out_part))
    qkv_grad = lax.all_to_all(sent, "ctx", split_axis=0, concat_axis=0, tiled=True)
    spread_len = levels * BLOCK + BLOCK
    by_distance_grad = sum(
        jnp.pad(distance_grads[level], (level * BLOCK, spread_len - (level + 2) * BLOCK))
        for level in range(levels)
    )[BLOCK - 1 : BLOCK - 1 + reach]
    head_bias_grad = jnp.sum(jnp.where(bucket_hot, by_distance_grad[:, None], 0.0), axis=0)
    bias_grad = head_bias_grad[:, None] * head_hot[None, :]

    sums = flat_pack((router_grad, gain_moe_grad, stat_terms, gain_attn_grad, bias_grad), 96)
    chain = []
    scatter_stride = 2 * stride
    while scatter_stride < groups:
        chain.append(functools.partial(scatter_half, ctx=ctx, groups=groups, stride=scatter_stride))
        scatter_stride *= 2
    chain.append(
        lambda part: (part[0] + across(part[1].astype(jnp.bfloat16)).astype(jnp.float32)).astype(
            jnp.bfloat16
        )
    )
    gather_stride = groups // 2
    while gather_stride >= 1:
        chain.append(functools.partial(gather_half, ctx=ctx, groups=groups, stride=gather_stride))
        gather_stride //= 2
    stage = 0

    def beside(piece):
        nonlocal stage, sums, out_part, in_shard, down_shard, qkv_grad
        if stage > 0:
            piece, sums, out_part = lax.optimization_barrier((piece, sums, out_part))
        if stage == 1:
            piece, qkv_grad = lax.optimization_barrier((piece, qkv_grad))
        if stage == 3:
            piece, in_shard, down_shard = lax.optimization_barrier((piece, in_shard, down_shard))
        if 1 << stage <= groups:
            sums = sum_step(sums, groups, 1 << stage)
        if stage < len(chain):
            out_part = chain[stage](out_part)
        stage += 1
        return piece

    gathered = ring.gather(head_shard, beside)
    while stage < max(len(chain), groups.bit_length()):
        beside(head_shard)
    qkv_shard = assemble_weight_gradient(source, gathered, head_dim)
    qkv_grad = jnp.transpose(qkv_grad.reshape(head_count, 3, head_dim, local_rows), (1, 0, 2, 3))
    qkv_grad = qkv_grad.reshape(3 * width, local_rows)

    def feature_grad(weight):
        return lax.dot_general(
            qkv_grad, weight, (((0,), (1,)), ((), ())), preferred_element_type=jnp.float32
        )

    norm_attn_grad = in_order(feature_grad(w_qkv), feature_grad(qkv_other), 1)
    _, norm_attn_back = jax.vjp(rms_norm, stream, gain_attn)
    stream_from_norm, _ = norm_attn_back(norm_attn_grad)
    hidden_grad = (resid_grad + stream_from_norm).astype(jnp.bfloat16)

    out_shard = out_part.astype(jnp.float32)
    sums = sums.reshape(-1)
    cuts = np.cumsum([width * experts, width, 4, width, bucket_count * head_count])
    router_sum = sums[: cuts[0]].reshape(width, experts)
    gain_moe_sum = sums[cuts[0] : cuts[1]]
    stat_sums = sums[cuts[1] : cuts[2]]
    gain_attn_sum = sums[cuts[2] : cuts[3]]
    bias_sum = sums[cuts[3] : cuts[4]].reshape(bucket_count, head_count)
    stats = jnp.sqrt(stat_sums[:3] / (stat_sums[3] * width))
    return (
        final.astype(jnp.bfloat16)[None],
        hidden_grad[None],
        qkv_shard,
        out_shard,
        in_shard[None],
        down_shard[None],
        router_sum,
        gain_attn_sum,
        gain_moe_sum,
        bias_sum,
        stats,
    )


def choose_device(groups, planes, *arguments):
    w_router, rel_bias = arguments[10], arguments[13]
    local_rows = arguments[0].shape[1]
    fits = (
        planes == 2
        and rel_bias.shape[1] == groups
        and 2 * w_router.shape[1] == groups
        and local_rows == 128
    )
    return (fast_device if fits else general_device)(*arguments)


def solution(mesh):
    per_device = functools.partial(choose_device, mesh.shape["ctx"], mesh.shape["wa"])
    placed = (
        P("wa", "ctx", None),
        P("wa", "ctx", None),
        P("wa", None),
        P("wa", None),
        P("wa", "ctx", None),
        P(),
        P("wa", None),
        P("wa", None),
        P("ctx", "wa", None),
        P("ctx", "wa", None),
        P(),
        P(),
        P(),
        P(),
    )
    return jax.shard_map(
        per_device,
        mesh=mesh,
        in_specs=placed,
        out_specs=(
            P("wa", "ctx", None),
            P("wa", "ctx", None),
            P("wa", None),
            P("wa", None),
            P("ctx", "wa", None),
            P("ctx", "wa", None),
            P(),
            P(),
            P(),
            P(),
            P(),
        ),
        check_vma=False,
    )
```

```python
import math

import jax
import jax.numpy as jnp
from jax import lax
from jax.experimental import pallas as pl
from jax.experimental.pallas import tpu as pltpu
from jax.sharding import PartitionSpec as P
import functools
import numpy as np

NSEQ = 8


NORM_EPSILON = 1e-06
MASKED_SCORE = -1e30
TOP_PRECISION = lax.Precision.HIGHEST


def rms_norm(features, scale_gain):
    return (
        features
        * lax.rsqrt(jnp.mean(features * features, axis=-1, keepdims=True) + NORM_EPSILON)
        * scale_gain
    )


def glu_act(gate_up):
    middle = gate_up.shape[-1] // 2
    return jax.nn.gelu(gate_up[..., :middle], approximate=True) * gate_up[..., middle:]


def segment_of(positions, bounds):
    return jnp.sum((positions[:, None] >= bounds[None, :]).astype(jnp.int32), axis=1)


def lead_dot(left, right, precision=None):
    return lax.dot_general(
        left,
        right,
        (((0,), (0,)), ((), ())),
        precision=precision,
        preferred_element_type=jnp.float32,
    )


def tail_dot(left, right):
    return lax.dot_general(
        left, right, (((1,), (1,)), ((), ())), preferred_element_type=jnp.float32
    )


def pair_scores(
    queries, key_rows, query_pos, query_seg, key_pos, key_seg, bucket_starts, bias_table
):
    bucket_count = bias_table.shape[0]
    raw_scores = jnp.einsum("qhd,khd->hqk", queries, key_rows, preferred_element_type=jnp.float32)
    distance = query_pos[:, None] - key_pos[None, :]
    clipped = jnp.maximum(distance, 0)
    bucket_ids = jnp.sum(
        (clipped[:, :, None] >= bucket_starts[None, None, 1:]).astype(jnp.int32), axis=2
    )
    bucket_hot = (
        bucket_ids[:, :, None] == jnp.arange(bucket_count, dtype=jnp.int32)[None, None, :]
    ).astype(jnp.float32)
    bias_block = jnp.einsum("qkb,bh->hqk", bucket_hot, bias_table, precision=TOP_PRECISION)
    scores = raw_scores * 0.125 + bias_block
    allowed = (
        (query_seg[:, None] == key_seg[None, :]) & (distance >= 0) & (query_seg[:, None] < NSEQ)
    )
    return (scores, allowed, bucket_hot)


def attend_piece(
    running, pieces, queries, query_pos, query_seg, perm_row, bounds, bucket_starts, bias_table
):
    key_rows, value_rows = pieces
    piece_rows = key_rows.shape[0]
    head_count = queries.shape[1]
    block_rows = math.gcd(piece_rows, 512)
    keys_split = key_rows.reshape(piece_rows, head_count, -1)
    values_split = value_rows.reshape(piece_rows, head_count, -1)

    def step(step_index, state):
        row_max, totals, weighted = state
        offset = step_index * block_rows
        key_block = lax.dynamic_slice_in_dim(keys_split, offset, block_rows, 0)
        value_block = lax.dynamic_slice_in_dim(values_split, offset, block_rows, 0)
        key_pos = lax.dynamic_slice_in_dim(perm_row, offset, block_rows, 0)
        key_seg = segment_of(key_pos, bounds)
        scores, allowed, _ = pair_scores(
            queries, key_block, query_pos, query_seg, key_pos, key_seg, bucket_starts, bias_table
        )
        new_max = jnp.maximum(row_max, jnp.max(jnp.where(allowed, scores, MASKED_SCORE), axis=2))
        factor = jnp.exp(row_max - new_max)
        exp_scores = jnp.exp(jnp.where(allowed, scores - new_max[:, :, None], MASKED_SCORE))
        totals = totals * factor + jnp.sum(exp_scores, axis=2)
        weighted = weighted * factor[:, :, None] + jnp.einsum(
            "hqk,khd->hqd",
            exp_scores.astype(jnp.bfloat16),
            value_block,
            preferred_element_type=jnp.float32,
        )
        return (new_max, totals, weighted)

    return lax.fori_loop(0, piece_rows // block_rows, step, running)


def block_grads(
    queries,
    dout_low,
    log_total,
    row_delta,
    query_pos,
    query_seg,
    key_block,
    value_block,
    key_pos,
    key_seg,
    bucket_starts,
    bias_table,
):
    scores, allowed, bucket_hot = pair_scores(
        queries, key_block, query_pos, query_seg, key_pos, key_seg, bucket_starts, bias_table
    )
    attn_probs = jnp.exp(jnp.where(allowed, scores - log_total[:, :, None], MASKED_SCORE))
    prob_grad = jnp.einsum(
        "qhd,khd->hqk", dout_low, value_block, preferred_element_type=jnp.float32
    )
    score_grad = (attn_probs * (prob_grad - row_delta[:, :, None])).astype(jnp.bfloat16)
    query_grad = 0.125 * jnp.einsum(
        "hqk,khd->qhd", score_grad, key_block, preferred_element_type=jnp.float32
    )
    key_grad = 0.125 * jnp.einsum(
        "hqk,qhd->khd", score_grad, queries, preferred_element_type=jnp.float32
    )
    value_grad = jnp.einsum(
        "hqk,qhd->khd",
        attn_probs.astype(jnp.bfloat16),
        dout_low,
        preferred_element_type=jnp.float32,
    )
    bias_grad = jnp.einsum(
        "hqk,qkb->bh",
        score_grad,
        bucket_hot.astype(jnp.bfloat16),
        preferred_element_type=jnp.float32,
    )
    return (query_grad, key_grad, value_grad, bias_grad)


def general_device(
    hidden_in,
    out_grad,
    lengths,
    permutation,
    routes,
    bucket_table,
    w_qkv,
    w_out,
    w_in,
    w_down,
    w_router,
    gain_attn,
    gain_moe,
    rel_bias,
):
    stream = hidden_in[0].astype(jnp.float32)
    local_rows = stream.shape[0]
    model_width = stream.shape[1]
    head_count = rel_bias.shape[1]
    bucket_count = rel_bias.shape[0]
    head_dim = model_width // head_count
    experts = w_router.shape[1]
    slot_cap = 4 * local_rows // experts
    groups = lax.axis_size("ctx")
    perm_row = permutation[0]
    bounds = jnp.cumsum(lengths[0])
    own_start = lax.axis_index("ctx") * local_rows
    query_pos = lax.dynamic_slice_in_dim(perm_row, own_start, local_rows, 0)
    query_seg = segment_of(query_pos, bounds)
    is_valid = (query_seg < NSEQ).astype(jnp.float32)
    bucket_starts = jnp.sum(
        (bucket_table[:, None] < jnp.arange(bucket_count, dtype=jnp.int32)[None, :]).astype(
            jnp.int32
        ),
        axis=0,
    )
    qkv_full, out_full, in_full, down_full = (
        lax.all_gather(w_qkv, "wa", axis=0, tiled=True),
        lax.all_gather(w_out, "wa", axis=0, tiled=True),
        lax.all_gather(w_in[0], "wa", axis=0, tiled=True),
        lax.all_gather(w_down[0], "wa", axis=0, tiled=True),
    )
    normed_attn = rms_norm(stream, gain_attn)
    normed_attn_low = normed_attn.astype(jnp.bfloat16)
    qkv = jnp.dot(normed_attn_low, qkv_full, preferred_element_type=jnp.float32).astype(
        jnp.bfloat16
    )
    queries = qkv[:, :model_width].reshape(local_rows, head_count, head_dim)
    key_rows = qkv[:, model_width : 2 * model_width]
    value_rows = qkv[:, 2 * model_width :]
    initial = (
        jnp.full((head_count, local_rows), MASKED_SCORE, jnp.float32),
        jnp.zeros((head_count, local_rows), jnp.float32),
        jnp.zeros((head_count, local_rows, head_dim), jnp.float32),
    )
    row_max, totals, weighted = attend_piece(
        initial,
        (
            lax.all_gather(key_rows, "ctx", axis=0, tiled=True),
            lax.all_gather(value_rows, "ctx", axis=0, tiled=True),
        ),
        queries,
        query_pos,
        query_seg,
        perm_row,
        bounds,
        bucket_starts,
        rel_bias,
    )
    safe_totals = jnp.where(query_seg[None, :] < NSEQ, totals, 1.0)
    log_total = row_max + jnp.log(safe_totals)
    attn_heads = weighted / safe_totals[:, :, None]
    attn_mix = jnp.transpose(attn_heads, (1, 0, 2)).reshape(local_rows, model_width)
    attn_low = attn_mix.astype(jnp.bfloat16)
    attn_out = jnp.dot(attn_low, out_full, preferred_element_type=jnp.float32)
    resid = stream + attn_out
    normed_moe = rms_norm(resid, gain_moe)
    normed_moe_low = normed_moe.astype(jnp.bfloat16)
    normed_moe_wide = normed_moe_low.astype(jnp.float32)
    logits = jnp.dot(normed_moe_wide, w_router, precision=TOP_PRECISION)
    route_rows = routes[0]
    expert_ids = jnp.arange(experts, dtype=jnp.int32)
    first_hot = route_rows[:, 0:1] == expert_ids[None, :]
    second_hot = route_rows[:, 1:2] == expert_ids[None, :]
    chosen = jnp.stack(
        [
            jnp.sum(jnp.where(first_hot, logits, 0.0), axis=1),
            jnp.sum(jnp.where(second_hot, logits, 0.0), axis=1),
        ],
        axis=1,
    )
    gate_probs = jax.nn.softmax(chosen, axis=1)
    counts = jnp.cumsum((first_hot | second_hot).astype(jnp.int32), axis=0)
    first_slot = jnp.sum(jnp.where(first_hot, counts - 1, 0), axis=1)
    second_slot = jnp.sum(jnp.where(second_hot, counts - 1, 0), axis=1)
    first_lane = route_rows[:, 0] * slot_cap + first_slot
    second_lane = route_rows[:, 1] * slot_cap + second_slot
    lane_ids = jnp.arange(experts * slot_cap, dtype=jnp.int32)
    first_pick = (first_lane[:, None] == lane_ids[None, :]).astype(jnp.bfloat16)
    second_pick = (second_lane[:, None] == lane_ids[None, :]).astype(jnp.bfloat16)
    dispatch = (
        lead_dot(first_pick, normed_moe_low) + lead_dot(second_pick, normed_moe_low)
    ).astype(jnp.bfloat16)
    spread = jnp.broadcast_to(
        dispatch.reshape(experts, 1, slot_cap, model_width), (experts, 2, slot_cap, model_width)
    ).reshape(groups, slot_cap, model_width)
    received = lax.all_to_all(spread, "ctx", split_axis=0, concat_axis=0, tiled=True)
    item_count = received.shape[1]
    row_block = received.reshape(-1, model_width)
    gate_up = jnp.dot(row_block, in_full, preferred_element_type=jnp.float32)
    hidden = glu_act(gate_up).astype(jnp.bfloat16)
    partial_value = tail_dot(hidden, down_full).astype(jnp.bfloat16)
    returned = lax.all_to_all(
        partial_value.reshape(groups, item_count, model_width),
        "ctx",
        split_axis=0,
        concat_axis=0,
        tiled=True,
    )
    returned, gate_up_kept, received_kept = (
        returned,
        gate_up.reshape(groups, item_count, -1),
        received,
    )
    halves = returned.reshape(experts, 2, slot_cap, model_width)
    first_half = halves[:, 0].reshape(-1, model_width)
    second_half = halves[:, 1].reshape(-1, model_width)
    picked_first = jnp.dot(first_pick, first_half, preferred_element_type=jnp.float32) + jnp.dot(
        first_pick, second_half, preferred_element_type=jnp.float32
    )
    picked_second = jnp.dot(second_pick, first_half, preferred_element_type=jnp.float32) + jnp.dot(
        second_pick, second_half, preferred_element_type=jnp.float32
    )
    moe_out = gate_probs[:, 0:1] * picked_first + gate_probs[:, 1:2] * picked_second
    final = resid + moe_out
    valid_col = is_valid[:, None]
    stat_terms = jnp.stack(
        [
            jnp.sum(valid_col * final * final),
            jnp.sum(valid_col * attn_out * attn_out),
            jnp.sum(valid_col * moe_out * moe_out),
        ]
    )
    valid_count = jnp.sum(is_valid)
    grad_final = out_grad[0].astype(jnp.float32)
    first_dy = (gate_probs[:, 0:1] * grad_final).astype(jnp.bfloat16)
    second_dy = (gate_probs[:, 1:2] * grad_final).astype(jnp.bfloat16)
    gate_grad = jnp.stack(
        [jnp.sum(grad_final * picked_first, axis=1), jnp.sum(grad_final * picked_second, axis=1)],
        axis=1,
    )
    _, gate_back = jax.vjp(lambda chosen_in: jax.nn.softmax(chosen_in, axis=1), chosen)
    (chosen_grad,) = gate_back(gate_grad)
    logit_grad = jnp.where(first_hot, chosen_grad[:, 0:1], 0.0) + jnp.where(
        second_hot, chosen_grad[:, 1:2], 0.0
    )
    router_grad = lead_dot(normed_moe_wide, logit_grad, TOP_PRECISION)
    norm_moe_grad = jnp.dot(logit_grad, w_router.T, precision=TOP_PRECISION)
    dy_slots = (lead_dot(first_pick, first_dy) + lead_dot(second_pick, second_dy)).astype(
        jnp.bfloat16
    )
    dy_spread = jnp.broadcast_to(
        dy_slots.reshape(experts, 1, slot_cap, model_width), (experts, 2, slot_cap, model_width)
    ).reshape(groups, slot_cap, model_width)
    received_grad = lax.all_to_all(dy_spread, "ctx", split_axis=0, concat_axis=0, tiled=True)
    rows_grad = received_grad.reshape(-1, model_width)
    rows_kept = received_kept.reshape(-1, model_width)
    gate_up_rows = gate_up_kept.reshape(rows_grad.shape[0], -1)
    hidden_rows, act_back = jax.vjp(glu_act, gate_up_rows)
    hidden_low = hidden_rows.astype(jnp.bfloat16)
    hidden_grad_rows = jnp.dot(rows_grad, down_full, preferred_element_type=jnp.float32)
    down_grad = lead_dot(rows_grad, hidden_low)
    (gate_up_grad,) = act_back(hidden_grad_rows)
    gate_up_low = gate_up_grad.astype(jnp.bfloat16)
    in_grad = lead_dot(rows_kept, gate_up_low)
    rows_back = tail_dot(gate_up_low, in_full).astype(jnp.bfloat16)
    returned_grad = lax.all_to_all(
        rows_back.reshape(groups, slot_cap, model_width),
        "ctx",
        split_axis=0,
        concat_axis=0,
        tiled=True,
    )
    grad_halves = returned_grad.reshape(experts, 2, slot_cap, model_width)
    first_back = grad_halves[:, 0].reshape(-1, model_width)
    second_back = grad_halves[:, 1].reshape(-1, model_width)
    norm_moe_grad = (
        norm_moe_grad
        + jnp.dot(first_pick, first_back, preferred_element_type=jnp.float32)
        + jnp.dot(first_pick, second_back, preferred_element_type=jnp.float32)
    )
    norm_moe_grad = (
        norm_moe_grad
        + jnp.dot(second_pick, first_back, preferred_element_type=jnp.float32)
        + jnp.dot(second_pick, second_back, preferred_element_type=jnp.float32)
    )
    _, norm_moe_back = jax.vjp(rms_norm, resid, gain_moe)
    resid_from_norm, gain_moe_grad = norm_moe_back(norm_moe_grad)
    resid_grad = grad_final + resid_from_norm
    attn_grad_low = resid_grad.astype(jnp.bfloat16)
    out_proj_grad = lead_dot(attn_low, attn_grad_low)
    mix_grad = tail_dot(attn_grad_low, out_full)
    dout_low = mix_grad.astype(jnp.bfloat16).reshape(local_rows, head_count, head_dim)
    row_delta = jnp.einsum("qhd,hqd->hq", dout_low.astype(jnp.float32), attn_heads)
    key_all, value_all = (
        lax.all_gather(key_rows, "ctx", axis=0, tiled=True),
        lax.all_gather(value_rows, "ctx", axis=0, tiled=True),
    )
    total_rows = key_all.shape[0]
    block_rows = math.gcd(total_rows, 512)
    keys_split = key_all.reshape(total_rows, head_count, head_dim)
    values_split = value_all.reshape(total_rows, head_count, head_dim)
    seg_all = segment_of(perm_row, bounds)

    def key_step(step_index, state):
        query_acc, bias_acc, pair_buffer = state
        offset = step_index * block_rows
        key_block = lax.dynamic_slice_in_dim(keys_split, offset, block_rows, 0)
        value_block = lax.dynamic_slice_in_dim(values_split, offset, block_rows, 0)
        key_pos = lax.dynamic_slice_in_dim(perm_row, offset, block_rows, 0)
        key_seg = lax.dynamic_slice_in_dim(seg_all, offset, block_rows, 0)
        query_grad, key_grad, value_grad, bias_grad = block_grads(
            queries,
            dout_low,
            log_total,
            row_delta,
            query_pos,
            query_seg,
            key_block,
            value_block,
            key_pos,
            key_seg,
            bucket_starts,
            rel_bias,
        )
        joined = jnp.concatenate(
            [
                key_grad.reshape(block_rows, model_width),
                value_grad.reshape(block_rows, model_width),
            ],
            axis=1,
        )
        pair_buffer = lax.dynamic_update_slice_in_dim(pair_buffer, joined, offset, 0)
        return (query_acc + query_grad, bias_acc + bias_grad, pair_buffer)

    start_state = (
        jnp.zeros((local_rows, head_count, head_dim), jnp.float32),
        jnp.zeros((bucket_count, head_count), jnp.float32),
        jnp.zeros((total_rows, 2 * model_width), jnp.float32),
    )
    query_acc, bias_total, pair_buffer = lax.fori_loop(
        0, total_rows // block_rows, key_step, start_state
    )
    pair_grad = lax.psum_scatter(
        pair_buffer.astype(jnp.bfloat16), "ctx", scatter_dimension=0, tiled=True
    ).astype(jnp.float32)
    query_total = query_acc.reshape(local_rows, model_width)
    key_total = pair_grad[:, :model_width]
    value_total = pair_grad[:, model_width:]
    qkv_grad_low = jnp.concatenate([query_total, key_total, value_total], axis=1).astype(
        jnp.bfloat16
    )
    qkv_weight_grad = lead_dot(normed_attn_low, qkv_grad_low)
    norm_attn_grad = tail_dot(qkv_grad_low, qkv_full)
    _, norm_attn_back = jax.vjp(rms_norm, stream, gain_attn)
    stream_from_norm, gain_attn_grad = norm_attn_back(norm_attn_grad)
    hidden_grad = (resid_grad + stream_from_norm).astype(jnp.bfloat16)
    qkv_shard, out_shard, in_shard, down_shard = (
        lax.psum_scatter(
            qkv_weight_grad.astype(jnp.bfloat16), "wa", scatter_dimension=0, tiled=True
        ).astype(jnp.float32),
        lax.psum_scatter(
            out_proj_grad.astype(jnp.bfloat16), "wa", scatter_dimension=0, tiled=True
        ).astype(jnp.float32),
        lax.psum_scatter(
            in_grad.astype(jnp.bfloat16), "wa", scatter_dimension=0, tiled=True
        ).astype(jnp.float32),
        lax.psum_scatter(
            down_grad.astype(jnp.bfloat16), "wa", scatter_dimension=0, tiled=True
        ).astype(jnp.float32),
    )
    qkv_shard, out_shard = (
        lax.psum(qkv_shard.astype(jnp.bfloat16), "ctx").astype(jnp.float32),
        lax.psum(out_shard.astype(jnp.bfloat16), "ctx").astype(jnp.float32),
    )
    stat_sums, count_sum, router_sum, gain_attn_sum, gain_moe_sum, bias_sum = lax.psum(
        (stat_terms, valid_count, router_grad, gain_attn_grad, gain_moe_grad, bias_total),
        ("ctx", "wa"),
    )
    stats = jnp.sqrt(stat_sums / (count_sum * model_width))
    return (
        final.astype(jnp.bfloat16)[None],
        hidden_grad[None],
        qkv_shard,
        out_shard,
        in_shard[None],
        down_shard[None],
        router_sum,
        gain_attn_sum,
        gain_moe_sum,
        bias_sum,
        stats,
    )


LARGE_COST = pl.CostEstimate(flops=200 << 30, bytes_accessed=1 << 20, transcendentals=0)
SMALL_COST = pl.CostEstimate(flops=1 << 20, bytes_accessed=1 << 16, transcendentals=0)
BLOCK = 256


def nt_dot(left, right):
    return lax.dot_general(
        left, right, (((1,), (1,)), ((), ())), preferred_element_type=jnp.float32
    )


def plain_dot(left, right):
    return jnp.dot(left, right, preferred_element_type=jnp.float32)


def block_at(index):
    return pl.ds(pl.multiple_of(index * BLOCK, BLOCK), BLOCK)


def segment_begin(positions, bounds):
    begin = positions * 0
    for index in range(NSEQ):
        begin = jnp.where(positions >= bounds[index], bounds[index], begin)
    return begin


def fill_bias_tiles(distance_rows, tiles):
    for level in range(tiles.shape[0]):
        spread = jnp.broadcast_to(distance_rows[level : level + 1, :], (BLOCK, 2 * BLOCK))
        tiles[level] = pltpu.roll(spread, BLOCK + 1, 1, stride=1, stride_axis=0)[:, :BLOCK]


def fill_sorter(perm, sorter):
    slots = perm.shape[1]

    def step(index, carry):
        wanted = lax.broadcasted_iota(jnp.int32, (BLOCK, slots), 0) + index * BLOCK
        sorter[block_at(index), :] = jnp.where(perm[...] == wanted, 1.0, 0.0).astype(jnp.bfloat16)
        return carry

    lax.fori_loop(0, slots // BLOCK, step, 0)


def pair_mask(key_block, query_pos, query_begin):
    key_pos = lax.broadcasted_iota(jnp.int32, (BLOCK, BLOCK), 0) + key_block * BLOCK
    return (key_pos <= query_pos) & (key_pos >= query_begin)


def attention_forward_kernel(
    piece_count, head_dim, source, bounds, weight, perm, distance_rows, *refs
):
    pieces = refs[:piece_count]
    mixed, sorted_out, rows_out, wide_out, log_out = refs[piece_count : piece_count + 5]
    raw, sorter, tiles, mixed_sorted = refs[piece_count + 5 :]
    slots = perm.shape[1]
    blocks = slots // BLOCK
    local_rows = mixed.shape[2]
    for index in range(piece_count):
        offset = pl.multiple_of(source[index] * local_rows, local_rows)
        raw[:, pl.ds(offset, pieces[index].shape[0])] = nt_dot(
            weight[...], pieces[index][...]
        ).astype(jnp.bfloat16)
    fill_bias_tiles(distance_rows, tiles)
    fill_sorter(perm, sorter)

    def sort_step(index, carry):
        columns = nt_dot(raw[...], sorter[block_at(index), :])
        sorted_out[:, block_at(index)] = columns.astype(jnp.bfloat16)
        rows_out[block_at(index), :] = jnp.transpose(columns[head_dim:]).astype(jnp.bfloat16)
        return carry

    lax.fori_loop(0, blocks, sort_step, 0)
    mixed_sorted[...] = jnp.zeros_like(mixed_sorted)
    total = bounds[NSEQ - 1]

    def query_step(query_block, carry):
        queries = sorted_out[:head_dim, block_at(query_block)] * 0.125
        query_pos = lax.broadcasted_iota(jnp.int32, (1, BLOCK), 1) + query_block * BLOCK
        query_begin = segment_begin(query_pos, bounds)
        first = segment_begin(query_block * BLOCK, bounds) // BLOCK

        def key_step(key_block, state):
            row_max, totals, weighted = state
            scores = plain_dot(rows_out[block_at(key_block), :head_dim], queries)
            scores = jnp.where(
                pair_mask(key_block, query_pos, query_begin),
                scores + tiles[query_block - key_block],
                MASKED_SCORE,
            )
            new_max = jnp.maximum(row_max, jnp.max(scores, axis=0, keepdims=True))
            factor = jnp.exp(row_max - new_max)
            exp_scores = jnp.exp(scores - new_max)
            totals = totals * factor + jnp.sum(exp_scores, axis=0, keepdims=True)
            values = sorted_out[2 * head_dim :, block_at(key_block)]
            weighted = weighted * factor + plain_dot(values, exp_scores.astype(jnp.bfloat16))
            return (new_max, totals, weighted)

        row_max, totals, weighted = lax.fori_loop(
            first,
            query_block + 1,
            key_step,
            (
                jnp.full((1, BLOCK), MASKED_SCORE, jnp.float32),
                jnp.zeros((1, BLOCK), jnp.float32),
                jnp.zeros((head_dim, BLOCK), jnp.float32),
            ),
        )
        outcome = jnp.where(query_pos < total, weighted / totals, 0.0)
        wide_out[:, block_at(query_block)] = outcome
        log_out[:, block_at(query_block)] = row_max + jnp.log(totals)
        mixed_sorted[:, block_at(query_block)] = outcome.astype(jnp.bfloat16)
        return carry

    lax.fori_loop(0, (total + BLOCK - 1) // BLOCK, query_step, 0)
    for index in range(blocks):
        columns = plain_dot(mixed_sorted[...], sorter[:, index * BLOCK : (index + 1) * BLOCK])
        columns = columns.astype(jnp.bfloat16)
        for part in range(BLOCK // local_rows):
            mixed[index * (BLOCK // local_rows) + part] = columns[
                :, part * local_rows : (part + 1) * local_rows
            ]


def attention_backward_kernel(
    piece_count,
    head_dim,
    source,
    plane,
    bounds,
    received,
    perm,
    distance_rows,
    sorted_in,
    rows_in,
    wide_in,
    log_in,
    weight,
    *refs,
):
    pieces = refs[:piece_count]
    sent, own_out, other_out, gain_out, distance_out = refs[piece_count : piece_count + 5]
    dout_raw, dout_sorted, sorter, tiles, tile_grads, grad_acc, grad_sorted, grad_out = refs[
        piece_count + 5 :
    ]
    slots = perm.shape[1]
    blocks = slots // BLOCK
    groups, _, local_rows = received.shape
    for index in range(groups):
        dout_raw[:, index * local_rows : (index + 1) * local_rows] = received[index]
    fill_bias_tiles(distance_rows, tiles)
    fill_sorter(perm, sorter)

    def sort_step(index, carry):
        columns = nt_dot(dout_raw[...], sorter[block_at(index), :])
        dout_sorted[:, block_at(index)] = columns.astype(jnp.bfloat16)
        return carry

    lax.fori_loop(0, blocks, sort_step, 0)
    tile_grads[...] = jnp.zeros_like(tile_grads)
    grad_acc[...] = jnp.zeros_like(grad_acc)
    total = bounds[NSEQ - 1]

    def query_step(query_block, carry):
        queries = sorted_in[:head_dim, block_at(query_block)] * 0.125
        douts = dout_sorted[:, block_at(query_block)]
        row_delta = jnp.sum(
            douts.astype(jnp.float32) * wide_in[:, block_at(query_block)], axis=0, keepdims=True
        )
        log_total = log_in[:, block_at(query_block)]
        query_pos = lax.broadcasted_iota(jnp.int32, (1, BLOCK), 1) + query_block * BLOCK
        query_begin = segment_begin(query_pos, bounds)
        inside = query_pos < total
        first = segment_begin(query_block * BLOCK, bounds) // BLOCK

        def key_step(key_block, query_grad):
            rows = rows_in[block_at(key_block), :]
            scores = plain_dot(rows[:, :head_dim], queries) + tiles[query_block - key_block]
            probs = jnp.exp(
                jnp.where(
                    pair_mask(key_block, query_pos, query_begin) & inside,
                    scores - log_total,
                    MASKED_SCORE,
                )
            )
            prob_grad = plain_dot(rows[:, head_dim:], douts)
            score_grad = (probs * (prob_grad - row_delta)).astype(jnp.bfloat16)
            tile_grads[query_block - key_block] += score_grad.astype(jnp.float32)
            grad_acc[head_dim : 2 * head_dim, block_at(key_block)] += nt_dot(queries, score_grad)
            grad_acc[2 * head_dim :, block_at(key_block)] += nt_dot(
                douts, probs.astype(jnp.bfloat16)
            )
            keys = sorted_in[head_dim : 2 * head_dim, block_at(key_block)]
            return query_grad + plain_dot(keys, score_grad)

        query_grad = lax.fori_loop(
            first, query_block + 1, key_step, jnp.zeros((head_dim, BLOCK), jnp.float32)
        )
        grad_acc[:head_dim, block_at(query_block)] = query_grad * 0.125
        return carry

    lax.fori_loop(0, (total + BLOCK - 1) // BLOCK, query_step, 0)
    grad_sorted[...] = grad_acc[...].astype(jnp.bfloat16)
    for index in range(blocks):
        columns = plain_dot(grad_sorted[...], sorter[:, index * BLOCK : (index + 1) * BLOCK])
        columns = columns.astype(jnp.bfloat16)
        grad_out[:, index * BLOCK : (index + 1) * BLOCK] = columns
        for part in range(BLOCK // local_rows):
            sent[index * (BLOCK // local_rows) + part] = columns[
                :, part * local_rows : (part + 1) * local_rows
            ]
    head_total = jnp.zeros(weight.shape, jnp.float32)
    for index in range(piece_count):
        offset = pl.multiple_of(source[index] * local_rows, local_rows)
        head_total = head_total + plain_dot(
            grad_out[:, pl.ds(offset, pieces[index].shape[0])], pieces[index][...]
        )
    gain_out[...] = jnp.sum(weight[...].astype(jnp.float32) * head_total, axis=0, keepdims=True)
    half = weight.shape[1] // 2

    @pl.when(plane[0] == 0)
    def _():
        own_out[...] = head_total[:, :half]
        other_out[...] = head_total[:, half:].astype(jnp.bfloat16)

    @pl.when(plane[0] != 0)
    def _():
        own_out[...] = head_total[:, half:]
        other_out[...] = head_total[:, :half].astype(jnp.bfloat16)

    row_ids = lax.broadcasted_iota(jnp.int32, (BLOCK, BLOCK), 0)
    column_ids = lax.broadcasted_iota(jnp.int32, (BLOCK, BLOCK), 1)
    mirror = jnp.where(row_ids + column_ids == BLOCK - 1, 1.0, 0.0)
    for level in range(tiles.shape[0]):
        turned = jnp.dot(
            mirror, tile_grads[level], precision=TOP_PRECISION, preferred_element_type=jnp.float32
        )
        wide = jnp.concatenate([turned, jnp.zeros((BLOCK, BLOCK), jnp.float32)], axis=1)
        turned = pltpu.roll(wide, 0, 1, stride=1, stride_axis=0)
        distance_out[level : level + 1, :] = jnp.sum(turned, axis=0, keepdims=True)


def assemble_kernel(piece_count, head_dim, out_rows, source, *refs):
    pieces = refs[:piece_count]
    qkv_out, proj_out = refs[piece_count:]
    width = qkv_out.shape[1] // 3
    piece_rows, half = pieces[-1].shape
    core = source[piece_count - 2] % 2
    upper = proj_out.shape[0] // 2
    for index in range(piece_count - 1):
        chip = source[index] // 2
        if index < piece_count - 2:
            first, second = pieces[index][:piece_rows], pieces[index][piece_rows:]
        else:
            mine, theirs = pieces[index][...], pieces[index + 1][...]
            first = jnp.where(core == 0, mine, theirs)
            second = jnp.where(core == 0, theirs, mine)
        for part in range(3):
            span = slice(part * head_dim, (part + 1) * head_dim)
            columns = jnp.concatenate([first[span], second[span]], axis=0).astype(jnp.float32)
            offset = pl.multiple_of(part * width + chip * 2 * head_dim, 2 * head_dim)
            qkv_out[:, pl.ds(offset, 2 * head_dim)] = jnp.transpose(columns)
        for side, values in enumerate((first, second)):
            rows = pl.ds(pl.multiple_of(side * upper + chip * out_rows, out_rows), out_rows)
            low = values[3 * head_dim : 3 * head_dim + out_rows]
            proj_out[rows, :half] = low.astype(jnp.float32)
            proj_out[rows, half:] = values[3 * head_dim + out_rows :].astype(jnp.float32)


def assemble_weight_gradients(source, pieces, head_dim, width):
    piece_rows, half = pieces[-1].shape
    out_rows = (piece_rows - 3 * head_dim) // 2
    return pl.pallas_call(
        functools.partial(assemble_kernel, len(pieces), head_dim, out_rows),
        out_shape=(shaped((half, 3 * width), jnp.float32), shaped((half, width), jnp.float32)),
        in_specs=[smem()] + [vmem()] * len(pieces),
        out_specs=(vmem(), vmem()),
        cost_estimate=SMALL_COST,
    )(source, *pieces)


GELU_SCALE = math.sqrt(2.0 / math.pi)
LANES = 128


def tile_at(index, begin=0, size=LANES):
    return pl.ds(pl.multiple_of(begin + index * size, LANES), size)


def hbm():
    return pl.BlockSpec(memory_space=pl.ANY)


def expert_forward_kernel(
    units,
    mine,
    theirs,
    weights,
    part_mine,
    part_theirs,
    hidden_out,
    slope_out,
    act_out,
    in_weight,
    down_weight,
    hidden,
    gate_slope,
    act,
    even,
    odd,
    in_sem,
    down_sem,
    out_sem,
):
    count, width = mine.shape[0], in_weight.shape[0]
    tiles = units // LANES

    def fetch(tile, side):
        lanes = tile_at(tile, side * units)
        return pltpu.make_async_copy(
            weights.at[:, lanes], in_weight.at[:, lanes], in_sem.at[tile, side]
        )

    down_copy = pltpu.make_async_copy(weights.at[:, 2 * units :], down_weight, down_sem)
    for tile in range(tiles):
        for side in range(2):
            fetch(tile, side).start()
    down_copy.start()

    def arrived(tile):
        for side in range(2):
            fetch(tile, side).wait()

    def multiply(tile, target):
        weight = jnp.concatenate(
            [in_weight[:, tile_at(tile)], in_weight[:, tile_at(tile, units)]], axis=1
        )
        target[:count] = plain_dot(mine[:, :width], weight)
        target[count:] = plain_dot(theirs[:, :width], weight)

    def activate(tile, held):
        gate, up = held[:, :LANES], held[:, LANES:]
        square = gate * gate
        bent = jnp.tanh(gate * (GELU_SCALE + (0.044715 * GELU_SCALE) * square))
        share = 0.5 + 0.5 * bent
        slope = share + (0.5 - 0.5 * bent * bent) * (
            gate * (GELU_SCALE + (3.0 * 0.044715 * GELU_SCALE) * square)
        )
        active = gate * share
        hidden[:, tile_at(tile)] = (active * up).astype(jnp.bfloat16)
        gate_slope[:, tile_at(tile)] = (up * slope).astype(jnp.bfloat16)
        act[:, tile_at(tile)] = active.astype(jnp.bfloat16)

    arrived(0)
    multiply(0, even)

    def step(pair, carry):
        arrived(2 * pair + 1)
        arrived(2 * pair + 2)
        multiply(2 * pair + 1, odd)
        activate(2 * pair, even)
        multiply(2 * pair + 2, even)
        activate(2 * pair + 1, odd)
        return carry

    lax.fori_loop(0, (tiles - 1) // 2, step, 0)
    if tiles % 2 == 0:
        arrived(tiles - 1)
        multiply(tiles - 1, odd)
        activate(tiles - 2, even)
        activate(tiles - 1, odd)
    else:
        activate(tiles - 1, even)
    copies = [
        pltpu.make_async_copy(held, out, out_sem.at[index])
        for index, (held, out) in enumerate(
            ((hidden, hidden_out), (gate_slope, slope_out), (act, act_out))
        )
    ]
    for copy in copies:
        copy.start()
    down_copy.wait()

    def down_step(tile, carry):
        weight = down_weight[block_at(tile), :]
        part_theirs[:, block_at(tile)] = nt_dot(hidden[count:], weight).astype(jnp.bfloat16)
        part_mine[:, block_at(tile)] = nt_dot(hidden[:count], weight).astype(jnp.bfloat16)
        return carry

    lax.fori_loop(0, width // BLOCK, down_step, 0)
    for copy in copies:
        copy.wait()


def expert_forward(mine, theirs, weights, units):
    count, wide = mine.shape
    width = weights.shape[0]
    tall = (2 * count, units)
    return pl.pallas_call(
        functools.partial(expert_forward_kernel, units),
        out_shape=(
            shaped((count, width), jnp.bfloat16),
            shaped((count, width), jnp.bfloat16),
        )
        + (shaped(tall, jnp.bfloat16),) * 3,
        in_specs=[vmem(), vmem(), hbm()],
        out_specs=(vmem(), vmem(), hbm(), hbm(), hbm()),
        scratch_shapes=[
            pltpu.VMEM((width, 2 * units), jnp.bfloat16),
            pltpu.VMEM((width, units), jnp.bfloat16),
            pltpu.VMEM(tall, jnp.bfloat16),
            pltpu.VMEM(tall, jnp.bfloat16),
            pltpu.VMEM(tall, jnp.bfloat16),
            pltpu.VMEM((2 * count, 2 * LANES), jnp.float32),
            pltpu.VMEM((2 * count, 2 * LANES), jnp.float32),
            pltpu.SemaphoreType.DMA((units // LANES, 2)),
            pltpu.SemaphoreType.DMA,
            pltpu.SemaphoreType.DMA((3,)),
        ],
        cost_estimate=SMALL_COST,
    )(mine, theirs, weights)


def expert_backward_kernel(
    units,
    mine_left,
    mine_right,
    theirs_left,
    theirs_right,
    mine_rows,
    theirs_rows,
    slope_in,
    act_in,
    weights,
    back_mine,
    back_theirs,
    grads_out,
    scaled,
    in_weight,
    down_weight,
    gate_slope,
    act,
    unit_grads,
    tile_sem,
    in_sem,
    out_sem,
):
    count, half = mine_left.shape
    width = 2 * half
    spans = [(begin, min(BLOCK, units - begin)) for begin in range(0, units, BLOCK)]
    blocks = width // BLOCK
    tile_copies = []
    for index, (begin, size) in enumerate(spans):
        lanes = slice(begin, begin + size)
        far = slice(2 * units + begin, 2 * units + begin + size)
        tile_copies.append(
            (
                pltpu.make_async_copy(
                    weights.at[:, far], down_weight.at[:, lanes], tile_sem.at[index, 0]
                ),
                pltpu.make_async_copy(
                    slope_in.at[:, lanes], gate_slope.at[:, lanes], tile_sem.at[index, 1]
                ),
                pltpu.make_async_copy(act_in.at[:, lanes], act.at[:, lanes], tile_sem.at[index, 2]),
            )
        )
    in_copies = [
        pltpu.make_async_copy(
            weights.at[index * BLOCK : (index + 1) * BLOCK, : 2 * units],
            in_weight.at[index * BLOCK : (index + 1) * BLOCK, :],
            in_sem.at[index],
        )
        for index in range(blocks)
    ]
    for copies in tile_copies:
        for copy in copies:
            copy.start()
    for copy in in_copies:
        copy.start()
    for index, pair in enumerate(
        ((mine_left, mine_right, mine_rows), (theirs_left, theirs_right, theirs_rows))
    ):
        span = slice(index * count, (index + 1) * count)
        gate = jnp.sum(pair[2][:, width:].astype(jnp.float32), axis=1, keepdims=True)
        for side in range(2):
            scaled[span, side * half : (side + 1) * half] = (
                gate * pair[side][...].astype(jnp.float32)
            ).astype(jnp.bfloat16)
    for copies, (begin, size) in zip(tile_copies, spans):
        for copy in copies:
            copy.wait()
        lanes = slice(begin, begin + size)
        for index in range(2):
            span = slice(index * count, (index + 1) * count)
            hidden_grad = plain_dot(scaled[span], down_weight[:, lanes])
            unit_grads[span, lanes] = (
                hidden_grad * gate_slope[span, lanes].astype(jnp.float32)
            ).astype(jnp.bfloat16)
            unit_grads[span, units + begin : units + begin + size] = (
                hidden_grad * act[span, lanes].astype(jnp.float32)
            ).astype(jnp.bfloat16)
    out_copy = pltpu.make_async_copy(unit_grads, grads_out, out_sem)
    out_copy.start()
    for index in range(blocks):
        in_copies[index].wait()

    def step(tile, carry):
        weight = in_weight[block_at(tile), :]
        back_theirs[:, block_at(tile)] = nt_dot(unit_grads[count:], weight).astype(jnp.bfloat16)
        back_mine[:, block_at(tile)] = nt_dot(unit_grads[:count], weight).astype(jnp.bfloat16)
        return carry

    lax.fori_loop(0, blocks, step, 0)
    out_copy.wait()


def expert_backward(parts, rows, gate_slope, act, weights):
    count, half = parts[0].shape
    units = act.shape[1]
    width = 2 * half
    return pl.pallas_call(
        functools.partial(expert_backward_kernel, units),
        out_shape=(
            shaped((count, width), jnp.bfloat16),
            shaped((count, width), jnp.bfloat16),
            shaped((2 * count, 2 * units), jnp.bfloat16),
            shaped((2 * count, width), jnp.bfloat16),
        ),
        in_specs=[vmem()] * 6 + [hbm()] * 3,
        out_specs=(vmem(), vmem(), hbm(), vmem()),
        scratch_shapes=[
            pltpu.VMEM((width, 2 * units), jnp.bfloat16),
            pltpu.VMEM((width, units), jnp.bfloat16),
            pltpu.VMEM((2 * count, units), jnp.bfloat16),
            pltpu.VMEM((2 * count, units), jnp.bfloat16),
            pltpu.VMEM((2 * count, 2 * units), jnp.bfloat16),
            pltpu.SemaphoreType.DMA((-(-units // BLOCK), 3)),
            pltpu.SemaphoreType.DMA((width // BLOCK,)),
            pltpu.SemaphoreType.DMA,
        ],
        cost_estimate=SMALL_COST,
    )(*parts, *rows, gate_slope, act, weights)


def turned_product_kernel(*refs):
    parts, right, out, turned = refs[:-3], refs[-3], refs[-2], refs[-1]
    width, columns = turned.shape[0], out.shape[1]
    at = 0
    for part in parts:
        count = part.shape[0]
        turned[:, at : at + count] = jnp.transpose(part[:, :width])
        at += count

    def step(tile, carry):
        out[:, block_at(tile)] = plain_dot(turned[...], right[:, block_at(tile)]).astype(
            jnp.bfloat16
        )
        return carry

    lax.fori_loop(0, columns // BLOCK, step, 0)
    if columns % BLOCK:
        rest = slice(columns - columns % BLOCK, columns)
        out[:, rest] = plain_dot(turned[...], right[:, rest]).astype(jnp.bfloat16)


def turned_product(parts, right, width):
    rows, columns = right.shape
    return pl.pallas_call(
        turned_product_kernel,
        out_shape=shaped((width, columns), jnp.bfloat16),
        in_specs=[vmem()] * (len(parts) + 1),
        out_specs=vmem(),
        scratch_shapes=[pltpu.VMEM((width, rows), jnp.bfloat16)],
        cost_estimate=SMALL_COST,
    )(*parts, right)


def close_moe_kernel(
    plane,
    back,
    pick,
    base,
    resid,
    gain,
    out_grad,
    out_own,
    out_other,
    mixed,
    core,
    resid_grad,
    gain_grad,
    mix_grad,
    kept,
    given,
):
    norm_grad = base[...] + plain_dot(pick[...], back[...])
    features = resid[...]
    scale = lax.rsqrt(jnp.mean(features * features, axis=1, keepdims=True) + NORM_EPSILON)
    shape = features * scale
    gain_grad[...] = jnp.sum(norm_grad * shape, axis=0, keepdims=True)
    inner = norm_grad * gain[...]
    total = scale * (inner - shape * jnp.mean(inner * shape, axis=1, keepdims=True))
    total = total + out_grad[...].astype(jnp.float32)
    resid_grad[...] = total
    low = total.astype(jnp.bfloat16)
    half = out_own.shape[0]
    own_at = pl.multiple_of(plane[0] * half, half)
    mix_grad[pl.ds(own_at, half), :] = nt_dot(out_own[...], low).astype(jnp.bfloat16)
    other_at = pl.multiple_of((1 - plane[0]) * half, half)
    mix_grad[pl.ds(other_at, half), :] = nt_dot(out_other[...], low).astype(jnp.bfloat16)
    quarter = half // 2
    for index, begin in enumerate((own_at, other_at)):
        keep_at = pl.multiple_of(begin + core[0] * quarter, quarter)
        kept[index] = plain_dot(mixed[pl.ds(keep_at, quarter), :], low).astype(jnp.bfloat16)
        give_at = pl.multiple_of(begin + (1 - core[0]) * quarter, quarter)
        given[index] = plain_dot(mixed[pl.ds(give_at, quarter), :], low).astype(jnp.bfloat16)


def close_moe(plane, core, back, pick, base, resid, gain, out_grad, out_own, out_other, mixed):
    rows, width = resid.shape
    quarter = out_own.shape[0] // 2
    return pl.pallas_call(
        close_moe_kernel,
        out_shape=(
            shaped((rows, width), jnp.float32),
            shaped((1, width), jnp.float32),
            shaped((width, rows), jnp.bfloat16),
            shaped((2, quarter, width), jnp.bfloat16),
            shaped((2, quarter, width), jnp.bfloat16),
        ),
        in_specs=[smem()] + [vmem()] * 9 + [smem()],
        out_specs=(vmem(),) * 5,
        cost_estimate=SMALL_COST,
    )(plane, back, pick, base, resid, gain, out_grad, out_own, out_other, mixed, core)


def vmem():
    return pl.BlockSpec(memory_space=pltpu.VMEM)


def smem():
    return pl.BlockSpec(memory_space=pltpu.SMEM)


def shaped(shape, dtype):
    return jax.ShapeDtypeStruct(shape, dtype)


def attention_forward(source, bounds, weight, perm, distance_rows, pieces, head_dim):
    slots = perm.shape[1]
    local_rows = pieces[-1].shape[0]
    groups = slots // local_rows
    levels = distance_rows.shape[0]
    return pl.pallas_call(
        functools.partial(attention_forward_kernel, len(pieces), head_dim),
        out_shape=(
            shaped((groups, head_dim, local_rows), jnp.bfloat16),
            shaped((3 * head_dim, slots), jnp.bfloat16),
            shaped((slots, 2 * head_dim), jnp.bfloat16),
            shaped((head_dim, slots), jnp.float32),
            shaped((1, slots), jnp.float32),
        ),
        in_specs=[smem(), smem()] + [vmem()] * (3 + len(pieces)),
        out_specs=(vmem(),) * 5,
        scratch_shapes=[
            pltpu.VMEM((3 * head_dim, slots), jnp.bfloat16),
            pltpu.VMEM((slots, slots), jnp.bfloat16),
            pltpu.VMEM((levels, BLOCK, BLOCK), jnp.float32),
            pltpu.VMEM((head_dim, slots), jnp.bfloat16),
        ],
        cost_estimate=SMALL_COST,
    )(source, bounds, weight, perm, distance_rows, *pieces)


def attention_backward(
    source, plane, bounds, received, perm, distance_rows, saved, weight, pieces, head_dim
):
    slots = perm.shape[1]
    groups, _, local_rows = received.shape
    levels = distance_rows.shape[0]
    width = weight.shape[1]
    return pl.pallas_call(
        functools.partial(attention_backward_kernel, len(pieces), head_dim),
        out_shape=(
            shaped((groups, 3 * head_dim, local_rows), jnp.bfloat16),
            shaped((3 * head_dim, width // 2), jnp.float32),
            shaped((3 * head_dim, width // 2), jnp.bfloat16),
            shaped((1, width), jnp.float32),
            shaped((levels, 2 * BLOCK), jnp.float32),
        ),
        in_specs=[smem()] * 3 + [vmem()] * (8 + len(pieces)),
        out_specs=(vmem(),) * 5,
        scratch_shapes=[
            pltpu.VMEM((head_dim, slots), jnp.bfloat16),
            pltpu.VMEM((head_dim, slots), jnp.bfloat16),
            pltpu.VMEM((slots, slots), jnp.bfloat16),
            pltpu.VMEM((levels, BLOCK, BLOCK), jnp.float32),
            pltpu.VMEM((levels, BLOCK, BLOCK), jnp.float32),
            pltpu.VMEM((3 * head_dim, slots), jnp.float32),
            pltpu.VMEM((3 * head_dim, slots), jnp.bfloat16),
            pltpu.VMEM((3 * head_dim, slots), jnp.bfloat16),
        ],
        cost_estimate=LARGE_COST,
    )(source, plane, bounds, received, perm, distance_rows, *saved, weight, *pieces)


class Ring:
    def __init__(self, groups):
        self.chips = groups // 2
        order = list(range(0, self.chips, 2)) + list(range(1, self.chips, 2))[::-1]
        self.swap = [(index, index ^ 1) for index in range(groups)]
        self.same_core = [[2 * chip + core for chip in range(self.chips)] for core in range(2)]
        self.onward = [
            (2 * order[at] + core, 2 * order[(at + (1, -1)[core]) % self.chips] + core)
            for at in range(self.chips)
            for core in range(2)
        ]
        self.steps = (self.chips - 1) // 2
        slots = 1 + 2 * self.steps + 2
        table = np.zeros((groups, slots), np.int32)
        for at, chip in enumerate(order):
            for core in range(2):
                way = (-1, 1)[core]
                row = [2 * chip]
                for step in range(1, self.steps + 1):
                    row.append(2 * order[(at + way * step) % self.chips])
                    row.append(2 * order[(at - way * step) % self.chips])
                far = 2 * order[(at + self.chips // 2) % self.chips]
                table[2 * chip + core] = row + [far + core, far + 1 - core]
        self.table = table
        self.forward = [
            (2 * order[at] + core, 2 * order[(at + 1) % self.chips] + core)
            for at in range(self.chips)
            for core in range(2)
        ]
        self.backward = [(end, begin) for begin, end in self.forward]
        self.row_table = np.zeros((groups, groups), np.int32)
        for at, chip in enumerate(order):
            turns = [0] + [way * step for step in range(1, self.steps + 1) for way in (-1, 1)]
            turns.append(self.chips // 2)
            for core in range(2):
                near = [2 * order[(at + turn) % self.chips] + core for turn in turns]
                self.row_table[2 * chip + core] = near + [index ^ 1 for index in near]

    def swapped(self, piece):
        return lax.ppermute(piece, "ctx", self.swap)

    def gather_rows(self, piece, beside):
        half = piece.shape[0] // 2
        pieces = [piece]
        ahead = behind = piece
        for _ in range(self.steps):
            ahead, behind = beside(ahead, behind)
            ahead = lax.ppermute(ahead, "ctx", self.forward)
            behind = lax.ppermute(behind, "ctx", self.backward)
            pieces += [ahead, behind]
        ahead, behind = beside(ahead, behind)
        pieces.append(
            jnp.concatenate(
                [
                    lax.ppermute(ahead[:half], "ctx", self.forward),
                    lax.ppermute(behind[half:], "ctx", self.backward),
                ],
                axis=0,
            )
        )
        return pieces + [self.swapped(item) for item in pieces]

    def gather(self, piece, core, beside=lambda block: block):
        rows = piece.shape[0]
        piece = beside(piece)
        other = self.swapped(piece)
        block = jnp.where(
            core == 0,
            jnp.concatenate([piece, other], axis=0),
            jnp.concatenate([other, piece], axis=0),
        )
        slots = [block]
        for _ in range(self.steps):
            block = lax.ppermute(beside(block), "ctx", self.onward)
            slots += [block, self.swapped(block)]
        block = beside(block)
        half = lax.ppermute(jnp.where(core == 0, block[:rows], block[rows:]), "ctx", self.onward)
        half = beside(half)
        return slots + [half, self.swapped(half)]


def across(values):
    return lax.ppermute(values, "wa", [(0, 1), (1, 0)])


def sum_step(values, groups, stride):
    if stride >= groups:
        return values + across(values)
    return values + lax.ppermute(values, "ctx", [(index, index ^ stride) for index in range(groups)])


def fast_device(
    hidden_in,
    out_grad,
    lengths,
    permutation,
    routes,
    bucket_table,
    w_qkv,
    w_out,
    w_in,
    w_down,
    w_router,
    gain_attn,
    gain_moe,
    rel_bias,
):
    stream = hidden_in[0].astype(jnp.float32)
    local_rows, width = stream.shape
    bucket_count, head_count = rel_bias.shape
    head_dim = width // head_count
    experts = w_router.shape[1]
    slot_cap = 4 * local_rows // experts
    groups = lax.axis_size("ctx")
    half_width = width // 2
    ring = Ring(groups)
    ctx = lax.axis_index("ctx")
    core = ctx % 2
    on_low = lax.axis_index("wa") == 0
    plane = lax.axis_index("wa").reshape(1)
    perm_row = permutation[0]
    slots = perm_row.shape[0]
    bounds = jnp.cumsum(lengths[0])
    own_start = ctx * local_rows
    query_pos = lax.dynamic_slice_in_dim(perm_row, own_start, local_rows, 0)
    is_valid = (segment_of(query_pos, bounds) < NSEQ).astype(jnp.float32)
    source = lax.dynamic_index_in_dim(jnp.asarray(ring.row_table), ctx, 0, keepdims=False)
    block_source = lax.dynamic_index_in_dim(jnp.asarray(ring.table), ctx, 0, keepdims=False)

    def in_order(own, other, axis):
        return jnp.where(
            on_low,
            jnp.concatenate([own, other], axis=axis),
            jnp.concatenate([other, own], axis=axis),
        )

    def core_part(weight):
        half = weight.shape[0] // 2
        return lax.dynamic_slice_in_dim(weight, core * half, half, 0)

    def join_parts(mine):
        theirs = ring.swapped(mine)
        return jnp.where(
            core == 0,
            jnp.concatenate([mine, theirs], axis=0),
            jnp.concatenate([theirs, mine], axis=0),
        )

    head_weight = jnp.concatenate(
        [
            lax.dynamic_slice_in_dim(w_qkv, block * width + ctx * head_dim, head_dim, 1)
            for block in range(3)
        ],
        axis=1,
    ).T
    head_weight = in_order(head_weight, across(head_weight), 1)
    units = w_down.shape[2]
    out_own = w_out
    out_mine = across(core_part(w_out))
    own_weights = jnp.concatenate([w_in[0], w_down[0]], axis=1)

    head_hot = (jnp.arange(head_count, dtype=jnp.int32) == ctx).astype(jnp.float32)
    head_bias = jnp.sum(rel_bias * head_hot[None, :], axis=1)
    reach = bucket_table.shape[0]
    bucket_hot = bucket_table[:, None] == jnp.arange(bucket_count, dtype=jnp.int32)[None, :]
    by_distance = jnp.sum(jnp.where(bucket_hot, head_bias[None, :], 0.0), axis=1)
    levels = reach // BLOCK + 1
    padded = jnp.pad(by_distance, (BLOCK - 1, levels * BLOCK + BLOCK - reach + 1))
    distance_rows = jnp.stack(
        [padded[level * BLOCK : level * BLOCK + 2 * BLOCK] for level in range(levels)]
    )

    normed_attn_low = rms_norm(stream, gain_attn).astype(jnp.bfloat16)
    route_rows = routes[0]
    expert_ids = jnp.arange(experts, dtype=jnp.int32)
    first_hot = route_rows[:, 0:1] == expert_ids[None, :]
    second_hot = route_rows[:, 1:2] == expert_ids[None, :]
    counts = jnp.cumsum((first_hot | second_hot).astype(jnp.int32), axis=0)
    first_slot = jnp.sum(jnp.where(first_hot, counts - 1, 0), axis=1)
    second_slot = jnp.sum(jnp.where(second_hot, counts - 1, 0), axis=1)
    first_lane = route_rows[:, 0] * slot_cap + first_slot
    second_lane = route_rows[:, 1] * slot_cap + second_slot
    lane_ids = jnp.arange(experts * slot_cap, dtype=jnp.int32)
    first_at = first_lane[:, None] == lane_ids[None, :]
    second_at = second_lane[:, None] == lane_ids[None, :]
    first_pick = first_at.astype(jnp.bfloat16)
    second_pick = second_at.astype(jnp.bfloat16)
    any_pick = (first_at | second_at).astype(jnp.bfloat16)

    def exchange(values):
        return lax.all_to_all(
            values,
            "ctx",
            split_axis=0,
            concat_axis=0,
            tiled=True,
            axis_index_groups=ring.same_core,
        )

    out_grad_slots = lead_dot(any_pick, out_grad[0]).astype(jnp.bfloat16)

    qkv_part = core_part(w_qkv)
    perm_lanes = perm_row[None, :]
    turns = 0

    def prepare(ahead, behind):
        nonlocal turns, head_weight, distance_rows, source, bounds, perm_lanes, out_mine, own_weights
        nonlocal out_grad_slots
        turns += 1
        if turns == 2:
            ahead, behind, own_weights = lax.optimization_barrier((ahead, behind, own_weights))
        if turns == 3:
            ahead, behind, head_weight, distance_rows, source, bounds, perm_lanes, out_mine = (
                lax.optimization_barrier(
                    (
                        ahead,
                        behind,
                        head_weight,
                        distance_rows,
                        source,
                        bounds,
                        perm_lanes,
                        out_mine,
                    )
                )
            )
        if turns == 4:
            ahead, behind, out_grad_slots = lax.optimization_barrier(
                (ahead, behind, out_grad_slots)
            )
        return ahead, behind

    pieces = ring.gather_rows(normed_attn_low, prepare)
    out_other = join_parts(out_mine)
    expert_weights = lax.all_gather(own_weights, "wa", axis=0, tiled=True)

    out_grad_slots, _ = lax.optimization_barrier((out_grad_slots, pieces[2 * ring.steps + 1]))
    grads_left = exchange(out_grad_slots[:, :half_width])
    mixed, *saved = attention_forward(
        source, bounds, head_weight, perm_lanes, distance_rows, pieces, head_dim
    )
    mixed, grads_left = lax.optimization_barrier((mixed, grads_left))
    mixed = lax.all_to_all(mixed, "ctx", split_axis=0, concat_axis=0, tiled=True)
    mixed, qkv_part = lax.optimization_barrier((mixed, qkv_part))
    mixed = mixed.reshape(width, local_rows)
    mixed_low, mixed_high = mixed[:half_width], mixed[half_width:]
    mixed_own = jnp.where(on_low, mixed_low, mixed_high)
    mixed_other = jnp.where(on_low, mixed_high, mixed_low)
    attn_out = lead_dot(mixed_own, out_own) + lead_dot(mixed_other, out_other)
    resid = stream + attn_out
    normed_moe_low = rms_norm(resid, gain_moe).astype(jnp.bfloat16)
    normed_moe_wide = normed_moe_low.astype(jnp.float32)
    logits = jnp.dot(normed_moe_wide, w_router, precision=TOP_PRECISION)
    chosen = jnp.stack(
        [
            jnp.sum(jnp.where(first_hot, logits, 0.0), axis=1),
            jnp.sum(jnp.where(second_hot, logits, 0.0), axis=1),
        ],
        axis=1,
    )
    gate_probs = jax.nn.softmax(chosen, axis=1)
    grad_final = out_grad[0].astype(jnp.float32)
    slot_gate = jnp.sum(
        jnp.where(first_at, gate_probs[:, 0:1], 0.0)
        + jnp.where(second_at, gate_probs[:, 1:2], 0.0),
        axis=0,
    )
    gate_parts = []
    for _ in range(3):
        gate_parts.append(lax.reduce_precision(slot_gate, 8, 7))
        slot_gate = slot_gate - gate_parts[-1]
    gate_parts = jnp.pad(jnp.stack(gate_parts, axis=1), ((0, 0), (0, LANES - 3)))
    rows_mine = exchange(
        jnp.concatenate(
            [
                lead_dot(any_pick, normed_moe_low).astype(jnp.bfloat16),
                gate_parts.astype(jnp.bfloat16),
            ],
            axis=1,
        )
    )
    rows_theirs = ring.swapped(rows_mine)
    out_grad_slots, qkv_part, rows_mine = lax.optimization_barrier(
        (out_grad_slots, qkv_part, rows_mine)
    )
    grads_right = exchange(out_grad_slots[:, half_width:])
    qkv_parts = lax.all_gather(qkv_part, "wa", axis=0, tiled=True)
    def chip_total(mine, theirs):
        return (mine.astype(jnp.float32) + ring.swapped(theirs).astype(jnp.float32)).astype(
            jnp.bfloat16
        )

    part_mine, part_theirs, hidden, gate_slope, act = expert_forward(
        rows_mine, rows_theirs, expert_weights, units
    )
    part_theirs, grads_right = lax.optimization_barrier((part_theirs, grads_right))
    partial_total = chip_total(part_mine, part_theirs)
    partial_total, gate_slope = lax.optimization_barrier((partial_total, gate_slope))
    returned = exchange(partial_total)
    back_mine, back_theirs, unit_grads, scaled = expert_backward(
        (grads_left, grads_right, ring.swapped(grads_left), ring.swapped(grads_right)),
        (rows_mine, rows_theirs),
        gate_slope,
        act,
        expert_weights,
    )
    down_grads = turned_product((scaled,), hidden, width)
    back_mine, back_theirs, down_grads = lax.optimization_barrier(
        (back_mine, back_theirs, down_grads)
    )
    back_total = chip_total(back_mine, back_theirs)
    back_total, returned, down_grads = lax.optimization_barrier((back_total, returned, down_grads))
    rows_back = exchange(back_total)

    def plane_sum(values):
        return lax.psum_scatter(values, "wa", scatter_dimension=0, tiled=True).astype(jnp.float32)

    picked_first = plain_dot(first_pick, returned)
    picked_second = plain_dot(second_pick, returned)
    moe_out = gate_probs[:, 0:1] * picked_first + gate_probs[:, 1:2] * picked_second
    final = resid + moe_out

    valid_col = is_valid[:, None]
    stat_terms = jnp.stack(
        [
            jnp.sum(valid_col * final * final),
            jnp.sum(valid_col * attn_out * attn_out),
            jnp.sum(valid_col * moe_out * moe_out),
            jnp.sum(is_valid),
        ]
    )
    gate_grad = jnp.stack(
        [jnp.sum(grad_final * picked_first, axis=1), jnp.sum(grad_final * picked_second, axis=1)],
        axis=1,
    )
    _, gate_back = jax.vjp(lambda chosen_in: jax.nn.softmax(chosen_in, axis=1), chosen)
    (chosen_grad,) = gate_back(gate_grad)
    logit_grad = jnp.where(first_hot, chosen_grad[:, 0:1], 0.0) + jnp.where(
        second_hot, chosen_grad[:, 1:2], 0.0
    )
    router_grad = lead_dot(logit_grad, normed_moe_wide, TOP_PRECISION)
    norm_moe_grad = jnp.dot(logit_grad, w_router.T, precision=TOP_PRECISION)
    norm_moe_grad, router_grad, unit_grads = lax.optimization_barrier(
        (norm_moe_grad, router_grad, unit_grads)
    )
    in_grads = turned_product((rows_mine, rows_theirs), unit_grads, width)
    rows_back, in_grads, qkv_parts = lax.optimization_barrier((rows_back, in_grads, qkv_parts))
    down_shard, in_shard = plane_sum(down_grads), plane_sum(in_grads)
    part_rows = qkv_part.shape[0]
    qkv_other = join_parts(jnp.where(on_low, qkv_parts[part_rows:], qkv_parts[:part_rows]))
    resid_grad, gain_moe_grad, mix_grad, kept, given = close_moe(
        plane,
        core.reshape(1),
        rows_back,
        any_pick,
        norm_moe_grad,
        resid,
        gain_moe[None, :],
        out_grad[0],
        out_own,
        out_other,
        mixed,
    )
    dout = lax.all_to_all(
        mix_grad.reshape(groups, head_dim, local_rows),
        "ctx",
        split_axis=0,
        concat_axis=0,
        tiled=True,
    )
    kept = kept.astype(jnp.float32) + ring.swapped(given).astype(jnp.float32)
    share = kept.shape[1] // ring.chips
    kept = jnp.transpose(kept.reshape(2, ring.chips, share, width), (1, 0, 2, 3))
    kept = exchange(kept.astype(jnp.bfloat16))
    sent, head_own, head_given, gain_sums, distance_grads = attention_backward(
        source,
        plane,
        bounds,
        dout,
        perm_lanes,
        distance_rows,
        saved,
        head_weight,
        pieces,
        head_dim,
    )
    proj = jnp.sum(kept.astype(jnp.float32), axis=0)

    def column_halves(values):
        return jnp.concatenate([values[:, :half_width], values[:, half_width:]], axis=0)

    head_given = jnp.concatenate([head_given, column_halves(proj[1]).astype(jnp.bfloat16)], axis=0)
    head_own = jnp.concatenate([head_own, column_halves(proj[0])], axis=0)
    head_shard = (head_own + across(head_given).astype(jnp.float32)).astype(jnp.bfloat16)
    head_shard, gain_sums, distance_grads = lax.optimization_barrier(
        (head_shard, gain_sums, distance_grads)
    )
    gain_attn_grad = gain_sums[0] / gain_attn
    qkv_grad = lax.all_to_all(sent, "ctx", split_axis=0, concat_axis=0, tiled=True)
    spread_len = levels * BLOCK + BLOCK
    by_distance_grad = sum(
        jnp.pad(distance_grads[level], (level * BLOCK, spread_len - (level + 2) * BLOCK))
        for level in range(levels)
    )[BLOCK - 1 : BLOCK - 1 + reach]
    head_bias_grad = jnp.sum(jnp.where(bucket_hot, by_distance_grad[:, None], 0.0), axis=0)
    bias_grad = head_bias_grad[:, None] * head_hot[None, :]

    tail_row = jnp.concatenate([bias_grad.reshape(-1), stat_terms])
    sums = jnp.concatenate(
        [
            router_grad,
            gain_moe_grad.reshape(1, width),
            gain_attn_grad[None, :],
            jnp.pad(tail_row, (0, width - tail_row.shape[0]))[None, :],
        ],
        axis=0,
    )
    stage = 0

    def beside(piece):
        nonlocal stage, sums, in_shard, down_shard, qkv_grad
        if stage > 1:
            piece, sums = lax.optimization_barrier((piece, sums))
        if stage == 2:
            piece, qkv_grad = lax.optimization_barrier((piece, qkv_grad))
        if stage == 3:
            piece, down_shard = lax.optimization_barrier((piece, down_shard))
        if stage == 4:
            piece, in_shard = lax.optimization_barrier((piece, in_shard))
        if stage >= 1 and 1 << (stage - 1) <= groups:
            sums = sum_step(sums, groups, 1 << (stage - 1))
        stage += 1
        return piece

    gathered = ring.gather(head_shard, core, beside)
    while 1 << (stage - 1) <= groups:
        beside(head_shard)
    qkv_shard, out_shard = assemble_weight_gradients(block_source, gathered, head_dim, width)
    qkv_grad = jnp.transpose(qkv_grad.reshape(head_count, 3, head_dim, local_rows), (1, 0, 2, 3))
    qkv_grad = qkv_grad.reshape(3 * width, local_rows)

    def feature_grad(weight):
        return lax.dot_general(
            qkv_grad, weight, (((0,), (1,)), ((), ())), preferred_element_type=jnp.float32
        )

    norm_attn_grad = in_order(feature_grad(w_qkv), feature_grad(qkv_other), 1)
    _, norm_attn_back = jax.vjp(rms_norm, stream, gain_attn)
    stream_from_norm, _ = norm_attn_back(norm_attn_grad)
    hidden_grad = (resid_grad + stream_from_norm).astype(jnp.bfloat16)

    router_sum = sums[:experts].T
    gain_moe_sum, gain_attn_sum = sums[experts], sums[experts + 1]
    biases = bucket_count * head_count
    bias_sum = sums[experts + 2, :biases].reshape(bucket_count, head_count)
    stat_sums = sums[experts + 2, biases : biases + 4]
    stats = jnp.sqrt(stat_sums[:3] / (stat_sums[3] * width))
    return (
        final.astype(jnp.bfloat16)[None],
        hidden_grad[None],
        qkv_shard,
        out_shard,
        in_shard[None],
        down_shard[None],
        router_sum,
        gain_attn_sum,
        gain_moe_sum,
        bias_sum,
        stats,
    )


def choose_device(groups, planes, *arguments):
    w_router, rel_bias = arguments[10], arguments[13]
    local_rows = arguments[0].shape[1]
    fits = (
        planes == 2
        and rel_bias.shape[1] == groups
        and 2 * w_router.shape[1] == groups
        and local_rows == 128
    )
    return (fast_device if fits else general_device)(*arguments)


def solution(mesh):
    per_device = functools.partial(choose_device, mesh.shape["ctx"], mesh.shape["wa"])
    placed = (
        P("wa", "ctx", None),
        P("wa", "ctx", None),
        P("wa", None),
        P("wa", None),
        P("wa", "ctx", None),
        P(),
        P("wa", None),
        P("wa", None),
        P("ctx", "wa", None),
        P("ctx", "wa", None),
        P(),
        P(),
        P(),
        P(),
    )
    return jax.shard_map(
        per_device,
        mesh=mesh,
        in_specs=placed,
        out_specs=(
            P("wa", "ctx", None),
            P("wa", "ctx", None),
            P("wa", None),
            P("wa", None),
            P("ctx", "wa", None),
            P("ctx", "wa", None),
            P(),
            P(),
            P(),
            P(),
            P(),
        ),
        check_vma=False,
    )
```
